512 devices in a mesh: space: 64 (over x, y, core), load: 8 (over z).
Axes of the slice: x: 4, y: 8, z: 8, core: 2. Of those that a mesh axis runs over, the one named last changes fastest.
Arguments:
- forward_disp: float32 [8, 3, 128, 128, 128], P('load', None, 'space'), may hold values from -6 to 6
- adjoint_rhs: float32 [8, 3, 128, 128, 128], P('load', None, 'space'), may hold values from -72 to 72
- modulus_factor: float32 [128, 128, 128], P('space'), may hold values from 0.5 to 2
- zone_base: float32 [8], replicated, may hold values from 0.3 to 3
- zone_ids: int32 [128, 128, 128], P('space'), may hold values from 0 to 7
- fixed_mask: int32 [128, 128, 128], P('space'), may hold values 0 or 1
Outputs:
- adjoint_disp: float32 [8, 3, 128, 128, 128], P('load', None, 'space')
- modulus_grad: float32 [128, 128, 128], P('space', 'load')
The draws below stay inside these ranges and needn't reach their ends.
All inputs are finite; a program needn't handle non-finite values. No bound on the sum of `fixed_mask` on one device may be relied on, other than what follows from the above.
Results may differ from the reference program's by a relative error of at most 0.00016.
Values sent between devices are 32-bit elements; how exact they have to be, the bound alone decides.
A program may use at most 64 MiB of HBM per device.

```python
import math
import jax
import jax.numpy as jnp
import numpy as np
from jax import lax

NX = 128
NY = 128
ZONES = 8
ITERS = 2
NZ = 128
LOADS = 8


def draw_adjoint_rhs(key, part):
    keys = jax.random.split(jax.random.fold_in(key, 17), 3)
    shape = (LOADS, 3, NZ, NY, NX)
    depth = (jnp.arange(NZ, dtype=jnp.float32) + 0.5) / NZ - 0.5
    spread = math.log(10.0) / 2.0
    rows = jnp.exp(jax.random.uniform(keys[1], (NY,), jnp.float32, -spread, spread))
    columns = jnp.exp(jax.random.uniform(keys[2], (NX,), jnp.float32, -spread, spread))
    base = jnp.clip(jax.random.normal(keys[0], shape, jnp.float32), -4.0, 4.0)
    rising = jnp.exp(math.log(3.0) * depth)
    values = base * rising[:, None, None] * rows[:, None] * columns[None, :]
    return values


def set_ends(array, key, least, largest):
    shape = array.shape
    index_at = [jax.random.randint(jax.random.fold_in(key, axis), (), 0, shape[axis]) for axis in range(len(shape))]
    array = array.at[tuple(index_at)].set(least)
    longest = shape.index(max(shape))
    index_at[longest] = (index_at[longest] + 1) % shape[longest]
    return array.at[tuple(index_at)].set(largest)


def block_levels(own_key, dims, cuts, low, largest):
    loudness, own = 1.0, jax.random.fold_in(own_key, 6)
    for dim, blocks in cuts:
        steps = jnp.exp(jax.random.uniform(jax.random.fold_in(own, dim), (blocks,), jnp.float32, low / len(cuts), largest / len(cuts)))
        loudness = loudness * jnp.repeat(steps, dims[dim] // blocks).reshape([-1 if axis == dim else 1 for axis in range(len(dims))])
    return loudness


def bell_draw(key, extent, scale, limit, cuts=(), held_as=jnp.bfloat16):
    factor_of = block_levels(key, extent, cuts, -0.22, 0.18) if cuts else 1.0
    result = jax.random.normal(key, extent, jnp.float32) * scale * factor_of
    return jnp.minimum(jnp.maximum(result, -limit), limit).astype(held_as)


def setup_inputs(seed: int = 0) -> dict:
    splits = jax.random.split(jax.random.key(seed), 7)
    forward_disp = bell_draw(splits[0], (LOADS, 3, NZ, NY, NX), 1.0, 6.0, ((0, 8), (2, 64)), jnp.float32)
    adjoint_rhs = draw_adjoint_rhs(jax.random.fold_in(splits[6], 71), 0)
    modulus_factor = jnp.clip(jnp.exp(math.log(2.0) - 1.3862944 * jax.random.uniform(splits[2], (NZ, NY, NX), jnp.float32) ** block_levels(splits[2], (NZ, NY, NX), ((0, 64),), -0.2, 0.2)), 0.5, 2.0)
    zone_base = jnp.clip(jnp.exp(jax.random.uniform(splits[3], (ZONES,), jnp.float32, math.log(0.3), math.log(3.0))), 0.3, 3.0)
    zone_ids = set_ends(jax.random.randint(splits[4], (NZ, NY, NX), 0, ZONES), jax.random.fold_in(splits[4], 1), 0, ZONES - 1).astype(jnp.int32)
    fixed_mask = set_ends((jax.random.randint(splits[5], (NZ, NY, NX), 0, 8) < 1).astype(jnp.int32), jax.random.fold_in(splits[5], 1), 0, 1)
    return {"forward_disp": forward_disp, "adjoint_rhs": adjoint_rhs, "modulus_factor": modulus_factor, "zone_base": zone_base, "zone_ids": zone_ids, "fixed_mask": fixed_mask}


def unit_stiffness():
    poisson = 0.3
    lame_first = poisson / ((1.0 + poisson) * (1.0 - 2.0 * poisson))
    shear_mod = 0.5 / (1.0 + poisson)
    elastic = np.zeros((6, 6))
    elastic[:3, :3] = lame_first
    for index in range(3):
        elastic[index, index] += 2.0 * shear_mod
        elastic[index + 3, index + 3] = shear_mod
    points = [0.5 - 0.5 / np.sqrt(3.0), 0.5 + 0.5 / np.sqrt(3.0)]
    stiffness = np.zeros((24, 24))
    for point_z in points:
        for point_y in points:
            for point_x in points:
                gradient = np.zeros((3, 8))
                for corner in range(8):
                    off_z, off_y, off_x = (corner // 4, corner // 2 % 2, corner % 2)
                    shape_x = point_x if off_x else 1.0 - point_x
                    shape_y = point_y if off_y else 1.0 - point_y
                    shape_z = point_z if off_z else 1.0 - point_z
                    sign_x = 1.0 if off_x else -1.0
                    sign_y = 1.0 if off_y else -1.0
                    sign_z = 1.0 if off_z else -1.0
                    gradient[0, corner] = sign_x * shape_y * shape_z
                    gradient[1, corner] = shape_x * sign_y * shape_z
                    gradient[2, corner] = shape_x * shape_y * sign_z
                strain_map = np.zeros((6, 24))
                for corner in range(8):
                    strain_map[0, corner] = gradient[0, corner]
                    strain_map[1, 8 + corner] = gradient[1, corner]
                    strain_map[2, 16 + corner] = gradient[2, corner]
                    strain_map[3, corner] = gradient[1, corner]
                    strain_map[3, 8 + corner] = gradient[0, corner]
                    strain_map[4, 8 + corner] = gradient[2, corner]
                    strain_map[4, 16 + corner] = gradient[1, corner]
                    strain_map[5, 16 + corner] = gradient[0, corner]
                    strain_map[5, corner] = gradient[2, corner]
                stiffness += strain_map.T @ elastic @ strain_map / 8.0
    return stiffness

def corner_offsets(corner):
    return (corner // 4, corner // 2 % 2, corner % 2)

def element_vectors(extended):
    lead = extended.ndim - 4
    padded = jnp.pad(extended, [(0, 0)] * (lead + 2) + [(0, 1), (0, 1)])
    layers = extended.shape[-3] - 1
    height = extended.shape[-2]
    width = extended.shape[-1]
    pieces = []
    for corner in range(8):
        off_z, off_y, off_x = corner_offsets(corner)
        pieces.append(padded[..., off_z:off_z + layers, off_y:off_y + height, off_x:off_x + width])
    stacked = jnp.stack(pieces, axis=-4)
    return stacked.reshape(stacked.shape[:lead] + (24, layers, height, width))

def stiff_product(vectors, stiffness):
    return jnp.einsum('ab,...bzyx->...azyx', stiffness, vectors, precision=lax.Precision.HIGHEST)

def assemble(forces):
    lead = forces.ndim - 4
    layers, height, width = forces.shape[-3:]
    split = forces.reshape(forces.shape[:lead] + (3, 8, layers, height, width))
    total = None
    for corner in range(8):
        off_z, off_y, off_x = corner_offsets(corner)
        placed = jnp.pad(split[..., corner, :, :, :], [(0, 0)] * (lead + 1) + [(off_z, 1 - off_z), (off_y, 1 - off_y), (off_x, 1 - off_x)])
        total = placed if total is None else total + placed
    return total[..., :height, :width]

def node_diagonal(padded, layers, height, width):
    total = None
    for corner in range(8):
        off_z, off_y, off_x = corner_offsets(corner)
        piece = padded[1 - off_z:1 - off_z + layers, 1 - off_y:1 - off_y + height, 1 - off_x:1 - off_x + width]
        total = piece if total is None else total + piece
    return total

def reference(forward_disp, adjoint_rhs, modulus_factor, zone_base, zone_ids, fixed_mask):
    stiffness = jnp.asarray(unit_stiffness(), jnp.float32)
    zone_scale = zone_base[zone_ids]
    modulus = modulus_factor * zone_scale
    free = (1 - fixed_mask).astype(jnp.float32)
    padded = jnp.pad(modulus, ((1, 0), (1, 0), (1, 0)))
    diagonal = node_diagonal(padded, NZ, NY, NX) * stiffness[0, 0]
    inverse = free / diagonal

    def extend(field):
        return jnp.pad(field, ((0, 0), (0, 1), (0, 0), (0, 0)))

    def operate(field):
        forces = stiff_product(element_vectors(extend(field)), stiffness) * modulus
        return free * assemble(forces)[:, :NZ]

    def solve_case(total, pair):
        rhs, forward = pair
        residual = free * rhs
        precond = inverse * residual
        direction = precond
        norm_now = jnp.sum(residual * precond)
        solution = jnp.zeros_like(residual)
        for iteration in range(ITERS):
            image = operate(direction)
            step_size = norm_now / jnp.sum(direction * image)
            solution = solution + step_size * direction
            residual = residual - step_size * image
            precond = inverse * residual
            norm_next = jnp.sum(residual * precond)
            direction = precond + norm_next / norm_now * direction
            norm_now = norm_next
        forward_vec = element_vectors(extend(forward))
        solution_vec = element_vectors(extend(solution))
        term = lax.optimization_barrier(jnp.sum(solution_vec * stiff_product(forward_vec, stiffness), axis=0))
        return (total + term, solution)
    grad_sum, adjoint = lax.scan(solve_case, jnp.zeros((NZ, NY, NX), jnp.float32), (adjoint_rhs, forward_disp))
    return (adjoint, zone_scale * grad_sum)
```

```python
import functools

import jax
import jax.numpy as jnp
import numpy as np
from jax import lax
from jax.experimental import pallas as pl
from jax.experimental.pallas import tpu as pltpu
from jax.sharding import PartitionSpec as P

F32 = jnp.float32
MESH = pl.DeviceIdType.MESH
ROWS = 128
BLOCK = 8
BLOCKS = ROWS // BLOCK

POISSON = 0.3
SHEAR = 0.5 / (1.0 + POISSON)
KAPPA = 2.0 * POISSON / (1.0 - 2.0 * POISSON)
UNIT = SHEAR / 16.0
DIAG = SHEAR * (KAPPA + 4.0) / 9.0


def shifted_down(value, lane_last):
    return jnp.where(lane_last, 0.0, pltpu.roll(value, ROWS - 1, 1))


def plane_modes(here, after, lane_last):
    total, slope = here + after, after - here
    total_next, slope_next = shifted_down(total, lane_last), shifted_down(slope, lane_last)
    return (total + total_next, total_next - total, slope + slope_next, slope_next - slope)


def strains(low, high):
    (u, v, w) = [
        (
            l[1] + h[1],
            l[2] + h[2],
            h[0] - l[0],
            l[3] + h[3],
            h[1] - l[1],
            h[2] - l[2],
            h[3] - l[3],
        )
        for l, h in zip(low, high)
    ]
    return (
        u[0], v[1], w[2],
        u[1] + v[0], u[2] + w[0], v[2] + w[1],
        u[3], w[5], u[4], v[5], v[3], w[4],
        u[5], v[4], w[3],
        u[6], v[6], w[6],
    )


def stresses(e):
    trace = KAPPA * (e[0] + e[1] + e[2])
    out = [2.0 * e[0] + trace, 2.0 * e[1] + trace, 2.0 * e[2] + trace, e[3], e[4], e[5]]
    own, cross = 1.0, KAPPA / 3.0
    for a, b in ((6, 7), (8, 9), (10, 11)):
        both = cross * (e[a] + e[b])
        out += [own * e[a] + both, own * e[b] + both]
    third = 1.0 / 3.0
    shear = (e[12] + e[13] + e[14]) * third
    out += [e[12] * third + shear, e[13] * third + shear, e[14] * third + shear]
    last = (KAPPA + 4.0) / 9.0
    out += [e[15] * last, e[16] * last, e[17] * last]
    return out


def corner_modes(f):
    return (
        (f[0], f[3], f[4], f[6], f[8], f[12], f[15]),
        (f[3], f[1], f[5], f[10], f[13], f[9], f[16]),
        (f[4], f[5], f[2], f[14], f[11], f[7], f[17]),
    )


def onto_lower(g):
    return (-g[2], g[0] - g[4], g[1] - g[5], g[3] - g[6])


def onto_upper(g):
    return (g[2], g[0] + g[4], g[1] + g[5], g[3] + g[6])


def dot(a, b):
    total = None
    for left, right in zip(a, b):
        term = left * right
        total = term if total is None else total + term
    return total


def kernel(
    fwd_hbm, rhs_hbm, fac_hbm, base_ref, ids_hbm, msk_hbm,
    x_out, grad_out,
    fac, ids, msk, rhs, fw, sc, m, y0, y1, inv, r0, r0h, ff, g0, g1, g0r, g1r,
    part, r1, mid, r2, coef, r3,
    load_sem, halo_send, halo_recv, z_send, z_recv, s1_send, s1_recv, s2_send, s2_recv, s3_send, s3_recv,
    *, spaces, loads, group,
):
    s = lax.axis_index("space")
    load = lax.axis_index("load")
    above, below = lax.rem(s + 1, spaces), lax.rem(s + spaces - 1, spaces)
    wide = spaces // group
    within, outer = lax.rem(s, group), s // group
    rows = ROWS // loads

    def local(src, dst, index):
        return pltpu.make_async_copy(src, dst, load_sem.at[index])

    loaded = [
        local(fac_hbm, fac, 0),
        local(ids_hbm, ids, 1),
        local(msk_hbm, msk, 2),
        local(rhs_hbm.at[0], rhs, 3),
        local(fwd_hbm.at[0, :, pl.ds(0, 2)], fw.at[:, pl.ds(0, 2), pl.ds(0, ROWS)], 4),
    ]
    for copy in loaded:
        copy.start()

    near = [{"space": above}, {"space": below}]
    stage1 = [lax.rem(within + i, group) for i in range(1, group)]
    stage2 = [lax.rem(outer + i, wide) for i in range(1, wide)]
    stage3 = [lax.rem(load + i, loads) for i in range(1, loads)]
    peers1 = [{"space": outer * group + i} for i in stage1]
    peers2 = [{"space": i * group + within} for i in stage2]
    peers3 = [{"load": i} for i in stage3]
    barrier = pltpu.get_barrier_semaphore()
    everyone = near + peers1 + peers2 + peers3
    for peer in everyone:
        pl.semaphore_signal(barrier, inc=1, device_id=peer, device_id_type=MESH)

    def remote(src, dst, send, recv, device):
        return pltpu.make_async_remote_copy(
            src_ref=src, dst_ref=dst, send_sem=send, recv_sem=recv, device_id=device, device_id_type=MESH
        )

    lanes = lax.broadcasted_iota(jnp.int32, (BLOCK, ROWS), 1)
    lane_first, lane_last = lanes == 0, lanes == ROWS - 1
    row_first = lax.broadcasted_iota(jnp.int32, (BLOCK, ROWS), 0) == 0
    zero = jnp.zeros((BLOCK, ROWS), F32)

    for layer in range(4):
        m[layer, 0:BLOCK, :] = zero
        for c in range(3):
            y0[layer, c, ROWS : ROWS + BLOCK, :] = zero
    for plane in range(3):
        for c in range(3):
            y1[plane, c, ROWS : ROWS + BLOCK, :] = zero
            fw[c, plane, ROWS : ROWS + BLOCK, :] = zero

    def over_blocks(body, carry=None, start=0, stop=BLOCKS):
        if carry is None:
            lax.fori_loop(start, stop, lambda b, _: (body(pl.multiple_of(b * BLOCK, BLOCK)), 0)[1], 0)
            return None
        return lax.fori_loop(start, stop, lambda b, held: body(pl.multiple_of(b * BLOCK, BLOCK), held), carry)

    loaded[0].wait()
    loaded[1].wait()
    bases = [base_ref[i] for i in range(base_ref.shape[0])]

    def moduli(row):
        for layer in range(2):
            zone = ids[layer, pl.ds(row, BLOCK), :]
            scale = jnp.full((BLOCK, ROWS), bases[0], F32)
            for i in range(1, len(bases)):
                scale = jnp.where(zone == i, bases[i], scale)
            sc[layer, pl.ds(row, BLOCK), :] = scale
            m[1 + layer, pl.ds(row + BLOCK, BLOCK), :] = fac[layer, pl.ds(row, BLOCK), :] * scale

    over_blocks(moduli)

    pl.semaphore_wait(barrier, len(everyone))
    body_rows = pl.ds(BLOCK, ROWS)
    whole = pl.ds(0, ROWS)
    m_up = remote(m.at[2, body_rows], m.at[0, body_rows], halo_send.at[0], halo_recv.at[0], {"space": above})
    m_down = remote(m.at[1, body_rows], m.at[3, body_rows], halo_send.at[1], halo_recv.at[1], {"space": below})
    m_up.start()
    m_down.start()

    loaded[2].wait()
    loaded[3].wait()

    def inverse_diagonal(low, high, row):
        here = m[low, pl.ds(row + BLOCK, BLOCK), :] + m[high, pl.ds(row + BLOCK, BLOCK), :]
        before = m[low, pl.ds(row + BLOCK - 1, BLOCK), :] + m[high, pl.ds(row + BLOCK - 1, BLOCK), :]
        total = here + before
        total = total + jnp.where(lane_first, 0.0, pltpu.roll(total, 1, 1))
        return 1.0 / (DIAG * total)

    def own_first(row):
        at = pl.ds(row, BLOCK)
        free_low = (1 - msk[0, at, :]).astype(F32)
        free_high = (1 - msk[1, at, :]).astype(F32)
        inverse = free_high * inverse_diagonal(1, 2, row)
        inv[1, at, :] = inverse
        for c in range(3):
            r0[0, c, at, :] = free_low * rhs[c, 0, at, :]
            high = free_high * rhs[c, 1, at, :]
            r0[1, c, at, :] = high
            y0[2, c, at, :] = inverse * high

    over_blocks(own_first)
    r_down = remote(r0.at[0], r0h, halo_send.at[2], halo_recv.at[2], {"space": below})
    y_up = remote(y0.at[2, :, whole], y0.at[0, :, whole], halo_send.at[3], halo_recv.at[3], {"space": above})
    r_down.start()
    y_up.start()
    loaded[4].wait()
    f_down = remote(
        fw.at[:, 0, whole], fw.at[:, 2, whole], halo_send.at[4], halo_recv.at[4], {"space": below}
    )
    f_down.start()

    def modes(ref_at, row):
        out = []
        for c in range(3):
            here, after = ref_at(c, pl.ds(row, BLOCK)), ref_at(c, pl.ds(row + 1, BLOCK))
            out.append(plane_modes(here, after, lane_last))
        return out

    def forward_stress(layer):
        def body(row):
            low = modes(lambda c, at: fw[c, layer, at, :], row)
            high = modes(lambda c, at: fw[c, layer + 1, at, :], row)
            for i, value in enumerate(stresses(strains(low, high))):
                ff[layer, i, pl.ds(row, BLOCK), :] = value

        over_blocks(body)

    forward_stress(0)

    m_up.wait_recv()
    m_down.wait_recv()
    r_down.wait_recv()
    y_up.wait_recv()

    @pl.when(s == 0)
    def _():
        m[0, BLOCK : BLOCK + ROWS, :] = jnp.zeros((ROWS, ROWS), F32)

    @pl.when(s == spaces - 1)
    def _():
        r0h[...] = jnp.zeros((3, ROWS, ROWS), F32)

    def own_second(row):
        at = pl.ds(row, BLOCK)
        inverse = (1 - msk[0, at, :]).astype(F32) * inverse_diagonal(0, 1, row)
        inv[0, at, :] = inverse
        beyond = inverse_diagonal(2, 3, row)
        for c in range(3):
            y0[1, c, at, :] = inverse * r0[0, c, at, :]
            y0[3, c, at, :] = beyond * r0h[c, at, :]

    over_blocks(own_second)

    def product(row, held):
        carried, norm, curve, next_norm = held
        at = pl.ds(row, BLOCK)
        planes = [modes(lambda c, where: y0[p, c, where, :], row) for p in range(4)]
        onto = [None, None]
        for layer in range(3):
            modulus = UNIT * m[layer, pl.ds(row + BLOCK, BLOCK), :]
            force = corner_modes([modulus * f for f in stresses(strains(planes[layer], planes[layer + 1]))])
            for plane, spread in ((layer - 1, onto_lower), (layer, onto_upper)):
                if 0 <= plane < 2:
                    new = [spread(g) for g in force]
                    if onto[plane] is None:
                        onto[plane] = new
                    else:
                        onto[plane] = [tuple(a + b for a, b in zip(o, n)) for o, n in zip(onto[plane], new)]
        passed = []
        for plane in range(2):
            inverse = inv[plane, at, :]
            for c in range(3):
                g = onto[plane][c]
                sums = (g[0] - g[1]) + jnp.where(lane_first, 0.0, pltpu.roll(g[0] + g[1], 1, 1))
                slopes = (g[2] - g[3]) + jnp.where(lane_first, 0.0, pltpu.roll(g[2] + g[3], 1, 1))
                rolled = pltpu.roll(sums + slopes, 1, 0)
                force = (sums - slopes) + jnp.where(row_first, carried[3 * plane + c], rolled)
                passed.append(rolled)
                image = inverse * force
                y1[plane, c, at, :] = image
                field = y0[1 + plane, c, at, :]
                norm = norm + r0[plane, c, at, :] * field
                curve = curve + force * field
                next_norm = next_norm + force * image
        return tuple(passed), norm, curve, next_norm

    _, norm, curve, next_norm = over_blocks(product, ((zero,) * 6, zero, zero, zero))

    y1_down = remote(y1.at[0, :, whole], y1.at[2, :, whole], halo_send.at[5], halo_recv.at[5], {"space": below})
    y1_down.start()

    def against_forward(ref, first, layer, out, energy):
        def body(row, held):
            low = modes(lambda c, at: ref[first + layer, c, at, :], row)
            high = modes(lambda c, at: ref[first + layer + 1, c, at, :], row)
            e = strains(low, high)
            at = pl.ds(row, BLOCK)
            out[layer, at, :] = UNIT * dot(e, [ff[layer, i, at, :] for i in range(18)])
            if energy:
                held = held + (UNIT * m[1 + layer, pl.ds(row + BLOCK, BLOCK), :]) * dot(e, stresses(e))
            return held

        return body

    f_down.wait_recv()

    @pl.when(s == spaces - 1)
    def _():
        fw[:, 2, 0:ROWS, :] = jnp.zeros((3, ROWS, ROWS), F32)

    forward_stress(1)
    for layer in range(2):
        over_blocks(against_forward(y0, 1, layer, g0, False), zero)

    def exchange(src, dst, sems):
        copies = []
        for slot, peer in zip(stage3, peers3):
            copy = remote(
                src.at[:, pl.ds(pl.multiple_of(slot * rows, rows), rows)], dst.at[load],
                z_send.at[sems, slot], z_recv.at[sems, load], peer,
            )
            copy.start()
            copies.append(copy)
        return copies

    sent = exchange(g0, g0r, 0)
    energy = over_blocks(against_forward(y1, 0, 0, g1, True), zero)
    y1_down.wait_recv()

    @pl.when(s == spaces - 1)
    def _():
        y1[2, :, 0:ROWS, :] = jnp.zeros((3, ROWS, ROWS), F32)

    energy = over_blocks(against_forward(y1, 0, 1, g1, True), energy)

    part[0:1, :] = jnp.sum(norm, axis=0, keepdims=True)
    part[1:2, :] = jnp.sum(curve, axis=0, keepdims=True)
    part[2:3, :] = jnp.sum(next_norm, axis=0, keepdims=True)
    part[3:4, :] = jnp.sum(energy, axis=0, keepdims=True)
    part[4:8, :] = jnp.zeros((4, ROWS), F32)
    for slot, peer in zip(stage1, peers1):
        copy = remote(part, r1.at[within], s1_send.at[slot], s1_recv.at[within], peer)
        copy.start()
        sent.append(copy)
    sent += exchange(g1, g1r, 1)
    r1[within] = part[...]

    def arrived(dst, slots, sems, like):
        for slot in slots:
            remote(like, dst.at[slot], sems.at[slot], sems.at[slot], near[0]).wait_recv()

    arrived(r1, stage1, s1_recv, part)
    total = r1[0]
    for i in range(1, group):
        total = total + r1[i]
    mid[...] = total
    for slot, peer in zip(stage2, peers2):
        copy = remote(mid, r2.at[outer], s2_send.at[slot], s2_recv.at[outer], peer)
        copy.start()
        sent.append(copy)
    r2[outer] = total
    arrived(r2, stage2, s2_recv, mid)
    total = r2[0]
    for i in range(1, wide):
        total = total + r2[i]

    sums = jnp.sum(total, axis=1, keepdims=True)
    sums = jnp.broadcast_to(sums, (BLOCK, ROWS))
    rr, rq, qq, qd = sums[0:1], sums[1:2], sums[2:3], sums[3:4]
    step = rr / rq
    norm_next = step * (step * qq) - rr
    ratio = norm_next / rr
    curve_next = rq - 2.0 * (step * qq) + step * (step * qd)
    step_next = norm_next / (curve_next - ratio * norm_next / step)
    first = step + step_next * (1.0 + ratio)
    second = -(step_next * step)
    coef[...] = jnp.concatenate([first, second, jnp.zeros((6, ROWS), F32)], axis=0)
    for slot, peer in zip(stage3, peers3):
        copy = remote(coef, r3.at[load], s3_send.at[slot], s3_recv.at[load], peer)
        copy.start()
        sent.append(copy)
    r3[load] = coef[...]
    first_all = jnp.broadcast_to(first, (BLOCK, ROWS))
    second_all = jnp.broadcast_to(second, (BLOCK, ROWS))

    def finish(row):
        at = pl.ds(row, BLOCK)
        for c in range(3):
            for plane in range(2):
                x_out[0, c, plane, at, :] = first_all * y0[1 + plane, c, at, :] + second_all * y1[plane, c, at, :]

    over_blocks(finish)

    mine = pl.ds(pl.multiple_of(load * rows, rows), rows)
    g0r[load] = g0[:, mine, :]
    g1r[load] = g1[:, mine, :]
    for slot in stage3:
        remote(g0.at[:, pl.ds(0, rows)], g0r.at[slot], z_send.at[0, slot], z_recv.at[0, slot], near[0]).wait_recv()
        remote(g1.at[:, pl.ds(0, rows)], g1r.at[slot], z_send.at[1, slot], z_recv.at[1, slot], near[0]).wait_recv()
    arrived(r3, stage3, s3_recv, coef)
    total = None
    for i in range(loads):
        term = r3[i, 0:1, :][None] * g0r[i] + r3[i, 1:2, :][None] * g1r[i]
        total = term if total is None else total + term
    grad_out[...] = sc[:, mine, :] * total

    for copy in (m_up, m_down, r_down, y_up, f_down, y1_down):
        copy.wait_send()
    for copy in sent:
        copy.wait_send()


def solution(mesh):
    spaces, loads = mesh.shape["space"], mesh.shape["load"]
    group = 16

    def shards(forward_disp, adjoint_rhs, modulus_factor, zone_base, zone_ids, fixed_mask):
        plane = (ROWS, ROWS)
        padded = (ROWS + BLOCK, ROWS)
        rows = ROWS // loads
        vmem = lambda *shape: pltpu.VMEM(shape, F32)
        ints = lambda *shape: pltpu.VMEM(shape, jnp.int32)
        dma = pltpu.SemaphoreType.DMA
        hbm = pl.BlockSpec(memory_space=pl.ANY)
        return pl.pallas_call(
            functools.partial(kernel, spaces=spaces, loads=loads, group=group),
            out_shape=(
                jax.ShapeDtypeStruct(forward_disp.shape, F32),
                jax.ShapeDtypeStruct((2, rows, ROWS), F32),
            ),
            in_specs=[hbm, hbm, hbm, pl.BlockSpec(memory_space=pltpu.SMEM), hbm, hbm],
            out_specs=(pl.BlockSpec(memory_space=pltpu.VMEM), pl.BlockSpec(memory_space=pltpu.VMEM)),
            scratch_shapes=[
                vmem(2, *plane), ints(2, *plane), ints(2, *plane), vmem(3, 2, *plane), vmem(3, 3, *padded),
                vmem(2, *plane), vmem(4, *padded), vmem(4, 3, *padded), vmem(3, 3, *padded),
                vmem(2, *plane), vmem(2, 3, *plane), vmem(3, *plane), vmem(2, 18, *plane),
                vmem(2, *plane), vmem(2, *plane), vmem(loads, 2, rows, ROWS), vmem(loads, 2, rows, ROWS),
                vmem(8, ROWS), vmem(group, 8, ROWS), vmem(8, ROWS), vmem(spaces // group, 8, ROWS),
                vmem(8, ROWS), vmem(loads, 8, ROWS),
                dma((5,)), dma((6,)), dma((6,)), dma((2, loads)), dma((2, loads)),
                dma((group,)), dma((group,)), dma((spaces // group,)), dma((spaces // group,)),
                dma((loads,)), dma((loads,)),
            ],
            compiler_params=pltpu.CompilerParams(collective_id=0, has_side_effects=True),
        )(forward_disp, adjoint_rhs, modulus_factor, zone_base, zone_ids, fixed_mask)

    placed = (
        P("load", None, "space", None, None),
        P("load", None, "space", None, None),
        P("space", None, None),
        P(),
        P("space", None, None),
        P("space", None, None),
    )
    return jax.shard_map(
        shards,
        mesh=mesh,
        in_specs=placed,
        out_specs=(P("load", None, "space", None, None), P("space", "load", None)),
        check_vma=False,
    )
```

```python
import functools

import jax
import jax.numpy as jnp
import numpy as np
from jax import lax
from jax.experimental import pallas as pl
from jax.experimental.pallas import tpu as pltpu
from jax.sharding import PartitionSpec as P

F32 = jnp.float32
MESH = pl.DeviceIdType.MESH
ROWS = 128
TILE = 8
LIMIT = 40 * 2**20

POISSON = 0.3
SHEAR = 0.5 / (1.0 + POISSON)
KAPPA = 2.0 * POISSON / (1.0 - 2.0 * POISSON)
UNIT = SHEAR / 16.0
DIAG = SHEAR * (KAPPA + 4.0) / 9.0


def shifted_down(value):
    last = lax.broadcasted_iota(jnp.int32, value.shape, 1) == ROWS - 1
    return jnp.where(last, 0.0, pltpu.roll(value, ROWS - 1, 1))


def shifted_up(value):
    first = lax.broadcasted_iota(jnp.int32, value.shape, 1) == 0
    return jnp.where(first, 0.0, pltpu.roll(value, 1, 1))


def plane_modes(here, after):
    total, slope = here + after, after - here
    total_next, slope_next = shifted_down(total), shifted_down(slope)
    return (total + total_next, total_next - total, slope + slope_next, slope_next - slope)


def strains(low, high):
    (u, v, w) = [
        (
            l[1] + h[1],
            l[2] + h[2],
            h[0] - l[0],
            l[3] + h[3],
            h[1] - l[1],
            h[2] - l[2],
            h[3] - l[3],
        )
        for l, h in zip(low, high)
    ]
    return (
        u[0], v[1], w[2],
        u[1] + v[0], u[2] + w[0], v[2] + w[1],
        u[3], w[5], u[4], v[5], v[3], w[4],
        u[5], v[4], w[3],
        u[6], v[6], w[6],
    )


def stresses(e):
    trace = KAPPA * (e[0] + e[1] + e[2])
    out = [2.0 * e[0] + trace, 2.0 * e[1] + trace, 2.0 * e[2] + trace, e[3], e[4], e[5]]
    own, cross = 1.0, KAPPA / 3.0
    for a, b in ((6, 7), (8, 9), (10, 11)):
        both = cross * (e[a] + e[b])
        out += [own * e[a] + both, own * e[b] + both]
    third = 1.0 / 3.0
    shear = (e[12] + e[13] + e[14]) * third
    out += [e[12] * third + shear, e[13] * third + shear, e[14] * third + shear]
    last = (KAPPA + 4.0) / 9.0
    out += [e[15] * last, e[16] * last, e[17] * last]
    return out


def corner_modes(f):
    return (
        (f[0], f[3], f[4], f[6], f[8], f[12], f[15]),
        (f[3], f[1], f[5], f[10], f[13], f[9], f[16]),
        (f[4], f[5], f[2], f[14], f[11], f[7], f[17]),
    )


def onto_lower(g):
    return (-g[2], g[0] - g[4], g[1] - g[5], g[3] - g[6])


def onto_upper(g):
    return (g[2], g[0] + g[4], g[1] + g[5], g[3] + g[6])


def dot(a, b):
    total = None
    for left, right in zip(a, b):
        term = left * right
        total = term if total is None else total + term
    return total


def folded(value):
    total = value[0:TILE]
    for i in range(1, value.shape[0] // TILE):
        total = total + value[i * TILE : (i + 1) * TILE]
    return total


def over_rows(body, size, carry=None):
    at = lambda b: pl.multiple_of(b * size, size)
    if carry is None:
        lax.fori_loop(0, ROWS // size, lambda b, _: (body(at(b)), 0)[1], 0)
        return None
    return lax.fori_loop(0, ROWS // size, lambda b, held: body(at(b), held), carry)


def kernel(
    fwd_hbm, rhs_hbm, fac_hbm, base_hbm, ids_hbm, msk_hbm,
    y0, y1, coef, gsum, scale_out,
    base, fac, ids, msk, rhs, fw, sc, m, y0h, y1h, inv, r0, r0h, ff, g0, g1, g0r, g1r,
    part, r1, mid, r2, r3,
    load_sem, halo_send, halo_recv, z_send, z_recv, s1_send, s1_recv, s2_send, s2_recv, s3_send, s3_recv,
    *, spaces, loads, group,
):
    s = lax.axis_index("space")
    load = lax.axis_index("load")
    above, below = lax.rem(s + 1, spaces), lax.rem(s + spaces - 1, spaces)
    wide = spaces // group
    within, outer = lax.rem(s, group), s // group
    rows = ROWS // loads

    def local(src, dst, index):
        return pltpu.make_async_copy(src, dst, load_sem.at[index])

    loaded = [
        local(base_hbm, base, 5),
        local(fac_hbm, fac, 0),
        local(ids_hbm, ids, 1),
        local(msk_hbm, msk, 2),
        local(rhs_hbm.at[0], rhs, 3),
        local(fwd_hbm.at[0, :, pl.ds(0, 2)], fw.at[:, pl.ds(0, 2), pl.ds(0, ROWS)], 4),
    ]
    for copy in loaded:
        copy.start()

    near = [{"space": above}, {"space": below}]
    stage1 = [lax.rem(within + i, group) for i in range(1, group)]
    stage2 = [lax.rem(outer + i, wide) for i in range(1, wide)]
    stage3 = [lax.rem(load + i, loads) for i in range(1, loads)]
    peers1 = [{"space": outer * group + i} for i in stage1]
    peers2 = [{"space": i * group + within} for i in stage2]
    peers3 = [{"load": i} for i in stage3]
    barrier = pltpu.get_barrier_semaphore()
    everyone = near + peers1 + peers2 + peers3
    for peer in everyone:
        pl.semaphore_signal(barrier, inc=1, device_id=peer, device_id_type=MESH)

    def remote(src, dst, send, recv, device):
        return pltpu.make_async_remote_copy(
            src_ref=src, dst_ref=dst, send_sem=send, recv_sem=recv, device_id=device, device_id_type=MESH
        )

    zero = jnp.zeros((TILE, ROWS), F32)
    past = slice(ROWS, ROWS + TILE)
    for layer in range(4):
        m[layer, 0:TILE, :] = zero
    for c in range(3):
        y1h[c, past, :] = zero
        for plane in range(2):
            y0[c, plane, past, :] = zero
            y0h[c, plane, past, :] = zero
            y1[c, plane, past, :] = zero
        for plane in range(3):
            fw[c, plane, past, :] = zero

    for copy in loaded[:3]:
        copy.wait()
    bases = [base[i] for i in range(base.shape[0])]

    def moduli(row, n=16):
        at = pl.ds(row, n)
        for layer in range(2):
            zone = ids[layer, at, :]
            scale = jnp.full((n, ROWS), bases[0], F32)
            for i in range(1, len(bases)):
                scale = jnp.where(zone == i, bases[i], scale)
            sc[layer, at, :] = scale
            m[1 + layer, pl.ds(row + TILE, n), :] = fac[layer, at, :] * scale

    over_rows(moduli, 16)
    loaded[3].wait()
    loaded[4].wait()

    def inverse_diagonal(low, high, row, n):
        here = m[low, pl.ds(row + TILE, n), :] + m[high, pl.ds(row + TILE, n), :]
        before = m[low, pl.ds(row + TILE - 1, n), :] + m[high, pl.ds(row + TILE - 1, n), :]
        total = here + before
        return 1.0 / (DIAG * (total + shifted_up(total)))

    def own_first(row, n=64):
        at = pl.ds(row, n)
        free_low = (1 - msk[0, at, :]).astype(F32)
        free_high = (1 - msk[1, at, :]).astype(F32)
        inverse = free_high * inverse_diagonal(1, 2, row, n)
        inv[1, at, :] = inverse
        for c in range(3):
            r0[c, 0, at, :] = free_low * rhs[c, 0, at, :]
            high = free_high * rhs[c, 1, at, :]
            r0[c, 1, at, :] = high
            y0[c, 1, at, :] = inverse * high

    over_rows(own_first, 64)

    pl.semaphore_wait(barrier, len(everyone))
    body_rows = pl.ds(TILE, ROWS)
    whole = pl.ds(0, ROWS)
    m_up = remote(m.at[2, body_rows], m.at[0, body_rows], halo_send.at[0], halo_recv.at[0], {"space": above})
    m_down = remote(m.at[1, body_rows], m.at[3, body_rows], halo_send.at[1], halo_recv.at[1], {"space": below})
    m_up.start()
    m_down.start()
    r_down = remote(r0.at[:, 0], r0h, halo_send.at[2], halo_recv.at[2], {"space": below})
    y_up = remote(y0.at[:, 1, whole], y0h.at[:, 0, whole], halo_send.at[3], halo_recv.at[3], {"space": above})
    r_down.start()
    y_up.start()
    loaded[5].wait()
    f_down = remote(
        fw.at[:, 0, whole], fw.at[:, 2, whole], halo_send.at[4], halo_recv.at[4], {"space": below}
    )
    f_down.start()

    def modes(plane, row, n):
        return [plane_modes(ref[pl.ds(row, n), :], ref[pl.ds(row + 1, n), :]) for ref in plane]

    y0_planes = [
        [y0h.at[c, 0] for c in range(3)],
        [y0.at[c, 0] for c in range(3)],
        [y0.at[c, 1] for c in range(3)],
        [y0h.at[c, 1] for c in range(3)],
    ]
    y1_planes = [
        [y1.at[c, 0] for c in range(3)],
        [y1.at[c, 1] for c in range(3)],
        [y1h.at[c] for c in range(3)],
    ]

    def forward_stress(layer, n):
        def body(row):
            low = modes([fw.at[c, layer] for c in range(3)], row, n)
            high = modes([fw.at[c, layer + 1] for c in range(3)], row, n)
            for i, value in enumerate(stresses(strains(low, high))):
                ff[layer, i, pl.ds(row, n), :] = value

        over_rows(body, n)

    forward_stress(0, 32)

    m_up.wait_recv()
    m_down.wait_recv()
    r_down.wait_recv()
    y_up.wait_recv()

    @pl.when(s == 0)
    def _():
        m[0, TILE : TILE + ROWS, :] = jnp.zeros((ROWS, ROWS), F32)

    @pl.when(s == spaces - 1)
    def _():
        r0h[...] = jnp.zeros((3, ROWS, ROWS), F32)

    def own_second(row, n=64):
        at = pl.ds(row, n)
        inverse = (1 - msk[0, at, :]).astype(F32) * inverse_diagonal(0, 1, row, n)
        inv[0, at, :] = inverse
        beyond = inverse_diagonal(2, 3, row, n)
        for c in range(3):
            y0[c, 0, at, :] = inverse * r0[c, 0, at, :]
            y0h[c, 1, at, :] = beyond * r0h[c, at, :]

    over_rows(own_second, 64)

    def product(row, held, n=16):
        carried, norm, curve, next_norm = held
        at = pl.ds(row, n)
        row_first = lax.broadcasted_iota(jnp.int32, (TILE, ROWS), 0) == 0
        planes = [modes(plane, row, n) for plane in y0_planes]
        onto = [None, None]
        for layer in range(3):
            modulus = UNIT * m[layer, pl.ds(row + TILE, n), :]
            force = corner_modes([modulus * f for f in stresses(strains(planes[layer], planes[layer + 1]))])
            for plane, spread in ((layer - 1, onto_lower), (layer, onto_upper)):
                if 0 <= plane < 2:
                    new = [spread(g) for g in force]
                    if onto[plane] is None:
                        onto[plane] = new
                    else:
                        onto[plane] = [tuple(a + b for a, b in zip(o, w)) for o, w in zip(onto[plane], new)]
        passed = []
        for plane in range(2):
            inverse = inv[plane, at, :]
            for c in range(3):
                g = onto[plane][c]
                sums = (g[0] - g[1]) + shifted_up(g[0] + g[1])
                slopes = (g[2] - g[3]) + shifted_up(g[2] + g[3])
                rolled = pltpu.roll(sums + slopes, 1, 0)
                head = jnp.where(row_first, carried[3 * plane + c], rolled[0:TILE])
                passed.append(rolled[0:TILE])
                if n > TILE:
                    head = jnp.concatenate([head, rolled[TILE:n]], axis=0)
                force = (sums - slopes) + head
                image = inverse * force
                y1[c, plane, at, :] = image
                field = y0[c, plane, at, :]
                norm = norm + folded(r0[c, plane, at, :] * field)
                curve = curve + folded(force * field)
                next_norm = next_norm + folded(force * image)
        return tuple(passed), norm, curve, next_norm

    _, norm, curve, next_norm = over_rows(product, 16, ((zero,) * 6, zero, zero, zero))

    y1_down = remote(y1.at[:, 0, whole], y1h.at[:, whole], halo_send.at[5], halo_recv.at[5], {"space": below})
    y1_down.start()

    def against_forward(planes, first, out, energy, n):
        def body(row, held):
            all_modes = [modes(plane, row, n) for plane in planes]
            at = pl.ds(row, n)
            for i in range(len(planes) - 1):
                layer = first + i
                e = strains(all_modes[i], all_modes[i + 1])
                out[layer, at, :] = UNIT * dot(e, [ff[layer, j, at, :] for j in range(18)])
                if energy:
                    held = held + folded((UNIT * m[1 + layer, pl.ds(row + TILE, n), :]) * dot(e, stresses(e)))
            return held

        return lambda held: over_rows(body, n, held)

    f_down.wait_recv()

    @pl.when(s == spaces - 1)
    def _():
        fw[:, 2, 0:ROWS, :] = jnp.zeros((3, ROWS, ROWS), F32)

    forward_stress(1, 32)
    against_forward(y0_planes[1:4], 0, g0, False, 16)(zero)

    def exchange(src, dst, sems):
        copies = []
        for slot, peer in zip(stage3, peers3):
            copy = remote(
                src.at[:, pl.ds(pl.multiple_of(slot * rows, rows), rows)], dst.at[load],
                z_send.at[sems, slot], z_recv.at[sems, load], peer,
            )
            copy.start()
            copies.append(copy)
        return copies

    sent = exchange(g0, g0r, 0)
    energy = against_forward(y1_planes[0:2], 0, g1, True, 32)(zero)
    y1_down.wait_recv()

    @pl.when(s == spaces - 1)
    def _():
        y1h[:, 0:ROWS, :] = jnp.zeros((3, ROWS, ROWS), F32)

    energy = against_forward(y1_planes[1:3], 1, g1, True, 32)(energy)

    part[0:1, :] = jnp.sum(norm, axis=0, keepdims=True)
    part[1:2, :] = jnp.sum(curve, axis=0, keepdims=True)
    part[2:3, :] = jnp.sum(next_norm, axis=0, keepdims=True)
    part[3:4, :] = jnp.sum(energy, axis=0, keepdims=True)
    part[4:8, :] = jnp.zeros((4, ROWS), F32)
    for slot, peer in zip(stage1, peers1):
        copy = remote(part, r1.at[within], s1_send.at[slot], s1_recv.at[within], peer)
        copy.start()
        sent.append(copy)
    sent += exchange(g1, g1r, 1)
    r1[within] = part[...]

    def arrived(dst, slots, sems, like):
        for slot in slots:
            remote(like, dst.at[slot], sems.at[slot], sems.at[slot], near[0]).wait_recv()

    arrived(r1, stage1, s1_recv, part)
    total = r1[0]
    for i in range(1, group):
        total = total + r1[i]
    mid[...] = total
    for slot, peer in zip(stage2, peers2):
        copy = remote(mid, r2.at[outer], s2_send.at[slot], s2_recv.at[outer], peer)
        copy.start()
        sent.append(copy)
    r2[outer] = total
    arrived(r2, stage2, s2_recv, mid)
    total = r2[0]
    for i in range(1, wide):
        total = total + r2[i]

    sums = jnp.sum(total, axis=1, keepdims=True)
    sums = jnp.broadcast_to(sums, (TILE, ROWS))
    rr, rq, qq, qd = sums[0:1], sums[1:2], sums[2:3], sums[3:4]
    step = rr / rq
    norm_next = step * (step * qq) - rr
    ratio = norm_next / rr
    curve_next = rq - 2.0 * (step * qq) + step * (step * qd)
    step_next = norm_next / (curve_next - ratio * norm_next / step)
    first = step + step_next * (1.0 + ratio)
    second = -(step_next * step)
    coef[...] = jnp.concatenate([first, second, jnp.zeros((6, ROWS), F32)], axis=0)
    for slot, peer in zip(stage3, peers3):
        copy = remote(coef, r3.at[load], s3_send.at[slot], s3_recv.at[load], peer)
        copy.start()
        sent.append(copy)
    r3[load] = coef[...]

    mine = pl.ds(pl.multiple_of(load * rows, rows), rows)
    g0r[load] = g0[:, mine, :]
    g1r[load] = g1[:, mine, :]
    scale_out[...] = sc[:, mine, :]
    for slot in stage3:
        remote(g0.at[:, pl.ds(0, rows)], g0r.at[slot], z_send.at[0, slot], z_recv.at[0, slot], near[0]).wait_recv()
        remote(g1.at[:, pl.ds(0, rows)], g1r.at[slot], z_send.at[1, slot], z_recv.at[1, slot], near[0]).wait_recv()
    arrived(r3, stage3, s3_recv, coef)
    total = None
    for i in range(loads):
        term = r3[i, 0:1, :][None] * g0r[i] + r3[i, 1:2, :][None] * g1r[i]
        total = term if total is None else total + term
    gsum[...] = total

    for copy in (m_up, m_down, r_down, y_up, f_down, y1_down):
        copy.wait_send()
    for copy in sent:
        copy.wait_send()


def finish(y0, y1, coef, gsum, scale, x_out, grad_out, x, grad, sem):
    grad[...] = scale[...] * gsum[...]
    copies = [pltpu.make_async_copy(grad, grad_out, sem.at[3])]
    copies[0].start()
    first = jnp.broadcast_to(coef[0:1, :], (ROWS, ROWS))
    second = jnp.broadcast_to(coef[1:2, :], (ROWS, ROWS))
    for c in range(3):
        for plane in range(2):
            x[c, plane] = first * y0[c, plane, 0:ROWS, :] + second * y1[c, plane, 0:ROWS, :]
        copy = pltpu.make_async_copy(x.at[c], x_out.at[0, c], sem.at[c])
        copy.start()
        copies.append(copy)
    for copy in copies:
        copy.wait()


def solution(mesh):
    spaces, loads = mesh.shape["space"], mesh.shape["load"]
    group = 16
    rows = ROWS // loads

    def shards(forward_disp, adjoint_rhs, modulus_factor, zone_base, zone_ids, fixed_mask):
        plane = (ROWS, ROWS)
        padded = (ROWS + TILE, ROWS)
        vmem = lambda *shape: pltpu.VMEM(shape, F32)
        ints = lambda *shape: pltpu.VMEM(shape, jnp.int32)
        dma = pltpu.SemaphoreType.DMA
        hbm = pl.BlockSpec(memory_space=pltpu.HBM)
        held = pl.BlockSpec(memory_space=pltpu.VMEM)
        out = lambda *shape: jax.ShapeDtypeStruct(shape, F32)
        pinned = [
            pltpu.with_memory_space_constraint(a, pltpu.HBM)
            for a in (forward_disp, adjoint_rhs, modulus_factor, zone_base, zone_ids, fixed_mask)
        ]
        y0, y1, coef, gsum, scale = pl.pallas_call(
            functools.partial(kernel, spaces=spaces, loads=loads, group=group),
            out_shape=(
                out(3, 2, *padded), out(3, 2, *padded), out(TILE, ROWS), out(2, rows, ROWS), out(2, rows, ROWS)
            ),
            in_specs=[hbm] * 6,
            out_specs=(held,) * 5,
            scratch_shapes=[
                pltpu.SMEM(zone_base.shape, F32),
                vmem(2, *plane), ints(2, *plane), ints(2, *plane), vmem(3, 2, *plane), vmem(3, 3, *padded),
                vmem(2, *plane), vmem(4, *padded), vmem(3, 2, *padded), vmem(3, *padded),
                vmem(2, *plane), vmem(3, 2, *plane), vmem(3, *plane), vmem(2, 18, *plane),
                vmem(2, *plane), vmem(2, *plane), vmem(loads, 2, rows, ROWS), vmem(loads, 2, rows, ROWS),
                vmem(TILE, ROWS), vmem(group, TILE, ROWS), vmem(TILE, ROWS), vmem(spaces // group, TILE, ROWS),
                vmem(loads, TILE, ROWS),
                dma((6,)), dma((6,)), dma((6,)), dma((2, loads)), dma((2, loads)),
                dma((group,)), dma((group,)), dma((spaces // group,)), dma((spaces // group,)),
                dma((loads,)), dma((loads,)),
            ],
            compiler_params=pltpu.CompilerParams(collective_id=0, has_side_effects=True, vmem_limit_bytes=LIMIT),
        )(*pinned)
        return pl.pallas_call(
            finish,
            out_shape=(out(1, 3, 2, *plane), out(2, rows, ROWS)),
            in_specs=[held] * 5,
            out_specs=(hbm, hbm),
            scratch_shapes=[vmem(3, 2, *plane), vmem(2, rows, ROWS), dma((4,))],
            compiler_params=pltpu.CompilerParams(vmem_limit_bytes=4 * 2**20),
        )(y0, y1, coef, gsum, scale)

    placed = (
        P("load", None, "space", None, None),
        P("load", None, "space", None, None),
        P("space", None, None),
        P(),
        P("space", None, None),
        P("space", None, None),
    )
    return jax.shard_map(
        shards,
        mesh=mesh,
        in_specs=placed,
        out_specs=(P("load", None, "space", None, None), P("space", "load", None)),
        check_vma=False,
    )
```

```python
import functools

import jax
import jax.numpy as jnp
import numpy as np
from jax import lax
from jax.experimental import pallas as pl
from jax.experimental.pallas import tpu as pltpu
from jax.sharding import PartitionSpec as P

F32 = jnp.float32
MESH = pl.DeviceIdType.MESH
ROWS = 128
TILE = 8
LONG = 8
STEP = 16
CHUNKS = 4
CHUNK = ROWS // CHUNKS
DONE = [0] + [(i + 1) * CHUNK - STEP for i in range(CHUNKS - 1)] + [ROWS]
LIMIT = 40 * 2**20

POISSON = 0.3
SHEAR = 0.5 / (1.0 + POISSON)
KAPPA = 2.0 * POISSON / (1.0 - 2.0 * POISSON)
UNIT = SHEAR / 16.0
DIAG = SHEAR * (KAPPA + 4.0) / 9.0


def shifted_down(value):
    last = lax.broadcasted_iota(jnp.int32, value.shape, 1) == ROWS - 1
    return jnp.where(last, 0.0, pltpu.roll(value, ROWS - 1, 1))


def shifted_up(value):
    first = lax.broadcasted_iota(jnp.int32, value.shape, 1) == 0
    return jnp.where(first, 0.0, pltpu.roll(value, 1, 1))


def plane_modes(here, after):
    total, slope = here + after, after - here
    total_next, slope_next = shifted_down(total), shifted_down(slope)
    return (total + total_next, total_next - total, slope + slope_next, slope_next - slope)


def strains(low, high):
    (u, v, w) = [
        (
            l[1] + h[1],
            l[2] + h[2],
            h[0] - l[0],
            l[3] + h[3],
            h[1] - l[1],
            h[2] - l[2],
            h[3] - l[3],
        )
        for l, h in zip(low, high)
    ]
    return (
        u[0], v[1], w[2],
        u[1] + v[0], u[2] + w[0], v[2] + w[1],
        u[3], w[5], u[4], v[5], v[3], w[4],
        u[5], v[4], w[3],
        u[6], v[6], w[6],
    )


def stresses(e):
    trace = KAPPA * (e[0] + e[1] + e[2])
    out = [2.0 * e[0] + trace, 2.0 * e[1] + trace, 2.0 * e[2] + trace, e[3], e[4], e[5]]
    own, cross = 1.0, KAPPA / 3.0
    for a, b in ((6, 7), (8, 9), (10, 11)):
        both = cross * (e[a] + e[b])
        out += [own * e[a] + both, own * e[b] + both]
    third = 1.0 / 3.0
    shear = (e[12] + e[13] + e[14]) * third
    out += [e[12] * third + shear, e[13] * third + shear, e[14] * third + shear]
    last = (KAPPA + 4.0) / 9.0
    out += [e[15] * last, e[16] * last, e[17] * last]
    return out


def corner_modes(f):
    return (
        (f[0], f[3], f[4], f[6], f[8], f[12], f[15]),
        (f[3], f[1], f[5], f[10], f[13], f[9], f[16]),
        (f[4], f[5], f[2], f[14], f[11], f[7], f[17]),
    )


def onto_lower(g):
    return (-g[2], g[0] - g[4], g[1] - g[5], g[3] - g[6])


def onto_upper(g):
    return (g[2], g[0] + g[4], g[1] + g[5], g[3] + g[6])


def dot(a, b):
    total = None
    for left, right in zip(a, b):
        term = left * right
        total = term if total is None else total + term
    return total


def folded(value):
    total = value[0:TILE]
    for i in range(1, value.shape[0] // TILE):
        total = total + value[i * TILE : (i + 1) * TILE]
    return total


def over_rows(body, size, carry=None, start=0, stop=ROWS):
    at = lambda b: pl.multiple_of(b * size, size)
    first, last = start // size, stop // size
    if carry is None:
        lax.fori_loop(first, last, lambda b, _: (body(at(b)), 0)[1], 0)
        return None
    return lax.fori_loop(first, last, lambda b, held: body(at(b), held), carry)


def kernel(
    fwd_hbm, rhs_hbm, fac_hbm, base_hbm, ids_hbm, msk_hbm,
    x_out, grad_out,
    base, fac, ids, msk, rhs, fw, sc, m, y0, y1, y0h, y1h, inv, r0, r0h, ff, g0, g1, g0r, g1r,
    part, r1, mid, r2, coefs,
    load_sem, halo_send, halo_recv, z_send, z_recv, s1_send, s1_recv, s2_send, s2_recv, known1, known2, known3,
    *, spaces, loads, group,
):
    s = lax.axis_index("space")
    load = lax.axis_index("load")
    above, below = lax.rem(s + 1, spaces), lax.rem(s + spaces - 1, spaces)
    wide = spaces // group
    within, outer = lax.rem(s, group), s // group
    rows = ROWS // loads

    def local(src, dst, index):
        return pltpu.make_async_copy(src, dst, load_sem.at[index])

    loaded = [
        local(base_hbm, base, 5),
        local(fac_hbm, fac, 0),
        local(ids_hbm, ids, 1),
        local(msk_hbm, msk, 2),
        local(rhs_hbm.at[0], rhs, 3),
        local(fwd_hbm.at[0, :, pl.ds(0, 2)], fw.at[:, pl.ds(0, 2), pl.ds(0, ROWS)], 4),
    ]
    for copy in loaded:
        copy.start()

    core, y = lax.rem(s, 2), lax.rem(s // 2, LONG)
    at_y = lambda step, c: {"space": outer * group + lax.rem(y + LONG + step, LONG) * 2 + c}
    at_x = lambda step: {"space": lax.rem(outer + wide + step, wide) * group + within}
    at_z = lambda step: {"load": lax.rem(load + loads + step, loads)}

    near = [{"space": above}, {"space": below}, at_y(0, 1 - core)]
    near += [at_y(step, c) for step in (1, -1) for c in range(2)] + [at_x(1), at_x(-1), at_z(1), at_z(-1)]
    next1 = [at_y(1, core), at_y(-1, core), at_x(1), at_x(-1), at_z(1), at_z(-1)]
    next2 = [at_y(2, core), at_y(-2, core), at_z(2), at_z(-2)]
    next3 = [at_x(1), at_x(-1), at_x(2)]

    def tell(sem, peers):
        for peer in peers:
            pl.semaphore_signal(sem, inc=1, device_id=peer, device_id_type=MESH)

    barrier = pltpu.get_barrier_semaphore()
    tell(barrier, near)

    stage1 = [lax.rem(within + i, group) for i in range(1, group)]
    peers1 = [{"space": outer * group + i} for i in stage1]
    stage2 = [(lax.rem(outer + i, wide), lax.rem(load + j, loads)) for i in range(wide) for j in range(loads)][1:]
    peers2 = [{"space": i * group + within, "load": j} for i, j in stage2]
    stage3 = [lax.rem(load + i, loads) for i in range(1, loads)]
    peers3 = [{"load": i} for i in stage3]

    def remote(src, dst, send, recv, device):
        return pltpu.make_async_remote_copy(
            src_ref=src, dst_ref=dst, send_sem=send, recv_sem=recv, device_id=device, device_id_type=MESH
        )

    zero = jnp.zeros((TILE, ROWS), F32)
    past = slice(ROWS, ROWS + TILE)
    for layer in range(4):
        m[layer, 0:TILE, :] = zero
    for c in range(3):
        y1h[c, past, :] = zero
        for plane in range(2):
            y0[c, plane, past, :] = zero
            y0h[c, plane, past, :] = zero
            y1[c, plane, past, :] = zero
        for plane in range(3):
            fw[c, plane, past, :] = zero

    for copy in loaded[:3]:
        copy.wait()
    bases = [base[i] for i in range(base.shape[0])]

    def moduli(row, n=16):
        at = pl.ds(row, n)
        for layer in range(2):
            zone = ids[layer, at, :]
            scale = jnp.full((n, ROWS), bases[0], F32)
            for i in range(1, len(bases)):
                scale = jnp.where(zone == i, bases[i], scale)
            sc[layer, at, :] = scale
            m[1 + layer, pl.ds(row + TILE, n), :] = fac[layer, at, :] * scale

    over_rows(moduli, 16)
    loaded[3].wait()
    loaded[4].wait()

    def inverse_diagonal(low, high, row, n):
        here = m[low, pl.ds(row + TILE, n), :] + m[high, pl.ds(row + TILE, n), :]
        before = m[low, pl.ds(row + TILE - 1, n), :] + m[high, pl.ds(row + TILE - 1, n), :]
        total = here + before
        return 1.0 / (DIAG * (total + shifted_up(total)))

    def own_first(row, n=64):
        at = pl.ds(row, n)
        free_low = (1 - msk[0, at, :]).astype(F32)
        free_high = (1 - msk[1, at, :]).astype(F32)
        inverse = free_high * inverse_diagonal(1, 2, row, n)
        inv[1, at, :] = inverse
        for c in range(3):
            r0[c, 0, at, :] = free_low * rhs[c, 0, at, :]
            high = free_high * rhs[c, 1, at, :]
            r0[c, 1, at, :] = high
            y0[c, 1, at, :] = inverse * high

    over_rows(own_first, 64)

    pl.semaphore_wait(barrier, len(near))
    tell(known1, next1)
    body_rows = pl.ds(TILE, ROWS)
    whole = pl.ds(0, ROWS)
    has_above, has_below = s < spaces - 1, s > 0
    up, down = {"space": above}, {"space": below}

    def start_up(*copies):
        @pl.when(has_above)
        def _():
            for copy in copies:
                copy.start()

    def start_down(*copies):
        @pl.when(has_below)
        def _():
            for copy in copies:
                copy.start()

    m_up = remote(m.at[2, body_rows], m.at[0, body_rows], halo_send.at[0], halo_recv.at[0], up)
    m_down = remote(m.at[1, body_rows], m.at[3, body_rows], halo_send.at[1], halo_recv.at[1], down)
    r_down, y_up, y1_down = [], [], []
    for i in range(CHUNKS):
        part_rows = pl.ds(i * CHUNK, CHUNK)
        r_down.append(
            remote(r0.at[:, 0, part_rows], r0h.at[:, part_rows], halo_send.at[3 + i], halo_recv.at[3 + i], down)
        )
        y_up.append(
            remote(
                y0.at[:, 1, part_rows], y0h.at[:, 0, part_rows],
                halo_send.at[3 + CHUNKS + i], halo_recv.at[3 + CHUNKS + i], up,
            )
        )
        done = pl.ds(DONE[i], DONE[i + 1] - DONE[i])
        y1_down.append(
            remote(
                y1.at[:, 0, done], y1h.at[:, done],
                halo_send.at[3 + 2 * CHUNKS + i], halo_recv.at[3 + 2 * CHUNKS + i], down,
            )
        )
    start_up(m_up, *y_up)
    start_down(m_down, *r_down)
    loaded[5].wait()
    f_down = remote(fw.at[:, 0, whole], fw.at[:, 2, whole], halo_send.at[2], halo_recv.at[2], down)
    start_down(f_down)

    def cleared(ref):
        def body(row):
            ref[pl.ds(row, 32), :] = jnp.zeros((32, ROWS), F32)

        over_rows(body, 32)

    @pl.when(s == 0)
    def _():
        cleared(m.at[0, body_rows])
        for c in range(3):
            cleared(y0h.at[c, 0])

    @pl.when(s == spaces - 1)
    def _():
        cleared(m.at[3, body_rows])
        for c in range(3):
            cleared(r0h.at[c])
            cleared(fw.at[c, 2])
            cleared(y1h.at[c])

    def wait_from_below(*copies):
        @pl.when(has_below)
        def _():
            for copy in copies:
                copy.wait_recv()

    def wait_from_above(*copies):
        @pl.when(has_above)
        def _():
            for copy in copies:
                copy.wait_recv()

    def modes(plane, row, n):
        return [plane_modes(ref[pl.ds(row, n), :], ref[pl.ds(row + 1, n), :]) for ref in plane]

    y0_planes = [
        [y0h.at[c, 0] for c in range(3)],
        [y0.at[c, 0] for c in range(3)],
        [y0.at[c, 1] for c in range(3)],
        [y0h.at[c, 1] for c in range(3)],
    ]
    y1_planes = [
        [y1.at[c, 0] for c in range(3)],
        [y1.at[c, 1] for c in range(3)],
        [y1h.at[c] for c in range(3)],
    ]

    def forward_stress(layer, n):
        def body(row):
            low = modes([fw.at[c, layer] for c in range(3)], row, n)
            high = modes([fw.at[c, layer + 1] for c in range(3)], row, n)
            for i, value in enumerate(stresses(strains(low, high))):
                ff[layer, i, pl.ds(row, n), :] = value

        over_rows(body, n)

    forward_stress(0, 32)

    wait_from_below(m_up)
    wait_from_above(m_down)
    pl.semaphore_wait(known1, len(next1))
    tell(known2, next2)

    def own_second(row, n=CHUNK):
        at = pl.ds(row, n)
        inverse = (1 - msk[0, at, :]).astype(F32) * inverse_diagonal(0, 1, row, n)
        inv[0, at, :] = inverse
        beyond = inverse_diagonal(2, 3, row, n)
        for c in range(3):
            y0[c, 0, at, :] = inverse * r0[c, 0, at, :]
            y0h[c, 1, at, :] = beyond * r0h[c, at, :]

    def product(row, held, n=16):
        carried, norm, curve, next_norm = held
        at = pl.ds(row, n)
        row_first = lax.broadcasted_iota(jnp.int32, (TILE, ROWS), 0) == 0
        planes = [modes(plane, row, n) for plane in y0_planes]
        onto = [None, None]
        for layer in range(3):
            modulus = UNIT * m[layer, pl.ds(row + TILE, n), :]
            force = corner_modes([modulus * f for f in stresses(strains(planes[layer], planes[layer + 1]))])
            for plane, spread in ((layer - 1, onto_lower), (layer, onto_upper)):
                if 0 <= plane < 2:
                    new = [spread(g) for g in force]
                    if onto[plane] is None:
                        onto[plane] = new
                    else:
                        onto[plane] = [tuple(a + b for a, b in zip(o, w)) for o, w in zip(onto[plane], new)]
        passed = []
        for plane in range(2):
            inverse = inv[plane, at, :]
            for c in range(3):
                g = onto[plane][c]
                sums = (g[0] - g[1]) + shifted_up(g[0] + g[1])
                slopes = (g[2] - g[3]) + shifted_up(g[2] + g[3])
                rolled = pltpu.roll(sums + slopes, 1, 0)
                head = jnp.where(row_first, carried[3 * plane + c], rolled[0:TILE])
                passed.append(rolled[0:TILE])
                if n > TILE:
                    head = jnp.concatenate([head, rolled[TILE:n]], axis=0)
                force = (sums - slopes) + head
                image = inverse * force
                y1[c, plane, at, :] = image
                field = y0[c, plane, at, :]
                norm = norm + folded(r0[c, plane, at, :] * field)
                curve = curve + folded(force * field)
                next_norm = next_norm + folded(force * image)
        return tuple(passed), norm, curve, next_norm

    held = ((zero,) * 6, zero, zero, zero)
    for i in range(CHUNKS):
        wait_from_above(r_down[i])
        wait_from_below(y_up[i])
        over_rows(own_second, CHUNK, None, i * CHUNK, (i + 1) * CHUNK)
        held = over_rows(product, STEP, held, DONE[i], DONE[i + 1])
        start_down(y1_down[i])
    _, norm, curve, next_norm = held
    pl.semaphore_wait(known2, len(next2))
    tell(known3, next3)

    def against_forward(planes, out, n):
        def body(row):
            all_modes = [modes(plane, row, n) for plane in planes]
            at = pl.ds(row, n)
            for layer in range(2):
                e = strains(all_modes[layer], all_modes[layer + 1])
                out[layer, at, :] = UNIT * dot(e, [ff[layer, j, at, :] for j in range(18)])

        over_rows(body, n)

    def energy_of(layer, n):
        def body(row, held):
            e = strains(modes(y1_planes[layer], row, n), modes(y1_planes[layer + 1], row, n))
            return held + folded((UNIT * m[1 + layer, pl.ds(row + TILE, n), :]) * dot(e, stresses(e)))

        return body

    energy = over_rows(energy_of(0, 32), 32, zero)
    wait_from_above(f_down)
    forward_stress(1, 32)
    against_forward(y0_planes[1:4], g0, 16)

    def exchange(src, dst, sems):
        copies = []
        for slot, peer in zip(stage3, peers3):
            copy = remote(
                src.at[:, pl.ds(pl.multiple_of(slot * rows, rows), rows)], dst.at[load],
                z_send.at[sems, slot], z_recv.at[sems, load], peer,
            )
            copy.start()
            copies.append(copy)
        return copies

    sent = exchange(g0, g0r, 0)
    for i in range(CHUNKS):
        wait_from_above(y1_down[i])
        first, last = DONE[i] - STEP, DONE[i + 1] - STEP
        energy = over_rows(energy_of(1, STEP), STEP, energy, max(first, 0), ROWS if i == CHUNKS - 1 else last)

    lane = lax.broadcasted_iota(jnp.int32, (1, ROWS), 1)
    quarter = ROWS // 4
    sums = [jnp.sum(jnp.sum(v, axis=0, keepdims=True), axis=1, keepdims=True) for v in (norm, curve, next_norm, energy)]
    part[...] = jnp.where(
        lane < 2 * quarter,
        jnp.where(lane < quarter, sums[0], sums[1]),
        jnp.where(lane < 3 * quarter, sums[2], sums[3]),
    )
    for slot, peer in zip(stage1, peers1):
        copy = remote(part, r1.at[within], s1_send.at[slot], s1_recv.at[within], peer)
        copy.start()
        sent.append(copy)
    r1[within] = part[...]
    against_forward(y1_planes, g1, 16)
    sent += exchange(g1, g1r, 1)

    for slot in stage1:
        remote(part, r1.at[slot], s1_send.at[slot], s1_recv.at[slot], up).wait_recv()
    total = r1[0]
    for i in range(1, group):
        total = total + r1[i]
    mid[...] = total
    pl.semaphore_wait(known3, len(next3))
    for (i, j), peer in zip(stage2, peers2):
        copy = remote(mid, r2.at[outer, load], s2_send.at[i, j], s2_recv.at[outer, load], peer)
        copy.start()
        sent.append(copy)
    r2[outer, load] = total

    def arrived(slots):
        for i, j in slots:
            remote(mid, r2.at[i, j], s2_send.at[i, j], s2_recv.at[i, j], up).wait_recv()

    def coefficients(sums):
        rr, rq, qq, qd = [sums[:, i * quarter : i * quarter + 1] for i in range(4)]
        step = rr / rq
        norm_next = step * (step * qq) - rr
        ratio = norm_next / rr
        curve_next = rq - 2.0 * (step * qq) + step * (step * qd)
        step_next = norm_next / (curve_next - ratio * norm_next / step)
        return step + step_next * (1.0 + ratio), -(step_next * step)

    def summed(j):
        total = r2[0, j]
        for i in range(1, wide):
            total = total + r2[i, j]
        return total

    arrived(stage2[loads * 1 - 1 :: loads])
    first, second = coefficients(summed(load))

    def solve(row, n=32):
        at = pl.ds(row, n)
        for c in range(3):
            for plane in range(2):
                x_out[c, plane, at, :] = first * y0[c, plane, at, :] + second * y1[c, plane, at, :]

    over_rows(solve, 32)

    mine = pl.ds(pl.multiple_of(load * rows, rows), rows)
    g0r[load] = g0[:, mine, :]
    g1r[load] = g1[:, mine, :]
    for slot in stage3:
        remote(g0.at[:, pl.ds(0, rows)], g0r.at[slot], z_send.at[0, slot], z_recv.at[0, slot], up).wait_recv()
        remote(g1.at[:, pl.ds(0, rows)], g1r.at[slot], z_send.at[1, slot], z_recv.at[1, slot], up).wait_recv()
    arrived([(i, j) for k, (i, j) in enumerate(stage2) if (k + 1) % loads])
    first, second = coefficients(jnp.concatenate([summed(j) for j in range(loads)], axis=0))
    coefs[0] = jnp.broadcast_to(first, (loads, ROWS))
    coefs[1] = jnp.broadcast_to(second, (loads, ROWS))
    total = None
    for i in range(loads):
        term = coefs[0, i : i + 1, :][None] * g0r[i] + coefs[1, i : i + 1, :][None] * g1r[i]
        total = term if total is None else total + term
    grad_out[...] = sc[:, mine, :] * total

    @pl.when(has_above)
    def _():
        for copy in (m_up, *y_up):
            copy.wait_send()

    @pl.when(has_below)
    def _():
        for copy in (m_down, f_down, *r_down, *y1_down):
            copy.wait_send()

    for copy in sent:
        copy.wait_send()


def finish(x, grad, x_out, grad_out, sem):
    copies = [pltpu.make_async_copy(x, x_out.at[0], sem.at[0]), pltpu.make_async_copy(grad, grad_out, sem.at[1])]
    for copy in copies:
        copy.start()
    for copy in copies:
        copy.wait()


def solution(mesh):
    spaces, loads = mesh.shape["space"], mesh.shape["load"]
    group = 2 * LONG
    rows = ROWS // loads

    def shards(forward_disp, adjoint_rhs, modulus_factor, zone_base, zone_ids, fixed_mask):
        plane = (ROWS, ROWS)
        padded = (ROWS + TILE, ROWS)
        vmem = lambda *shape: pltpu.VMEM(shape, F32)
        ints = lambda *shape: pltpu.VMEM(shape, jnp.int32)
        dma = pltpu.SemaphoreType.DMA
        hbm = pl.BlockSpec(memory_space=pltpu.HBM)
        held = pl.BlockSpec(memory_space=pltpu.VMEM)
        out = lambda *shape: jax.ShapeDtypeStruct(shape, F32)
        pinned = [
            pltpu.with_memory_space_constraint(a, pltpu.HBM)
            for a in (forward_disp, adjoint_rhs, modulus_factor, zone_base, zone_ids, fixed_mask)
        ]
        x, grad = pl.pallas_call(
            functools.partial(kernel, spaces=spaces, loads=loads, group=group),
            out_shape=(out(3, 2, *plane), out(2, rows, ROWS)),
            in_specs=[hbm] * 6,
            out_specs=(held,) * 2,
            scratch_shapes=[
                pltpu.SMEM(zone_base.shape, F32),
                vmem(2, *plane), ints(2, *plane), ints(2, *plane), vmem(3, 2, *plane), vmem(3, 3, *padded),
                vmem(2, *plane), vmem(4, *padded), vmem(3, 2, *padded), vmem(3, 2, *padded), vmem(3, 2, *padded), vmem(3, *padded),
                vmem(2, *plane), vmem(3, 2, *plane), vmem(3, *plane), vmem(2, 18, *plane),
                vmem(2, *plane), vmem(2, *plane), vmem(loads, 2, rows, ROWS), vmem(loads, 2, rows, ROWS),
                vmem(1, ROWS), vmem(group, 1, ROWS), vmem(1, ROWS), vmem(spaces // group, loads, 1, ROWS),
                vmem(2, loads, ROWS),
                dma((6,)), dma((3 + 3 * CHUNKS,)), dma((3 + 3 * CHUNKS,)), dma((2, loads)), dma((2, loads)),
                dma((group,)), dma((group,)), dma((spaces // group, loads)), dma((spaces // group, loads)),
                *[pltpu.SemaphoreType.REGULAR] * 3,
            ],
            compiler_params=pltpu.CompilerParams(collective_id=0, has_side_effects=True, vmem_limit_bytes=LIMIT),
        )(*pinned)
        return pl.pallas_call(
            finish,
            out_shape=(out(1, 3, 2, *plane), out(2, rows, ROWS)),
            in_specs=[held] * 2,
            out_specs=(hbm, hbm),
            scratch_shapes=[dma((2,))],
            compiler_params=pltpu.CompilerParams(vmem_limit_bytes=4 * 2**20),
        )(x, grad)

    placed = (
        P("load", None, "space", None, None),
        P("load", None, "space", None, None),
        P("space", None, None),
        P(),
        P("space", None, None),
        P("space", None, None),
    )
    return jax.shard_map(
        shards,
        mesh=mesh,
        in_specs=placed,
        out_specs=(P("load", None, "space", None, None), P("space", "load", None)),
        check_vma=False,
    )
```

```python
import functools

import jax
import jax.numpy as jnp
import numpy as np
from jax import lax
from jax.experimental import pallas as pl
from jax.experimental.pallas import tpu as pltpu
from jax.sharding import PartitionSpec as P

F32 = jnp.float32
MESH = pl.DeviceIdType.MESH
ROWS = 128
TILE = 8
LONG = 8
STEP = 16
CHUNKS = 4
CHUNK = ROWS // CHUNKS
DONE = [0] + [(i + 1) * CHUNK - STEP for i in range(CHUNKS - 1)] + [ROWS]
LIMIT = 40 * 2**20

POISSON = 0.3
SHEAR = 0.5 / (1.0 + POISSON)
KAPPA = 2.0 * POISSON / (1.0 - 2.0 * POISSON)
UNIT = SHEAR / 16.0
DIAG = SHEAR * (KAPPA + 4.0) / 9.0


def shifted_down(value):
    last = lax.broadcasted_iota(jnp.int32, value.shape, 1) == ROWS - 1
    return jnp.where(last, 0.0, pltpu.roll(value, ROWS - 1, 1))


def shifted_up(value):
    first = lax.broadcasted_iota(jnp.int32, value.shape, 1) == 0
    return jnp.where(first, 0.0, pltpu.roll(value, 1, 1))


def plane_modes(here, after):
    total, slope = here + after, after - here
    total_next, slope_next = shifted_down(total), shifted_down(slope)
    return (total + total_next, total_next - total, slope + slope_next, slope_next - slope)


def strains(low, high):
    (u, v, w) = [
        (
            l[1] + h[1],
            l[2] + h[2],
            h[0] - l[0],
            l[3] + h[3],
            h[1] - l[1],
            h[2] - l[2],
            h[3] - l[3],
        )
        for l, h in zip(low, high)
    ]
    return (
        u[0], v[1], w[2],
        u[1] + v[0], u[2] + w[0], v[2] + w[1],
        u[3], w[5], u[4], v[5], v[3], w[4],
        u[5], v[4], w[3],
        u[6], v[6], w[6],
    )


def stresses(e):
    trace = KAPPA * (e[0] + e[1] + e[2])
    out = [2.0 * e[0] + trace, 2.0 * e[1] + trace, 2.0 * e[2] + trace, e[3], e[4], e[5]]
    own, cross = 1.0, KAPPA / 3.0
    for a, b in ((6, 7), (8, 9), (10, 11)):
        both = cross * (e[a] + e[b])
        out += [own * e[a] + both, own * e[b] + both]
    third = 1.0 / 3.0
    shear = (e[12] + e[13] + e[14]) * third
    out += [e[12] * third + shear, e[13] * third + shear, e[14] * third + shear]
    last = (KAPPA + 4.0) / 9.0
    out += [e[15] * last, e[16] * last, e[17] * last]
    return out


def corner_modes(f):
    return (
        (f[0], f[3], f[4], f[6], f[8], f[12], f[15]),
        (f[3], f[1], f[5], f[10], f[13], f[9], f[16]),
        (f[4], f[5], f[2], f[14], f[11], f[7], f[17]),
    )


def onto_lower(g):
    return (-g[2], g[0] - g[4], g[1] - g[5], g[3] - g[6])


def onto_upper(g):
    return (g[2], g[0] + g[4], g[1] + g[5], g[3] + g[6])


def dot(a, b):
    total = None
    for left, right in zip(a, b):
        term = left * right
        total = term if total is None else total + term
    return total


def folded(value):
    total = value[0:TILE]
    for i in range(1, value.shape[0] // TILE):
        total = total + value[i * TILE : (i + 1) * TILE]
    return total


def over_rows(body, size, carry=None, start=0, stop=ROWS):
    at = lambda b: pl.multiple_of(b * size, size)
    first, last = start // size, stop // size
    if carry is None:
        lax.fori_loop(first, last, lambda b, _: (body(at(b)), 0)[1], 0)
        return None
    return lax.fori_loop(first, last, lambda b, held: body(at(b), held), carry)


def kernel(
    fwd_hbm, rhs_hbm, fac_hbm, base_hbm, ids_hbm, msk_hbm,
    x_hbm, grad_hbm,
    x_out, grad_out, base, fac, ids, msk, rhs, fw, sc, m, y0, y1, y0h, y1h, inv, r0, r0h, ff, g0, g1, gr,
    part, r1, mid, r2, coefs,
    load_sem, halo_send, halo_recv, sum_send, sum_recv, known1, known2, known3,
    *, spaces, loads, group,
):
    s = lax.axis_index("space")
    load = lax.axis_index("load")
    above, below = lax.rem(s + 1, spaces), lax.rem(s + spaces - 1, spaces)
    wide = spaces // group
    within, outer = lax.rem(s, group), s // group
    rows = ROWS // loads

    def local(src, dst, index):
        return pltpu.make_async_copy(src, dst, load_sem.at[index])

    loaded = [
        local(base_hbm, base, 5),
        local(fac_hbm, fac, 0),
        local(ids_hbm, ids, 1),
        local(msk_hbm, msk, 2),
        local(rhs_hbm.at[0], rhs, 3),
        local(fwd_hbm.at[0, :, pl.ds(0, 2)], fw.at[:, pl.ds(0, 2), pl.ds(0, ROWS)], 4),
    ]
    for copy in loaded:
        copy.start()

    core, y = lax.rem(s, 2), lax.rem(s // 2, LONG)
    at_y = lambda step, c: {"space": outer * group + lax.rem(y + LONG + step, LONG) * 2 + c}
    at_x = lambda step: {"space": lax.rem(outer + wide + step, wide) * group + within}
    at_z = lambda step: {"load": lax.rem(load + loads + step, loads)}

    near = [{"space": above}, {"space": below}, at_y(0, 1 - core)]
    near += [at_y(step, c) for step in (1, -1) for c in range(2)] + [at_x(1), at_x(-1), at_z(1), at_z(-1)]
    next1 = [at_y(1, core), at_y(-1, core), at_x(1), at_x(-1), at_z(1), at_z(-1)]
    next2 = [at_y(2, core), at_y(-2, core), at_z(2), at_z(-2)]
    next3 = [at_x(1), at_x(-1), at_x(2)]

    def tell(sem, peers):
        for peer in peers:
            pl.semaphore_signal(sem, inc=1, device_id=peer, device_id_type=MESH)

    barrier = pltpu.get_barrier_semaphore()
    tell(barrier, near)

    stage1 = [lax.rem(within + i, group) for i in range(1, group)]
    peers1 = [{"space": outer * group + i} for i in stage1]
    stage2 = [lax.rem(outer + i, wide) * group + within for i in range(wide)]
    peers_own = [{"space": i} for i in stage2[1:]]
    peers_other = [{"space": i, "load": lax.rem(load + j, loads)} for i in stage2 for j in range(1, loads)]
    stage3 = [lax.rem(load + i, loads) for i in range(1, loads)]
    peers3 = [{"load": i} for i in stage3]

    def remote(src, dst, send, recv, device):
        return pltpu.make_async_remote_copy(
            src_ref=src, dst_ref=dst, send_sem=send, recv_sem=recv, device_id=device, device_id_type=MESH
        )

    zero = jnp.zeros((TILE, ROWS), F32)
    past = slice(ROWS, ROWS + TILE)
    for layer in range(4):
        m[layer, 0:TILE, :] = zero
    for c in range(3):
        y1h[c, past, :] = zero
        for plane in range(2):
            y0[c, plane, past, :] = zero
            y0h[c, plane, past, :] = zero
            y1[c, plane, past, :] = zero
        for plane in range(3):
            fw[c, plane, past, :] = zero

    for copy in loaded[:3]:
        copy.wait()
    bases = [base[i] for i in range(base.shape[0])]

    def moduli(row, n=16):
        at = pl.ds(row, n)
        for layer in range(2):
            zone = ids[layer, at, :]
            scale = jnp.full((n, ROWS), bases[0], F32)
            for i in range(1, len(bases)):
                scale = jnp.where(zone == i, bases[i], scale)
            sc[layer, at, :] = scale
            m[1 + layer, pl.ds(row + TILE, n), :] = fac[layer, at, :] * scale

    over_rows(moduli, 16)
    loaded[3].wait()
    loaded[4].wait()

    def inverse_diagonal(low, high, row, n):
        here = m[low, pl.ds(row + TILE, n), :] + m[high, pl.ds(row + TILE, n), :]
        before = m[low, pl.ds(row + TILE - 1, n), :] + m[high, pl.ds(row + TILE - 1, n), :]
        total = here + before
        return 1.0 / (DIAG * (total + shifted_up(total)))

    def own_first(row, n=64):
        at = pl.ds(row, n)
        free_low = (1 - msk[0, at, :]).astype(F32)
        free_high = (1 - msk[1, at, :]).astype(F32)
        inverse = free_high * inverse_diagonal(1, 2, row, n)
        inv[1, at, :] = inverse
        for c in range(3):
            r0[c, 0, at, :] = free_low * rhs[c, 0, at, :]
            high = free_high * rhs[c, 1, at, :]
            r0[c, 1, at, :] = high
            y0[c, 1, at, :] = inverse * high

    over_rows(own_first, 64)

    pl.semaphore_wait(barrier, len(near))
    tell(known1, next1)
    body_rows = pl.ds(TILE, ROWS)
    whole = pl.ds(0, ROWS)
    has_above, has_below = s < spaces - 1, s > 0
    up, down = {"space": above}, {"space": below}

    def start_up(*copies):
        @pl.when(has_above)
        def _():
            for copy in copies:
                copy.start()

    def start_down(*copies):
        @pl.when(has_below)
        def _():
            for copy in copies:
                copy.start()

    m_up = remote(m.at[2, body_rows], m.at[0, body_rows], halo_send.at[0], halo_recv.at[0], up)
    m_down = remote(m.at[1, body_rows], m.at[3, body_rows], halo_send.at[1], halo_recv.at[1], down)
    r_down, y_up, y1_down = [], [], []
    for i in range(CHUNKS):
        part_rows = pl.ds(i * CHUNK, CHUNK)
        r_down.append(
            remote(r0.at[:, 0, part_rows], r0h.at[:, part_rows], halo_send.at[1], halo_recv.at[3 + i], down)
        )
        y_up.append(
            remote(
                y0.at[:, 1, part_rows], y0h.at[:, 0, part_rows],
                halo_send.at[0], halo_recv.at[3 + CHUNKS + i], up,
            )
        )
        done = pl.ds(DONE[i], DONE[i + 1] - DONE[i])
        y1_down.append(
            remote(
                y1.at[:, 0, done], y1h.at[:, done],
                halo_send.at[1], halo_recv.at[3 + 2 * CHUNKS + i], down,
            )
        )
    start_up(m_up, *y_up)
    start_down(m_down, *r_down)
    loaded[5].wait()
    f_down = remote(fw.at[:, 0, whole], fw.at[:, 2, whole], halo_send.at[1], halo_recv.at[2], down)
    start_down(f_down)

    def cleared(ref):
        def body(row):
            ref[pl.ds(row, 32), :] = jnp.zeros((32, ROWS), F32)

        over_rows(body, 32)

    @pl.when(s == 0)
    def _():
        cleared(m.at[0, body_rows])
        for c in range(3):
            cleared(y0h.at[c, 0])

    @pl.when(s == spaces - 1)
    def _():
        cleared(m.at[3, body_rows])
        for c in range(3):
            cleared(r0h.at[c])
            cleared(fw.at[c, 2])
            cleared(y1h.at[c])

    def wait_from_below(*copies):
        @pl.when(has_below)
        def _():
            for copy in copies:
                copy.wait_recv()

    def wait_from_above(*copies):
        @pl.when(has_above)
        def _():
            for copy in copies:
                copy.wait_recv()

    def modes(plane, row, n):
        return [plane_modes(ref[pl.ds(row, n), :], ref[pl.ds(row + 1, n), :]) for ref in plane]

    y0_planes = [
        [y0h.at[c, 0] for c in range(3)],
        [y0.at[c, 0] for c in range(3)],
        [y0.at[c, 1] for c in range(3)],
        [y0h.at[c, 1] for c in range(3)],
    ]
    y1_planes = [
        [y1.at[c, 0] for c in range(3)],
        [y1.at[c, 1] for c in range(3)],
        [y1h.at[c] for c in range(3)],
    ]

    def forward_stress(layer, n):
        def body(row):
            low = modes([fw.at[c, layer] for c in range(3)], row, n)
            high = modes([fw.at[c, layer + 1] for c in range(3)], row, n)
            for i, value in enumerate(stresses(strains(low, high))):
                ff[layer, i, pl.ds(row, n), :] = value

        over_rows(body, n)

    forward_stress(0, 32)

    wait_from_below(m_up)
    wait_from_above(m_down)
    pl.semaphore_wait(known1, len(next1))
    tell(known2, next2)

    def own_second(row, n=CHUNK):
        at = pl.ds(row, n)
        inverse = (1 - msk[0, at, :]).astype(F32) * inverse_diagonal(0, 1, row, n)
        inv[0, at, :] = inverse
        beyond = inverse_diagonal(2, 3, row, n)
        for c in range(3):
            y0[c, 0, at, :] = inverse * r0[c, 0, at, :]
            y0h[c, 1, at, :] = beyond * r0h[c, at, :]

    def product(row, held, n=16):
        carried, norm, curve, next_norm = held
        at = pl.ds(row, n)
        row_first = lax.broadcasted_iota(jnp.int32, (TILE, ROWS), 0) == 0
        planes = [modes(plane, row, n) for plane in y0_planes]
        onto = [None, None]
        for layer in range(3):
            modulus = UNIT * m[layer, pl.ds(row + TILE, n), :]
            force = corner_modes([modulus * f for f in stresses(strains(planes[layer], planes[layer + 1]))])
            for plane, spread in ((layer - 1, onto_lower), (layer, onto_upper)):
                if 0 <= plane < 2:
                    new = [spread(g) for g in force]
                    if onto[plane] is None:
                        onto[plane] = new
                    else:
                        onto[plane] = [tuple(a + b for a, b in zip(o, w)) for o, w in zip(onto[plane], new)]
        passed = []
        for plane in range(2):
            inverse = inv[plane, at, :]
            for c in range(3):
                g = onto[plane][c]
                sums = (g[0] - g[1]) + shifted_up(g[0] + g[1])
                slopes = (g[2] - g[3]) + shifted_up(g[2] + g[3])
                rolled = pltpu.roll(sums + slopes, 1, 0)
                head = jnp.where(row_first, carried[3 * plane + c], rolled[0:TILE])
                passed.append(rolled[0:TILE])
                if n > TILE:
                    head = jnp.concatenate([head, rolled[TILE:n]], axis=0)
                force = (sums - slopes) + head
                image = inverse * force
                y1[c, plane, at, :] = image
                field = y0[c, plane, at, :]
                norm = norm + folded(r0[c, plane, at, :] * field)
                curve = curve + folded(force * field)
                next_norm = next_norm + folded(force * image)
        return tuple(passed), norm, curve, next_norm

    held = ((zero,) * 6, zero, zero, zero)
    for i in range(CHUNKS):
        wait_from_above(r_down[i])
        wait_from_below(y_up[i])
        over_rows(own_second, CHUNK, None, i * CHUNK, (i + 1) * CHUNK)
        held = over_rows(product, STEP, held, DONE[i], DONE[i + 1])
        start_down(y1_down[i])
    _, norm, curve, next_norm = held
    pl.semaphore_wait(known2, len(next2))
    tell(known3, next3)

    def against_forward(planes, out, n):
        def body(row):
            all_modes = [modes(plane, row, n) for plane in planes]
            at = pl.ds(row, n)
            for layer in range(2):
                e = strains(all_modes[layer], all_modes[layer + 1])
                out[layer, at, :] = UNIT * dot(e, [ff[layer, j, at, :] for j in range(18)])

        over_rows(body, n)

    def energy_of(layer, n):
        def body(row, held):
            e = strains(modes(y1_planes[layer], row, n), modes(y1_planes[layer + 1], row, n))
            return held + folded((UNIT * m[1 + layer, pl.ds(row + TILE, n), :]) * dot(e, stresses(e)))

        return body

    energy = over_rows(energy_of(0, 32), 32, zero)
    wait_from_above(f_down)
    forward_stress(1, 32)
    against_forward(y0_planes[1:4], g0, 16)

    def taken(sem, ref):
        pltpu.make_async_copy(ref, ref, sem).wait()

    def exchange(src, slots):
        for slot, peer in zip(stage3, peers3):
            remote(
                src.at[:, pl.ds(pl.multiple_of(slot * rows, rows), rows)], gr.at[slots + load],
                sum_send.at[0], sum_recv.at[0], peer,
            ).start()

    exchange(g0, 0)
    for i in range(CHUNKS):
        wait_from_above(y1_down[i])
        first, last = DONE[i] - STEP, DONE[i + 1] - STEP
        energy = over_rows(energy_of(1, STEP), STEP, energy, max(first, 0), ROWS if i == CHUNKS - 1 else last)

    lane = lax.broadcasted_iota(jnp.int32, (1, ROWS), 1)
    quarter = ROWS // 4
    sums = [jnp.sum(jnp.sum(v, axis=0, keepdims=True), axis=1, keepdims=True) for v in (norm, curve, next_norm, energy)]
    part[...] = jnp.where(
        lane < 2 * quarter,
        jnp.where(lane < quarter, sums[0], sums[1]),
        jnp.where(lane < 3 * quarter, sums[2], sums[3]),
    )
    for peer in peers1:
        remote(part, r1.at[within], sum_send.at[1], sum_recv.at[1], peer).start()
    r1[within] = part[...]
    against_forward(y1_planes, g1, 16)
    exchange(g1, loads)

    taken(sum_recv.at[1], r1.at[pl.ds(0, group - 1)])
    total = r1[0]
    for i in range(1, group):
        total = total + r1[i]
    mid[...] = total
    pl.semaphore_wait(known3, len(next3))
    for peer in peers_own:
        remote(mid, r2.at[outer, load], sum_send.at[2], sum_recv.at[2], peer).start()
    for peer in peers_other:
        remote(mid, r2.at[outer, load], sum_send.at[3], sum_recv.at[3], peer).start()
    r2[outer, load] = total

    def coefficients(sums):
        rr, rq, qq, qd = [sums[:, i * quarter : i * quarter + 1] for i in range(4)]
        step = rr / rq
        norm_next = step * (step * qq) - rr
        ratio = norm_next / rr
        curve_next = rq - 2.0 * (step * qq) + step * (step * qd)
        step_next = norm_next / (curve_next - ratio * norm_next / step)
        return step + step_next * (1.0 + ratio), -(step_next * step)

    def summed(j):
        total = r2[0, j]
        for i in range(1, wide):
            total = total + r2[i, j]
        return total

    taken(sum_recv.at[2], r2.at[pl.ds(0, wide - 1), 0])
    first, second = coefficients(summed(load))

    def solve(row, n=32):
        at = pl.ds(row, n)
        for c in range(3):
            for plane in range(2):
                x_out[c, plane, at, :] = first * y0[c, plane, at, :] + second * y1[c, plane, at, :]

    over_rows(solve, 32)
    x_copy = pltpu.make_async_copy(x_out, x_hbm, load_sem.at[0])
    x_copy.start()

    mine = pl.ds(pl.multiple_of(load * rows, rows), rows)
    gr[load] = g0[:, mine, :]
    gr[loads + load] = g1[:, mine, :]
    taken(sum_recv.at[0], gr.at[pl.ds(0, 2 * (loads - 1))])

    taken(sum_send.at[0], gr.at[pl.ds(0, 2 * (loads - 1))])
    taken(sum_send.at[1], r1.at[pl.ds(0, group - 1)])

    @pl.when(has_above)
    def _():
        taken(halo_send.at[0], ff.at[0, pl.ds(0, 4)])

    @pl.when(has_below)
    def _():
        taken(halo_send.at[1], ff.at[0, pl.ds(0, 10)])

    taken(sum_recv.at[3], r2.at[pl.ds(0, wide), pl.ds(0, loads - 1)])
    first, second = coefficients(jnp.concatenate([summed(j) for j in range(loads)], axis=0))
    coefs[0] = jnp.broadcast_to(first, (loads, ROWS))
    coefs[1] = jnp.broadcast_to(second, (loads, ROWS))
    total = None
    for i in range(loads):
        term = coefs[0, i : i + 1, :][None] * gr[i] + coefs[1, i : i + 1, :][None] * gr[loads + i]
        total = term if total is None else total + term
    grad_out[...] = sc[:, mine, :] * total
    grad_copy = pltpu.make_async_copy(grad_out, grad_hbm, load_sem.at[1])
    grad_copy.start()

    taken(sum_send.at[3], r2.at[pl.ds(0, wide), pl.ds(0, loads - 1)])
    taken(sum_send.at[2], r2.at[pl.ds(0, wide - 1), 0])
    x_copy.wait()
    grad_copy.wait()


def finish(x, grad, x_out, grad_out, sem):
    copies = [pltpu.make_async_copy(x, x_out.at[0], sem.at[0]), pltpu.make_async_copy(grad, grad_out, sem.at[1])]
    for copy in copies:
        copy.start()
    for copy in copies:
        copy.wait()


def solution(mesh):
    spaces, loads = mesh.shape["space"], mesh.shape["load"]
    group = 2 * LONG
    rows = ROWS // loads

    def shards(forward_disp, adjoint_rhs, modulus_factor, zone_base, zone_ids, fixed_mask):
        plane = (ROWS, ROWS)
        padded = (ROWS + TILE, ROWS)
        vmem = lambda *shape: pltpu.VMEM(shape, F32)
        ints = lambda *shape: pltpu.VMEM(shape, jnp.int32)
        dma = pltpu.SemaphoreType.DMA
        hbm = pl.BlockSpec(memory_space=pltpu.HBM)
        anywhere = pl.BlockSpec(memory_space=pl.ANY)
        out = lambda *shape: jax.ShapeDtypeStruct(shape, F32)
        pinned = [
            pltpu.with_memory_space_constraint(a, pltpu.HBM)
            for a in (forward_disp, adjoint_rhs, modulus_factor, zone_base, zone_ids, fixed_mask)
        ]
        x, grad = pl.pallas_call(
            functools.partial(kernel, spaces=spaces, loads=loads, group=group),
            out_shape=(out(3, 2, *plane), out(2, rows, ROWS)),
            in_specs=[hbm] * 6,
            out_specs=(anywhere,) * 2,
            scratch_shapes=[
                vmem(3, 2, *plane), vmem(2, rows, ROWS), pltpu.SMEM(zone_base.shape, F32),
                vmem(2, *plane), ints(2, *plane), ints(2, *plane), vmem(3, 2, *plane), vmem(3, 3, *padded),
                vmem(2, *plane), vmem(4, *padded), vmem(3, 2, *padded), vmem(3, 2, *padded), vmem(3, 2, *padded), vmem(3, *padded),
                vmem(2, *plane), vmem(3, 2, *plane), vmem(3, *plane), vmem(2, 18, *plane),
                vmem(2, *plane), vmem(2, *plane), vmem(2 * loads, 2, rows, ROWS),
                vmem(1, ROWS), vmem(group, 1, ROWS), vmem(1, ROWS), vmem(spaces // group, loads, 1, ROWS),
                vmem(2, loads, ROWS),
                dma((6,)), dma((2,)), dma((3 + 3 * CHUNKS,)), dma((4,)), dma((4,)),
                *[pltpu.SemaphoreType.REGULAR] * 3,
            ],
            compiler_params=pltpu.CompilerParams(collective_id=0, has_side_effects=True, vmem_limit_bytes=LIMIT),
        )(*pinned)
        return pl.pallas_call(
            finish,
            out_shape=(out(1, 3, 2, *plane), out(2, rows, ROWS)),
            in_specs=[anywhere] * 2,
            out_specs=(hbm, hbm),
            scratch_shapes=[dma((2,))],
            compiler_params=pltpu.CompilerParams(vmem_limit_bytes=4 * 2**20),
        )(x, grad)

    placed = (
        P("load", None, "space", None, None),
        P("load", None, "space", None, None),
        P("space", None, None),
        P(),
        P("space", None, None),
        P("space", None, None),
    )
    return jax.shard_map(
        shards,
        mesh=mesh,
        in_specs=placed,
        out_specs=(P("load", None, "space", None, None), P("space", "load", None)),
        check_vma=False,
    )
```

```python
import functools

import jax
import jax.numpy as jnp
import numpy as np
from jax import lax
from jax.experimental import pallas as pl
from jax.experimental.pallas import tpu as pltpu
from jax.sharding import PartitionSpec as P

F32 = jnp.float32
MESH = pl.DeviceIdType.MESH
ROWS = 128
TILE = 8
LONG = 8
STEP = 16
CUTS = [0, 32, 64, 96, 112, ROWS]
CHUNKS = len(CUTS) - 1
DONE = [0] + [cut - STEP for cut in CUTS[1:-1]] + [ROWS]
LIMIT = 40 * 2**20

POISSON = 0.3
SHEAR = 0.5 / (1.0 + POISSON)
KAPPA = 2.0 * POISSON / (1.0 - 2.0 * POISSON)
UNIT = SHEAR / 16.0
DIAG = SHEAR * (KAPPA + 4.0) / 9.0


def shifted_down(value):
    last = lax.broadcasted_iota(jnp.int32, value.shape, 1) == ROWS - 1
    return jnp.where(last, 0.0, pltpu.roll(value, ROWS - 1, 1))


def shifted_up(value):
    first = lax.broadcasted_iota(jnp.int32, value.shape, 1) == 0
    return jnp.where(first, 0.0, pltpu.roll(value, 1, 1))


def plane_modes(pairs, row, n):
    out = []
    for sums, slopes in pairs:
        here, after = sums[pl.ds(row, n), :], sums[pl.ds(row + 1, n), :]
        slope, slope_after = slopes[pl.ds(row, n), :], slopes[pl.ds(row + 1, n), :]
        out.append((here + after, slope + slope_after, after - here, slope_after - slope))
    return out


def strains(low, high):
    (u, v, w) = [
        (
            l[1] + h[1],
            l[2] + h[2],
            h[0] - l[0],
            l[3] + h[3],
            h[1] - l[1],
            h[2] - l[2],
            h[3] - l[3],
        )
        for l, h in zip(low, high)
    ]
    return (
        u[0], v[1], w[2],
        u[1] + v[0], u[2] + w[0], v[2] + w[1],
        u[3], w[5], u[4], v[5], v[3], w[4],
        u[5], v[4], w[3],
        u[6], v[6], w[6],
    )


def stresses(e, modulus=None):
    third, last = 1.0 / 3.0, (KAPPA + 4.0) / 9.0
    if modulus is None:
        two = 2.0
        times = lambda value: value
    else:
        two, third, last = 2.0 * modulus, third * modulus, last * modulus
        times = lambda value: modulus * value
    half = (0.5 * KAPPA) * (e[0] + e[1] + e[2])
    out = [two * (e[0] + half), two * (e[1] + half), two * (e[2] + half), times(e[3]), times(e[4]), times(e[5])]
    for a, b in ((6, 7), (8, 9), (10, 11)):
        both = (KAPPA / 3.0) * (e[a] + e[b])
        out += [times(e[a] + both), times(e[b] + both)]
    shear = e[12] + e[13] + e[14]
    out += [third * (e[12] + shear), third * (e[13] + shear), third * (e[14] + shear)]
    out += [last * e[15], last * e[16], last * e[17]]
    return out


def corner_modes(f):
    return (
        (f[0], f[3], f[4], f[6], f[8], f[12], f[15]),
        (f[3], f[1], f[5], f[10], f[13], f[9], f[16]),
        (f[4], f[5], f[2], f[14], f[11], f[7], f[17]),
    )


def onto_plane(under, over):
    return (
        under[2] - over[2],
        (under[0] + under[4]) + (over[0] - over[4]),
        (under[1] + under[5]) + (over[1] - over[5]),
        (under[3] + under[6]) + (over[3] - over[6]),
    )


def dot(a, b):
    total = None
    for left, right in zip(a, b):
        term = left * right
        total = term if total is None else total + term
    return total


def folded(value):
    total = value[0:TILE]
    for i in range(1, value.shape[0] // TILE):
        total = total + value[i * TILE : (i + 1) * TILE]
    return total


def over_rows(body, size, carry=None, start=0, stop=ROWS):
    at = lambda b: pl.multiple_of(b * size, size)
    first, last = start // size, stop // size
    if carry is None:
        lax.fori_loop(first, last, lambda b, _: (body(at(b)), 0)[1], 0)
        return None
    return lax.fori_loop(first, last, lambda b, held: body(at(b), held), carry)


def kernel(
    fwd_hbm, rhs_hbm, fac_hbm, base_hbm, ids_hbm, msk_hbm,
    x_hbm, grad_hbm,
    x_out, grad_out, base, fac, ids, msk, rhs, fw, sc, m, y0, y1, y0h, y1h, y0x, y1x, fwx, passed, inv, r0, r0h, ff, g0, g1, gr,
    part, r1, mid, r2, coefs,
    load_sem, halo_send, halo_recv, sum_send, sum_recv, known1, known2, known3,
    *, spaces, loads, group,
):
    s = lax.axis_index("space")
    load = lax.axis_index("load")
    above, below = lax.rem(s + 1, spaces), lax.rem(s + spaces - 1, spaces)
    wide = spaces // group
    within, outer = lax.rem(s, group), s // group
    rows = ROWS // loads

    def local(src, dst, index):
        return pltpu.make_async_copy(src, dst, load_sem.at[index])

    loaded = [
        local(base_hbm, base, 5),
        local(fac_hbm, fac, 0),
        local(ids_hbm, ids, 1),
        local(msk_hbm, msk, 2),
        local(rhs_hbm.at[0], rhs, 3),
        local(fwd_hbm.at[0], fw.at[:, pl.ds(0, 2)], 4),
    ]
    for copy in loaded:
        copy.start()

    core, y = lax.rem(s, 2), lax.rem(s // 2, LONG)
    at_y = lambda step, c: {"space": outer * group + lax.rem(y + LONG + step, LONG) * 2 + c}
    at_x = lambda step: {"space": lax.rem(outer + wide + step, wide) * group + within}
    at_z = lambda step: {"load": lax.rem(load + loads + step, loads)}

    near = [{"space": above}, {"space": below}, at_y(0, 1 - core)]
    near += [at_y(step, c) for step in (1, -1) for c in range(2)] + [at_x(1), at_x(-1), at_z(1), at_z(-1)]
    next1 = [at_y(1, core), at_y(-1, core), at_x(1), at_x(-1), at_z(1), at_z(-1)]
    next2 = [at_y(2, core), at_y(-2, core), at_z(2), at_z(-2)]
    next3 = [at_x(1), at_x(-1), at_x(2)]

    def tell(sem, peers):
        for peer in peers:
            pl.semaphore_signal(sem, inc=1, device_id=peer, device_id_type=MESH)

    barrier = pltpu.get_barrier_semaphore()
    tell(barrier, near)

    far = lambda step, size: min(step, size - step)
    order1 = sorted(range(1, group), key=lambda i: -far(i // 2 + i % 2, LONG))
    order2 = sorted(
        ((i, j) for i in range(wide) for j in range(1, loads)), key=lambda ij: -far(ij[0], wide) - far(ij[1], loads)
    )
    stage1 = [lax.rem(within + i, group) for i in order1]
    peers1 = [{"space": outer * group + i} for i in stage1]
    stage2 = [lax.rem(outer + i, wide) * group + within for i in range(wide)]
    peers_own = [{"space": i} for i in stage2[1:]]
    peers_other = [{"space": stage2[i], "load": lax.rem(load + j, loads)} for i, j in order2]
    stage3 = [lax.rem(load + i, loads) for i in sorted(range(1, loads), key=lambda i: -far(i, loads))]
    peers3 = [{"load": i} for i in stage3]

    def remote(src, dst, send, recv, device):
        return pltpu.make_async_remote_copy(
            src_ref=src, dst_ref=dst, send_sem=send, recv_sem=recv, device_id=device, device_id_type=MESH
        )

    zero = jnp.zeros((TILE, ROWS), F32)
    past = slice(ROWS, ROWS + TILE)
    for layer in range(4):
        m[layer, 0:TILE, :] = zero
    for c in range(3):
        for k in range(2):
            passed[2 * c + k, 0:TILE, :] = zero
            for plane in range(3):
                y1x[plane, c, k, past, :] = zero
                fwx[plane, c, k, past, :] = zero
            for plane in range(4):
                y0x[plane, c, k, past, :] = zero

    for copy in loaded[:3]:
        copy.wait()
    bases = [base[i] for i in range(base.shape[0])]

    def moduli(row, n=16):
        at = pl.ds(row, n)
        for layer in range(2):
            zone = ids[layer, at, :]
            scale = jnp.full((n, ROWS), bases[0], F32)
            for i in range(1, len(bases)):
                scale = jnp.where(zone == i, bases[i], scale)
            scale = UNIT * scale
            sc[layer, at, :] = scale
            m[1 + layer, pl.ds(row + TILE, n), :] = fac[layer, at, :] * scale

    over_rows(moduli, 16)
    pl.semaphore_wait(barrier, len(near))
    body_rows = pl.ds(TILE, ROWS)
    has_above, has_below = s < spaces - 1, s > 0
    up, down = {"space": above}, {"space": below}

    def start_up(*copies):
        @pl.when(has_above)
        def _():
            for copy in copies:
                copy.start()

    def start_down(*copies):
        @pl.when(has_below)
        def _():
            for copy in copies:
                copy.start()

    m_up = remote(m.at[2, body_rows], m.at[0, body_rows], halo_send.at[0], halo_recv.at[0], up)
    m_down = remote(m.at[1, body_rows], m.at[3, body_rows], halo_send.at[1], halo_recv.at[1], down)
    start_up(m_up)
    start_down(m_down)
    tell(known1, next1)

    loaded[3].wait()
    loaded[4].wait()

    def inverse_diagonal(low, high, row, n):
        here = m[low, pl.ds(row + TILE, n), :] + m[high, pl.ds(row + TILE, n), :]
        before = m[low, pl.ds(row + TILE - 1, n), :] + m[high, pl.ds(row + TILE - 1, n), :]
        total = here + before
        return 1.0 / ((DIAG / UNIT) * (total + shifted_up(total)))

    def own_first(row, n=64):
        at = pl.ds(row, n)
        free_low = (1 - msk[0, at, :]).astype(F32)
        free_high = (1 - msk[1, at, :]).astype(F32)
        inverse = free_high * inverse_diagonal(1, 2, row, n)
        inv[1, at, :] = inverse
        for c in range(3):
            r0[c, 0, at, :] = free_low * rhs[c, 0, at, :]
            high = free_high * rhs[c, 1, at, :]
            r0[c, 1, at, :] = high
            y0[c, 1, at, :] = inverse * high

    over_rows(own_first, 64)

    r_down, y_up, y1_down = [], [], []
    for i in range(CHUNKS):
        part_rows = pl.ds(CUTS[i], CUTS[i + 1] - CUTS[i])
        r_down.append(
            remote(r0.at[:, 0, part_rows], r0h.at[:, part_rows], halo_send.at[1], halo_recv.at[3 + i], down)
        )
        y_up.append(
            remote(
                y0.at[:, 1, part_rows], y0h.at[:, part_rows],
                halo_send.at[0], halo_recv.at[3 + CHUNKS + i], up,
            )
        )
        done = pl.ds(DONE[i], DONE[i + 1] - DONE[i])
        y1_down.append(
            remote(
                y1.at[:, 0, done], y1h.at[:, done],
                halo_send.at[1], halo_recv.at[3 + 2 * CHUNKS + i], down,
            )
        )
    start_down(*r_down)
    start_up(*y_up)
    loaded[5].wait()
    f_down = remote(fw.at[:, 0], fw.at[:, 2], halo_send.at[1], halo_recv.at[2], down)
    start_down(f_down)

    def cleared(ref):
        def body(row):
            ref[pl.ds(row, 32), :] = jnp.zeros((32, ROWS), F32)

        over_rows(body, 32)

    @pl.when(s == 0)
    def _():
        cleared(m.at[0, body_rows])
        for c in range(3):
            cleared(y0h.at[c])

    @pl.when(s == spaces - 1)
    def _():
        cleared(m.at[3, body_rows])
        for c in range(3):
            cleared(r0h.at[c])
            cleared(fw.at[c, 2])
            cleared(y1h.at[c])

    def wait_from_below(*copies):
        @pl.when(has_below)
        def _():
            for copy in copies:
                copy.wait_recv()

    def wait_from_above(*copies):
        @pl.when(has_above)
        def _():
            for copy in copies:
                copy.wait_recv()

    def along_x(value, out, at):
        after = shifted_down(value)
        out[0, at, :] = value + after
        out[1, at, :] = after - value

    def plane_along_x(planes, n):
        def body(row):
            at = pl.ds(row, n)
            for source, out in planes:
                for c in range(3):
                    along_x(source(c, at), out.at[c], at)

        over_rows(body, n)

    pairs = lambda ref: [(ref.at[c, 0], ref.at[c, 1]) for c in range(3)]
    y0_planes = [pairs(y0x.at[plane]) for plane in range(4)]
    y1_planes = [pairs(y1x.at[plane]) for plane in range(3)]
    fw_planes = [pairs(fwx.at[plane]) for plane in range(3)]

    def forward_stress(layer, n):
        def body(row):
            low = plane_modes(fw_planes[layer], row, n)
            high = plane_modes(fw_planes[layer + 1], row, n)
            for i, value in enumerate(stresses(strains(low, high))):
                ff[layer, i, pl.ds(row, n), :] = value

        over_rows(body, n)

    plane_along_x([(lambda c, at: y0[c, 1, at, :], y0x.at[2])], 32)
    plane_along_x([(lambda c, at, k=k: fw[c, k, at, :], fwx.at[k]) for k in range(2)], 32)
    forward_stress(0, 32)

    wait_from_below(m_up)
    wait_from_above(m_down)
    pl.semaphore_wait(known1, len(next1))
    tell(known2, next2)

    def own_second(row, n):
        at = pl.ds(row, n)
        inverse = (1 - msk[0, at, :]).astype(F32) * inverse_diagonal(0, 1, row, n)
        inv[0, at, :] = inverse
        beyond = inverse_diagonal(2, 3, row, n)
        for c in range(3):
            field = inverse * r0[c, 0, at, :]
            y0[c, 0, at, :] = field
            along_x(y0h[c, at, :], y0x.at[0, c], at)
            along_x(field, y0x.at[1, c], at)
            along_x(beyond * r0h[c, at, :], y0x.at[3, c], at)

    def product(row, next_norm, n=STEP):
        at = pl.ds(row, n)
        planes = [plane_modes(plane, row, n) for plane in y0_planes]
        layers = []
        for layer in range(3):
            modulus = m[layer, pl.ds(row + TILE, n), :]
            layers.append(corner_modes(stresses(strains(planes[layer], planes[layer + 1]), modulus)))
        for plane in range(2):
            inverse = inv[plane, at, :]
            for c in range(3):
                g = onto_plane(layers[plane][c], layers[plane + 1][c])
                sums = (g[0] - g[1]) + shifted_up(g[0] + g[1])
                slopes = (g[2] - g[3]) + shifted_up(g[2] + g[3])
                passed[3 * plane + c, pl.ds(row + TILE, n), :] = sums + slopes
                force = (sums - slopes) + passed[3 * plane + c, pl.ds(row + TILE - 1, n), :]
                image = inverse * force
                y1[c, plane, at, :] = image
                next_norm = next_norm + folded(force * image)
        return next_norm

    next_norm = zero
    for i in range(CHUNKS):
        wait_from_above(r_down[i])
        wait_from_below(y_up[i])
        own_second(CUTS[i], CUTS[i + 1] - CUTS[i])
        next_norm = over_rows(product, STEP, next_norm, DONE[i], DONE[i + 1])
        start_down(y1_down[i])
    pl.semaphore_wait(known2, len(next2))
    tell(known3, next3)

    def against_forward(planes, out, n):
        def body(row):
            all_modes = [plane_modes(plane, row, n) for plane in planes]
            at = pl.ds(row, n)
            for layer in range(2):
                e = strains(all_modes[layer], all_modes[layer + 1])
                out[layer, at, :] = dot(e, [ff[layer, j, at, :] for j in range(18)])

        over_rows(body, n)

    def energy_of(layer, n):
        def body(row, held):
            e = strains(plane_modes(y1_planes[layer], row, n), plane_modes(y1_planes[layer + 1], row, n))
            return held + folded(m[1 + layer, pl.ds(row + TILE, n), :] * dot(e, stresses(e)))

        return body

    def against_rhs(row, held, n=32):
        norm, curve = held
        at = pl.ds(row, n)
        for c in range(3):
            for plane in range(2):
                residual = r0[c, plane, at, :]
                norm = norm + folded(residual * y0[c, plane, at, :])
                curve = curve + folded(residual * y1[c, plane, at, :])
        return norm, curve

    plane_along_x([(lambda c, at, k=k: y1[c, k, at, :], y1x.at[k]) for k in range(2)], 32)
    energy = over_rows(energy_of(0, 32), 32, zero)
    norm, curve = over_rows(against_rhs, 32, (zero, zero))
    wait_from_above(f_down)
    plane_along_x([(lambda c, at: fw[c, 2, at, :], fwx.at[2])], 32)
    forward_stress(1, 32)
    against_forward(y0_planes[1:4], g0, 16)

    def taken(sem, ref):
        pltpu.make_async_copy(ref, ref, sem).wait()

    def exchange(src, slots):
        for slot, peer in zip(stage3, peers3):
            remote(
                src.at[:, pl.ds(pl.multiple_of(slot * rows, rows), rows)], gr.at[slots + load],
                sum_send.at[0], sum_recv.at[0], peer,
            ).start()

    exchange(g0, 0)
    for i in range(CHUNKS):
        wait_from_above(y1_down[i])
        part_rows = pl.ds(DONE[i], DONE[i + 1] - DONE[i])
        for c in range(3):
            along_x(y1h[c, part_rows, :], y1x.at[2, c], part_rows)
        first, last = DONE[i] - STEP, DONE[i + 1] - STEP
        energy = over_rows(energy_of(1, STEP), STEP, energy, max(first, 0), ROWS if i == CHUNKS - 1 else last)

    lane = lax.broadcasted_iota(jnp.int32, (1, ROWS), 1)
    quarter = ROWS // 4
    sums = [jnp.sum(jnp.sum(v, axis=0, keepdims=True), axis=1, keepdims=True) for v in (norm, curve, next_norm, energy)]
    part[...] = jnp.where(
        lane < 2 * quarter,
        jnp.where(lane < quarter, sums[0], sums[1]),
        jnp.where(lane < 3 * quarter, sums[2], sums[3]),
    )
    for peer in peers1:
        remote(part, r1.at[within], sum_send.at[1], sum_recv.at[1], peer).start()
    r1[within] = part[...]
    against_forward(y1_planes, g1, 16)
    exchange(g1, loads)

    taken(sum_recv.at[1], r1.at[pl.ds(0, group - 1)])
    total = r1[0]
    for i in range(1, group):
        total = total + r1[i]
    mid[...] = total
    pl.semaphore_wait(known3, len(next3))
    for peer in peers_other:
        remote(mid, r2.at[outer, load], sum_send.at[3], sum_recv.at[3], peer).start()
    for peer in peers_own:
        remote(mid, r2.at[outer, load], sum_send.at[2], sum_recv.at[2], peer).start()
    r2[outer, load] = total

    def coefficients(sums):
        rr, rq, qq, qd = [sums[:, i * quarter : i * quarter + 1] for i in range(4)]
        step = rr / rq
        norm_next = step * (step * qq) - rr
        ratio = norm_next / rr
        curve_next = rq - 2.0 * (step * qq) + step * (step * qd)
        step_next = norm_next / (curve_next - ratio * norm_next / step)
        return step + step_next * (1.0 + ratio), -(step_next * step)

    def summed(j):
        total = r2[0, j]
        for i in range(1, wide):
            total = total + r2[i, j]
        return total

    taken(sum_recv.at[2], r2.at[pl.ds(0, wide - 1), 0])
    first, second = coefficients(summed(load))

    def solve(row, n=32):
        at = pl.ds(row, n)
        for c in range(3):
            for plane in range(2):
                x_out[c, plane, at, :] = first * y0[c, plane, at, :] + second * y1[c, plane, at, :]

    over_rows(solve, 32)
    x_copy = pltpu.make_async_copy(x_out, x_hbm, load_sem.at[0])
    x_copy.start()

    mine = pl.ds(pl.multiple_of(load * rows, rows), rows)
    gr[load] = g0[:, mine, :]
    gr[loads + load] = g1[:, mine, :]
    taken(sum_recv.at[0], gr.at[pl.ds(0, 2 * (loads - 1))])

    taken(sum_send.at[0], gr.at[pl.ds(0, 2 * (loads - 1))])
    taken(sum_send.at[1], r1.at[pl.ds(0, group - 1)])

    @pl.when(has_above)
    def _():
        taken(halo_send.at[0], ff.at[0, pl.ds(0, 4)])

    @pl.when(has_below)
    def _():
        taken(halo_send.at[1], ff.at[0, pl.ds(0, 10)])

    taken(sum_recv.at[3], r2.at[pl.ds(0, wide), pl.ds(0, loads - 1)])
    first, second = coefficients(jnp.concatenate([summed(j) for j in range(loads)], axis=0))
    coefs[0] = jnp.broadcast_to(first, (loads, ROWS))
    coefs[1] = jnp.broadcast_to(second, (loads, ROWS))
    total = None
    for i in range(loads):
        term = coefs[0, i : i + 1, :][None] * gr[i] + coefs[1, i : i + 1, :][None] * gr[loads + i]
        total = term if total is None else total + term
    grad_out[...] = sc[:, mine, :] * total
    grad_copy = pltpu.make_async_copy(grad_out, grad_hbm, load_sem.at[1])
    grad_copy.start()

    taken(sum_send.at[3], r2.at[pl.ds(0, wide), pl.ds(0, loads - 1)])
    taken(sum_send.at[2], r2.at[pl.ds(0, wide - 1), 0])
    x_copy.wait()
    grad_copy.wait()


def finish(x, grad, x_out, grad_out, sem):
    copies = [pltpu.make_async_copy(x, x_out.at[0], sem.at[0]), pltpu.make_async_copy(grad, grad_out, sem.at[1])]
    for copy in copies:
        copy.start()
    for copy in copies:
        copy.wait()


def solution(mesh):
    spaces, loads = mesh.shape["space"], mesh.shape["load"]
    group = 2 * LONG
    rows = ROWS // loads

    def shards(forward_disp, adjoint_rhs, modulus_factor, zone_base, zone_ids, fixed_mask):
        plane = (ROWS, ROWS)
        padded = (ROWS + TILE, ROWS)
        vmem = lambda *shape: pltpu.VMEM(shape, F32)
        ints = lambda *shape: pltpu.VMEM(shape, jnp.int32)
        dma = pltpu.SemaphoreType.DMA
        hbm = pl.BlockSpec(memory_space=pltpu.HBM)
        anywhere = pl.BlockSpec(memory_space=pl.ANY)
        out = lambda *shape: jax.ShapeDtypeStruct(shape, F32)
        pinned = [
            pltpu.with_memory_space_constraint(a, pltpu.HBM)
            for a in (forward_disp, adjoint_rhs, modulus_factor, zone_base, zone_ids, fixed_mask)
        ]
        x, grad = pl.pallas_call(
            functools.partial(kernel, spaces=spaces, loads=loads, group=group),
            out_shape=(out(3, 2, *plane), out(2, rows, ROWS)),
            in_specs=[hbm] * 6,
            out_specs=(anywhere,) * 2,
            scratch_shapes=[
                vmem(3, 2, *plane), vmem(2, rows, ROWS), pltpu.SMEM(zone_base.shape, F32),
                vmem(2, *plane), ints(2, *plane), ints(2, *plane), vmem(3, 2, *plane), vmem(3, 3, *plane),
                vmem(2, *plane), vmem(4, *padded), vmem(3, 2, *plane), vmem(3, 2, *plane), vmem(3, *plane), vmem(3, *plane),
                vmem(4, 3, 2, *padded), vmem(3, 3, 2, *padded), vmem(3, 3, 2, *padded), vmem(6, *padded),
                vmem(2, *plane), vmem(3, 2, *plane), vmem(3, *plane), vmem(2, 18, *plane),
                vmem(2, *plane), vmem(2, *plane), vmem(2 * loads, 2, rows, ROWS),
                vmem(1, ROWS), vmem(group, 1, ROWS), vmem(1, ROWS), vmem(spaces // group, loads, 1, ROWS),
                vmem(2, loads, ROWS),
                dma((6,)), dma((2,)), dma((3 + 3 * CHUNKS,)), dma((4,)), dma((4,)),
                *[pltpu.SemaphoreType.REGULAR] * 3,
            ],
            compiler_params=pltpu.CompilerParams(collective_id=0, has_side_effects=True, vmem_limit_bytes=LIMIT),
        )(*pinned)
        return pl.pallas_call(
            finish,
            out_shape=(out(1, 3, 2, *plane), out(2, rows, ROWS)),
            in_specs=[anywhere] * 2,
            out_specs=(hbm, hbm),
            scratch_shapes=[dma((2,))],
            compiler_params=pltpu.CompilerParams(vmem_limit_bytes=4 * 2**20),
        )(x, grad)

    placed = (
        P("load", None, "space", None, None),
        P("load", None, "space", None, None),
        P("space", None, None),
        P(),
        P("space", None, None),
        P("space", None, None),
    )
    return jax.shard_map(
        shards,
        mesh=mesh,
        in_specs=placed,
        out_specs=(P("load", None, "space", None, None), P("space", "load", None)),
        check_vma=False,
    )
```

```python
import functools

import jax
import jax.numpy as jnp
import numpy as np
from jax import lax
from jax.experimental import pallas as pl
from jax.experimental.pallas import tpu as pltpu
from jax.sharding import PartitionSpec as P

F32 = jnp.float32
MESH = pl.DeviceIdType.MESH
ROWS = 128
TILE = 8
LONG = 8
STEP = 16
CUTS = [0, 32, 64, 96, 112, ROWS]
CHUNKS = len(CUTS) - 1
EARLY = 72
DONE = [0] + [cut - STEP for cut in CUTS[1:-1]] + [ROWS]
LIMIT = 40 * 2**20

POISSON = 0.3
SHEAR = 0.5 / (1.0 + POISSON)
KAPPA = 2.0 * POISSON / (1.0 - 2.0 * POISSON)
UNIT = SHEAR / 16.0
DIAG = SHEAR * (KAPPA + 4.0) / 9.0


def shifted_down(value):
    last = lax.broadcasted_iota(jnp.int32, value.shape, 1) == ROWS - 1
    return jnp.where(last, 0.0, pltpu.roll(value, ROWS - 1, 1))


def shifted_up(value):
    first = lax.broadcasted_iota(jnp.int32, value.shape, 1) == 0
    return jnp.where(first, 0.0, pltpu.roll(value, 1, 1))


def plane_modes(pairs, row, n):
    out = []
    for sums, slopes in pairs:
        here, after = sums[pl.ds(row, n), :], sums[pl.ds(row + 1, n), :]
        slope, slope_after = slopes[pl.ds(row, n), :], slopes[pl.ds(row + 1, n), :]
        out.append((here + after, slope + slope_after, after - here, slope_after - slope))
    return out


def strains(low, high):
    (u, v, w) = [
        (
            l[1] + h[1],
            l[2] + h[2],
            h[0] - l[0],
            l[3] + h[3],
            h[1] - l[1],
            h[2] - l[2],
            h[3] - l[3],
        )
        for l, h in zip(low, high)
    ]
    return (
        u[0], v[1], w[2],
        u[1] + v[0], u[2] + w[0], v[2] + w[1],
        u[3], w[5], u[4], v[5], v[3], w[4],
        u[5], v[4], w[3],
        u[6], v[6], w[6],
    )


def stresses(e, modulus=None):
    third, last = 1.0 / 3.0, (KAPPA + 4.0) / 9.0
    if modulus is None:
        two = 2.0
        times = lambda value: value
    else:
        two, third, last = 2.0 * modulus, third * modulus, last * modulus
        times = lambda value: modulus * value
    half = (0.5 * KAPPA) * (e[0] + e[1] + e[2])
    out = [two * (e[0] + half), two * (e[1] + half), two * (e[2] + half), times(e[3]), times(e[4]), times(e[5])]
    for a, b in ((6, 7), (8, 9), (10, 11)):
        both = (KAPPA / 3.0) * (e[a] + e[b])
        out += [times(e[a] + both), times(e[b] + both)]
    shear = e[12] + e[13] + e[14]
    out += [third * (e[12] + shear), third * (e[13] + shear), third * (e[14] + shear)]
    out += [last * e[15], last * e[16], last * e[17]]
    return out


def corner_modes(f):
    return (
        (f[0], f[3], f[4], f[6], f[8], f[12], f[15]),
        (f[3], f[1], f[5], f[10], f[13], f[9], f[16]),
        (f[4], f[5], f[2], f[14], f[11], f[7], f[17]),
    )


def onto_plane(under, over):
    return (
        under[2] - over[2],
        (under[0] + under[4]) + (over[0] - over[4]),
        (under[1] + under[5]) + (over[1] - over[5]),
        (under[3] + under[6]) + (over[3] - over[6]),
    )


def dot(a, b):
    total = None
    for left, right in zip(a, b):
        term = left * right
        total = term if total is None else total + term
    return total


def folded(value):
    total = value[0:TILE]
    for i in range(1, value.shape[0] // TILE):
        total = total + value[i * TILE : (i + 1) * TILE]
    return total


def over_rows(body, size, carry=None, start=0, stop=ROWS):
    at = lambda b: pl.multiple_of(b * size, size)
    first, last = start // size, stop // size
    if carry is None:
        lax.fori_loop(first, last, lambda b, _: (body(at(b)), 0)[1], 0)
        return None
    return lax.fori_loop(first, last, lambda b, held: body(at(b), held), carry)


def kernel(
    fwd_hbm, rhs_hbm, fac_hbm, base_hbm, ids_hbm, msk_hbm,
    x_hbm, grad_hbm,
    x_out, grad_out, base, fac, ids, msk, rhs, fw, sc, m, y0, y1, y0h, y1h, y0x, y1x, fwx, passed, inv, beyond, r0, r0h, ff, g0, g1, gr,
    part, r1, mid, r2, coefs,
    load_sem, halo_send, halo_recv, sum_send, sum_recv, known1, known2, known3,
    *, spaces, loads, group,
):
    s = lax.axis_index("space")
    load = lax.axis_index("load")
    above, below = lax.rem(s + 1, spaces), lax.rem(s + spaces - 1, spaces)
    wide = spaces // group
    within, outer = lax.rem(s, group), s // group
    rows = ROWS // loads

    def local(src, dst, index):
        return pltpu.make_async_copy(src, dst, load_sem.at[index])

    loaded = [
        local(base_hbm, base, 5),
        local(fac_hbm, fac, 0),
        local(ids_hbm, ids, 1),
        local(msk_hbm, msk, 2),
        local(rhs_hbm.at[0], rhs, 3),
        local(fwd_hbm.at[0], fw.at[:, pl.ds(0, 2)], 4),
    ]
    for copy in loaded:
        copy.start()

    core, y = lax.rem(s, 2), lax.rem(s // 2, LONG)
    at_y = lambda step, c: {"space": outer * group + lax.rem(y + LONG + step, LONG) * 2 + c}
    at_x = lambda step: {"space": lax.rem(outer + wide + step, wide) * group + within}
    at_z = lambda step: {"load": lax.rem(load + loads + step, loads)}

    near = [{"space": above}, {"space": below}, at_y(0, 1 - core)]
    near += [at_y(step, c) for step in (1, -1) for c in range(2)] + [at_x(1), at_x(-1), at_z(1), at_z(-1)]
    next1 = [at_y(1, core), at_y(-1, core), at_x(1), at_x(-1), at_z(1), at_z(-1)]
    next2 = [at_y(2, core), at_y(-2, core), at_z(2), at_z(-2)]
    next3 = [at_x(1), at_x(-1), at_x(2)]

    def tell(sem, peers):
        for peer in peers:
            pl.semaphore_signal(sem, inc=1, device_id=peer, device_id_type=MESH)

    barrier = pltpu.get_barrier_semaphore()
    tell(barrier, near)

    far = lambda step, size: min(step, size - step)
    order1 = sorted(range(1, group), key=lambda i: -far(i // 2 + i % 2, LONG))
    order2 = sorted(
        ((i, j) for i in range(wide) for j in range(1, loads)), key=lambda ij: -far(ij[0], wide) - far(ij[1], loads)
    )
    stage1 = [lax.rem(within + i, group) for i in order1]
    peers1 = [{"space": outer * group + i} for i in stage1]
    stage2 = [lax.rem(outer + i, wide) * group + within for i in range(wide)]
    peers_own = [{"space": stage2[i]} for i in sorted(range(1, wide), key=lambda i: -far(i, wide))]
    peers_other = [{"space": stage2[i], "load": lax.rem(load + j, loads)} for i, j in order2]
    stage3 = [lax.rem(load + i, loads) for i in sorted(range(1, loads), key=lambda i: -far(i, loads))]
    peers3 = [{"load": i} for i in stage3]

    def remote(src, dst, send, recv, device):
        return pltpu.make_async_remote_copy(
            src_ref=src, dst_ref=dst, send_sem=send, recv_sem=recv, device_id=device, device_id_type=MESH
        )

    zero = jnp.zeros((TILE, ROWS), F32)
    past = slice(ROWS, ROWS + TILE)
    for layer in range(4):
        m[layer, 0:TILE, :] = zero
    for c in range(3):
        for k in range(2):
            passed[2 * c + k, 0:TILE, :] = zero
            for plane in range(3):
                y1x[plane, c, k, past, :] = zero
                fwx[plane, c, k, past, :] = zero
            for plane in range(4):
                y0x[plane, c, k, past, :] = zero

    for copy in loaded[:3]:
        copy.wait()
    bases = [base[i] for i in range(base.shape[0])]

    def moduli(row, n=16):
        at = pl.ds(row, n)
        for layer in range(2):
            zone = ids[layer, at, :]
            scale = jnp.full((n, ROWS), bases[0], F32)
            for i in range(1, len(bases)):
                scale = jnp.where(zone == i, bases[i], scale)
            scale = UNIT * scale
            sc[layer, at, :] = scale
            m[1 + layer, pl.ds(row + TILE, n), :] = fac[layer, at, :] * scale

    over_rows(moduli, 16)
    pl.semaphore_wait(barrier, len(near))
    body_rows = pl.ds(TILE, ROWS)
    has_above, has_below = s < spaces - 1, s > 0
    up, down = {"space": above}, {"space": below}

    def start_up(*copies):
        @pl.when(has_above)
        def _():
            for copy in copies:
                copy.start()

    def start_down(*copies):
        @pl.when(has_below)
        def _():
            for copy in copies:
                copy.start()

    m_up = remote(m.at[2, body_rows], m.at[0, body_rows], halo_send.at[0], halo_recv.at[0], up)
    m_down = remote(m.at[1, body_rows], m.at[3, body_rows], halo_send.at[1], halo_recv.at[1], down)
    start_up(m_up)
    start_down(m_down)
    tell(known1, next1)

    loaded[3].wait()
    loaded[4].wait()

    def inverse_diagonal(low, high, row, n):
        here = m[low, pl.ds(row + TILE, n), :] + m[high, pl.ds(row + TILE, n), :]
        before = m[low, pl.ds(row + TILE - 1, n), :] + m[high, pl.ds(row + TILE - 1, n), :]
        total = here + before
        return 1.0 / ((DIAG / UNIT) * (total + shifted_up(total)))

    def own_first(row, n=64):
        at = pl.ds(row, n)
        free_low = (1 - msk[0, at, :]).astype(F32)
        free_high = (1 - msk[1, at, :]).astype(F32)
        inverse = free_high * inverse_diagonal(1, 2, row, n)
        inv[1, at, :] = inverse
        for c in range(3):
            r0[c, 0, at, :] = free_low * rhs[c, 0, at, :]
            high = free_high * rhs[c, 1, at, :]
            r0[c, 1, at, :] = high
            y0[c, 1, at, :] = inverse * high

    over_rows(own_first, 64)

    r_down, y_up, y1_down = [], [], []
    for i in range(CHUNKS):
        part_rows = pl.ds(CUTS[i], CUTS[i + 1] - CUTS[i])
        r_down.append(
            remote(r0.at[:, 0, part_rows], r0h.at[:, part_rows], halo_send.at[1], halo_recv.at[3 + i], down)
        )
        y_up.append(
            remote(
                y0.at[:, 1, part_rows], y0h.at[:, part_rows],
                halo_send.at[0], halo_recv.at[3 + CHUNKS + i], up,
            )
        )
        done = pl.ds(DONE[i], DONE[i + 1] - DONE[i])
        y1_down.append(
            remote(
                y1.at[:, 0, done], y1h.at[:, done],
                halo_send.at[1], halo_recv.at[3 + 2 * CHUNKS + i], down,
            )
        )
    start_down(*r_down)
    start_up(*y_up)
    loaded[5].wait()
    f_down = [
        remote(fw.at[:, 0, part_rows], fw.at[:, 2, part_rows], halo_send.at[1], halo_recv.at[sem], down)
        for part_rows, sem in ((pl.ds(0, EARLY), 2), (pl.ds(EARLY, ROWS - EARLY), 3 + 3 * CHUNKS))
    ]
    start_down(f_down[0])

    def cleared(ref):
        def body(row):
            ref[pl.ds(row, 32), :] = jnp.zeros((32, ROWS), F32)

        over_rows(body, 32)

    @pl.when(s == 0)
    def _():
        cleared(m.at[0, body_rows])
        for c in range(3):
            cleared(y0h.at[c])

    @pl.when(s == spaces - 1)
    def _():
        cleared(m.at[3, body_rows])
        for c in range(3):
            cleared(r0h.at[c])
            cleared(fw.at[c, 2])
            cleared(y1h.at[c])

    def wait_from_below(*copies):
        @pl.when(has_below)
        def _():
            for copy in copies:
                copy.wait_recv()

    def wait_from_above(*copies):
        @pl.when(has_above)
        def _():
            for copy in copies:
                copy.wait_recv()

    def along_x(value, out, at):
        after = shifted_down(value)
        out[0, at, :] = value + after
        out[1, at, :] = after - value

    def plane_along_x(planes, n):
        def body(row):
            at = pl.ds(row, n)
            for source, out in planes:
                for c in range(3):
                    along_x(source(c, at), out.at[c], at)

        over_rows(body, n)

    pairs = lambda ref: [(ref.at[c, 0], ref.at[c, 1]) for c in range(3)]
    y0_planes = [pairs(y0x.at[plane]) for plane in range(4)]
    y1_planes = [pairs(y1x.at[plane]) for plane in range(3)]
    fw_planes = [pairs(fwx.at[plane]) for plane in range(3)]

    def forward_stress(layer, n, start=0, stop=ROWS):
        def body(row):
            low = plane_modes(fw_planes[layer], row, n)
            high = plane_modes(fw_planes[layer + 1], row, n)
            for i, value in enumerate(stresses(strains(low, high))):
                ff[layer, i, pl.ds(row, n), :] = value

        over_rows(body, n, None, start, stop)

    plane_along_x([(lambda c, at: y0[c, 1, at, :], y0x.at[2])], 32)
    plane_along_x([(lambda c, at, k=k: fw[c, k, at, :], fwx.at[k]) for k in range(2)], 32)
    forward_stress(0, 32)

    wait_from_below(m_up)
    wait_from_above(m_down)
    pl.semaphore_wait(known1, len(next1))
    tell(known2, next2)

    def own_second(row, n=ROWS):
        at = pl.ds(row, n)
        inverse = (1 - msk[0, at, :]).astype(F32) * inverse_diagonal(0, 1, row, n)
        inv[0, at, :] = inverse
        beyond[at, :] = inverse_diagonal(2, 3, row, n)
        for c in range(3):
            field = inverse * r0[c, 0, at, :]
            y0[c, 0, at, :] = field
            along_x(field, y0x.at[1, c], at)

    over_rows(own_second, ROWS)

    def halo(row, n):
        at = pl.ds(row, n)
        inverse = beyond[at, :]
        for c in range(3):
            along_x(y0h[c, at, :], y0x.at[0, c], at)
            along_x(inverse * r0h[c, at, :], y0x.at[3, c], at)

    def product(row, next_norm, n=STEP):
        at = pl.ds(row, n)
        planes = [plane_modes(plane, row, n) for plane in y0_planes]
        layers = []
        for layer in range(3):
            modulus = m[layer, pl.ds(row + TILE, n), :]
            layers.append(corner_modes(stresses(strains(planes[layer], planes[layer + 1]), modulus)))
        for plane in range(2):
            inverse = inv[plane, at, :]
            for c in range(3):
                g = onto_plane(layers[plane][c], layers[plane + 1][c])
                sums = (g[0] - g[1]) + shifted_up(g[0] + g[1])
                slopes = (g[2] - g[3]) + shifted_up(g[2] + g[3])
                passed[3 * plane + c, pl.ds(row + TILE, n), :] = sums + slopes
                force = (sums - slopes) + passed[3 * plane + c, pl.ds(row + TILE - 1, n), :]
                image = inverse * force
                y1[c, plane, at, :] = image
                next_norm = next_norm + folded(force * image)
        return next_norm

    next_norm = zero
    for i in range(CHUNKS):
        wait_from_above(r_down[i])
        wait_from_below(y_up[i])
        halo(CUTS[i], CUTS[i + 1] - CUTS[i])
        next_norm = over_rows(product, STEP, next_norm, DONE[i], DONE[i + 1])
        start_down(y1_down[i])
    start_down(f_down[1])
    pl.semaphore_wait(known2, len(next2))
    tell(known3, next3)

    def against_forward(planes, out, n, start=0, stop=ROWS):
        def body(row):
            all_modes = [plane_modes(plane, row, n) for plane in planes]
            at = pl.ds(row, n)
            for layer in range(2):
                e = strains(all_modes[layer], all_modes[layer + 1])
                out[layer, at, :] = dot(e, [ff[layer, j, at, :] for j in range(18)])

        over_rows(body, n, None, start, stop)

    def energy_of(layer, n):
        def body(row, held):
            e = strains(plane_modes(y1_planes[layer], row, n), plane_modes(y1_planes[layer + 1], row, n))
            return held + folded(m[1 + layer, pl.ds(row + TILE, n), :] * dot(e, stresses(e)))

        return body

    def against_rhs(row, held, n=32):
        norm, curve = held
        at = pl.ds(row, n)
        for c in range(3):
            for plane in range(2):
                residual = r0[c, plane, at, :]
                norm = norm + folded(residual * y0[c, plane, at, :])
                curve = curve + folded(residual * y1[c, plane, at, :])
        return norm, curve

    plane_along_x([(lambda c, at, k=k: y1[c, k, at, :], y1x.at[k]) for k in range(2)], 32)
    energy = over_rows(energy_of(0, 32), 32, zero)
    norm, curve = over_rows(against_rhs, 32, (zero, zero))
    def forward_halo(start, stop):
        at = pl.ds(start, stop - start)
        for c in range(3):
            along_x(fw[c, 2, at, :], fwx.at[2, c], at)

    half = ROWS // 2
    wait_from_above(f_down[0])
    forward_halo(0, EARLY)
    forward_stress(1, 32, 0, half)
    against_forward(y0_planes[1:4], g0, 16, 0, half)

    def taken(sem, ref):
        pltpu.make_async_copy(ref, ref, sem).wait()

    def exchange(src, slots, chosen=None):
        for slot, peer in zip(stage3, peers3):
            copy = remote(
                src.at[:, pl.ds(pl.multiple_of(slot * rows, rows), rows)], gr.at[slots + load],
                sum_send.at[0], sum_recv.at[0], peer,
            )
            if chosen is None:
                copy.start()
            else:
                pl.when(chosen(slot))(copy.start)

    exchange(g0, 0, lambda slot: slot < loads // 2)
    summed_up = lambda value: jnp.sum(jnp.sum(value, axis=0, keepdims=True), axis=1, keepdims=True)
    sums = [summed_up(value) for value in (norm, curve, next_norm)]
    for i in range(CHUNKS):
        wait_from_above(y1_down[i])
        part_rows = pl.ds(DONE[i], DONE[i + 1] - DONE[i])
        for c in range(3):
            along_x(y1h[c, part_rows, :], y1x.at[2, c], part_rows)
        first, last = DONE[i] - STEP, DONE[i + 1] - STEP
        energy = over_rows(energy_of(1, STEP), STEP, energy, max(first, 0), ROWS if i == CHUNKS - 1 else last)

    lane = lax.broadcasted_iota(jnp.int32, (1, ROWS), 1)
    quarter = ROWS // 4
    last = summed_up(energy)
    part[...] = jnp.where(
        lane < 2 * quarter,
        jnp.where(lane < quarter, sums[0], sums[1]),
        jnp.where(lane < 3 * quarter, sums[2], last),
    )
    for peer in peers1:
        remote(part, r1.at[within], sum_send.at[1], sum_recv.at[1], peer).start()
    r1[within] = part[...]
    wait_from_above(f_down[1])
    forward_halo(EARLY, ROWS)
    forward_stress(1, 32, half, ROWS)
    against_forward(y0_planes[1:4], g0, 16, half, ROWS)
    exchange(g0, 0, lambda slot: slot >= loads // 2)
    against_forward(y1_planes, g1, 16)
    exchange(g1, loads)

    taken(sum_recv.at[1], r1.at[pl.ds(0, group - 1)])
    total = r1[0]
    for i in range(1, group):
        total = total + r1[i]
    mid[...] = total
    pl.semaphore_wait(known3, len(next3))
    for peer in peers_own:
        remote(mid, r2.at[outer, load], sum_send.at[2], sum_recv.at[2], peer).start()
    for peer in peers_other:
        remote(mid, r2.at[outer, load], sum_send.at[3], sum_recv.at[3], peer).start()
    r2[outer, load] = total

    def coefficients(sums):
        rr, rq, qq, qd = [sums[:, i * quarter : i * quarter + 1] for i in range(4)]
        step = rr / rq
        norm_next = step * (step * qq) - rr
        ratio = norm_next / rr
        curve_next = rq - 2.0 * (step * qq) + step * (step * qd)
        step_next = norm_next / (curve_next - ratio * norm_next / step)
        return step + step_next * (1.0 + ratio), -(step_next * step)

    def summed(j):
        total = r2[0, j]
        for i in range(1, wide):
            total = total + r2[i, j]
        return total

    taken(sum_recv.at[2], r2.at[pl.ds(0, wide - 1), 0])
    first, second = coefficients(summed(load))

    def solve(row, n=ROWS):
        at = pl.ds(row, n)
        for c in range(3):
            for plane in range(2):
                x_out[c, plane, at, :] = first * y0[c, plane, at, :] + second * y1[c, plane, at, :]

    over_rows(solve, ROWS)
    x_copy = pltpu.make_async_copy(x_out, x_hbm, load_sem.at[0])
    x_copy.start()

    mine = pl.ds(pl.multiple_of(load * rows, rows), rows)
    gr[load] = g0[:, mine, :]
    gr[loads + load] = g1[:, mine, :]
    taken(sum_recv.at[0], gr.at[pl.ds(0, 2 * (loads - 1))])

    taken(sum_send.at[0], gr.at[pl.ds(0, 2 * (loads - 1))])
    taken(sum_send.at[1], r1.at[pl.ds(0, group - 1)])

    @pl.when(has_above)
    def _():
        taken(halo_send.at[0], ff.at[0, pl.ds(0, 4)])

    @pl.when(has_below)
    def _():
        taken(halo_send.at[1], ff.at[0, pl.ds(0, 10)])

    taken(sum_recv.at[3], r2.at[pl.ds(0, wide), pl.ds(0, loads - 1)])
    first, second = coefficients(jnp.concatenate([summed(j) for j in range(loads)], axis=0))
    coefs[0] = jnp.broadcast_to(first, (loads, ROWS))
    coefs[1] = jnp.broadcast_to(second, (loads, ROWS))
    total = None
    for i in range(loads):
        term = coefs[0, i : i + 1, :][None] * gr[i] + coefs[1, i : i + 1, :][None] * gr[loads + i]
        total = term if total is None else total + term
    grad_out[...] = sc[:, mine, :] * total
    grad_copy = pltpu.make_async_copy(grad_out, grad_hbm, load_sem.at[1])
    grad_copy.start()

    taken(sum_send.at[3], r2.at[pl.ds(0, wide), pl.ds(0, loads - 1)])
    taken(sum_send.at[2], r2.at[pl.ds(0, wide - 1), 0])
    x_copy.wait()
    grad_copy.wait()


def finish(x, grad, x_out, grad_out, sem):
    copies = [pltpu.make_async_copy(x, x_out.at[0], sem.at[0]), pltpu.make_async_copy(grad, grad_out, sem.at[1])]
    for copy in copies:
        copy.start()
    for copy in copies:
        copy.wait()


def solution(mesh):
    spaces, loads = mesh.shape["space"], mesh.shape["load"]
    group = 2 * LONG
    rows = ROWS // loads

    def shards(forward_disp, adjoint_rhs, modulus_factor, zone_base, zone_ids, fixed_mask):
        plane = (ROWS, ROWS)
        padded = (ROWS + TILE, ROWS)
        vmem = lambda *shape: pltpu.VMEM(shape, F32)
        ints = lambda *shape: pltpu.VMEM(shape, jnp.int32)
        dma = pltpu.SemaphoreType.DMA
        hbm = pl.BlockSpec(memory_space=pltpu.HBM)
        anywhere = pl.BlockSpec(memory_space=pl.ANY)
        out = lambda *shape: jax.ShapeDtypeStruct(shape, F32)
        pinned = [
            pltpu.with_memory_space_constraint(a, pltpu.HBM)
            for a in (forward_disp, adjoint_rhs, modulus_factor, zone_base, zone_ids, fixed_mask)
        ]
        x, grad = pl.pallas_call(
            functools.partial(kernel, spaces=spaces, loads=loads, group=group),
            out_shape=(out(3, 2, *plane), out(2, rows, ROWS)),
            in_specs=[hbm] * 6,
            out_specs=(anywhere,) * 2,
            scratch_shapes=[
                vmem(3, 2, *plane), vmem(2, rows, ROWS), pltpu.SMEM(zone_base.shape, F32),
                vmem(2, *plane), ints(2, *plane), ints(2, *plane), vmem(3, 2, *plane), vmem(3, 3, *plane),
                vmem(2, *plane), vmem(4, *padded), vmem(3, 2, *plane), vmem(3, 2, *plane), vmem(3, *plane), vmem(3, *plane),
                vmem(4, 3, 2, *padded), vmem(3, 3, 2, *padded), vmem(3, 3, 2, *padded), vmem(6, *padded),
                vmem(2, *plane), vmem(*plane), vmem(3, 2, *plane), vmem(3, *plane), vmem(2, 18, *plane),
                vmem(2, *plane), vmem(2, *plane), vmem(2 * loads, 2, rows, ROWS),
                vmem(1, ROWS), vmem(group, 1, ROWS), vmem(1, ROWS), vmem(spaces // group, loads, 1, ROWS),
                vmem(2, loads, ROWS),
                dma((6,)), dma((2,)), dma((4 + 3 * CHUNKS,)), dma((4,)), dma((4,)),
                *[pltpu.SemaphoreType.REGULAR] * 3,
            ],
            compiler_params=pltpu.CompilerParams(collective_id=0, has_side_effects=True, vmem_limit_bytes=LIMIT),
        )(*pinned)
        return pl.pallas_call(
            finish,
            out_shape=(out(1, 3, 2, *plane), out(2, rows, ROWS)),
            in_specs=[anywhere] * 2,
            out_specs=(hbm, hbm),
            scratch_shapes=[dma((2,))],
            compiler_params=pltpu.CompilerParams(vmem_limit_bytes=4 * 2**20),
        )(x, grad)

    placed = (
        P("load", None, "space", None, None),
        P("load", None, "space", None, None),
        P("space", None, None),
        P(),
        P("space", None, None),
        P("space", None, None),
    )
    return jax.shard_map(
        shards,
        mesh=mesh,
        in_specs=placed,
        out_specs=(P("load", None, "space", None, None), P("space", "load", None)),
        check_vma=False,
    )
```

```python
import functools

import jax
import jax.numpy as jnp
import numpy as np
from jax import lax
from jax.experimental import pallas as pl
from jax.experimental.pallas import tpu as pltpu
from jax.sharding import PartitionSpec as P

F32 = jnp.float32
MESH = pl.DeviceIdType.MESH
ROWS = 128
TILE = 8
LONG = 8
STEP = 16
CUTS = [0, 32, 64, 96, 112, ROWS]
CHUNKS = len(CUTS) - 1
EARLY = 72
DONE = [0] + [cut - STEP for cut in CUTS[1:]] + [ROWS]
PIECES = len(DONE) - 1
LIMIT = 40 * 2**20

POISSON = 0.3
SHEAR = 0.5 / (1.0 + POISSON)
KAPPA = 2.0 * POISSON / (1.0 - 2.0 * POISSON)
UNIT = SHEAR / 16.0
DIAG = SHEAR * (KAPPA + 4.0) / 9.0


def shifted_down(value):
    last = lax.broadcasted_iota(jnp.int32, value.shape, 1) == ROWS - 1
    return jnp.where(last, 0.0, pltpu.roll(value, ROWS - 1, 1))


def shifted_up(value):
    first = lax.broadcasted_iota(jnp.int32, value.shape, 1) == 0
    return jnp.where(first, 0.0, pltpu.roll(value, 1, 1))


def plane_modes(pairs, row, n):
    out = []
    for sums, slopes in pairs:
        here, after = sums[pl.ds(row, n), :], sums[pl.ds(row + 1, n), :]
        slope, slope_after = slopes[pl.ds(row, n), :], slopes[pl.ds(row + 1, n), :]
        out.append((here + after, slope + slope_after, after - here, slope_after - slope))
    return out


def strains(low, high):
    (u, v, w) = [
        (
            l[1] + h[1],
            l[2] + h[2],
            h[0] - l[0],
            l[3] + h[3],
            h[1] - l[1],
            h[2] - l[2],
            h[3] - l[3],
        )
        for l, h in zip(low, high)
    ]
    return (
        u[0], v[1], w[2],
        u[1] + v[0], u[2] + w[0], v[2] + w[1],
        u[3], w[5], u[4], v[5], v[3], w[4],
        u[5], v[4], w[3],
        u[6], v[6], w[6],
    )


def stresses(e, modulus=None):
    third, last = 1.0 / 3.0, (KAPPA + 4.0) / 9.0
    if modulus is None:
        two = 2.0
        times = lambda value: value
    else:
        two, third, last = 2.0 * modulus, third * modulus, last * modulus
        times = lambda value: modulus * value
    half = (0.5 * KAPPA) * (e[0] + e[1] + e[2])
    out = [two * (e[0] + half), two * (e[1] + half), two * (e[2] + half), times(e[3]), times(e[4]), times(e[5])]
    for a, b in ((6, 7), (8, 9), (10, 11)):
        both = (KAPPA / 3.0) * (e[a] + e[b])
        out += [times(e[a] + both), times(e[b] + both)]
    shear = e[12] + e[13] + e[14]
    out += [third * (e[12] + shear), third * (e[13] + shear), third * (e[14] + shear)]
    out += [last * e[15], last * e[16], last * e[17]]
    return out


def corner_modes(f):
    return (
        (f[0], f[3], f[4], f[6], f[8], f[12], f[15]),
        (f[3], f[1], f[5], f[10], f[13], f[9], f[16]),
        (f[4], f[5], f[2], f[14], f[11], f[7], f[17]),
    )


def onto_plane(under, over):
    return (
        under[2] - over[2],
        (under[0] + under[4]) + (over[0] - over[4]),
        (under[1] + under[5]) + (over[1] - over[5]),
        (under[3] + under[6]) + (over[3] - over[6]),
    )


def dot(a, b):
    total = None
    for left, right in zip(a, b):
        term = left * right
        total = term if total is None else total + term
    return total


def folded(value):
    total = value[0:TILE]
    for i in range(1, value.shape[0] // TILE):
        total = total + value[i * TILE : (i + 1) * TILE]
    return total


def over_rows(body, size, carry=None, start=0, stop=ROWS):
    at = lambda b: pl.multiple_of(b * size, size)
    first, last = start // size, stop // size
    if carry is None:
        lax.fori_loop(first, last, lambda b, _: (body(at(b)), 0)[1], 0)
        return None
    return lax.fori_loop(first, last, lambda b, held: body(at(b), held), carry)


def kernel(
    fwd_hbm, rhs_hbm, fac_hbm, base_hbm, ids_hbm, msk_hbm,
    x_hbm, grad_hbm,
    x_out, grad_out, base, fac, ids, msk, rhs, fw, sc, m, y0, y1, y0h, y1h, y0x, y1x, fwx, passed, inv, beyond, r0, r0h, ff, g0, g1, gr,
    part, r1, mid, r2, coefs,
    load_sem, halo_send, halo_recv, sum_send, sum_recv, known1, known2, known3,
    *, spaces, loads, group,
):
    s = lax.axis_index("space")
    load = lax.axis_index("load")
    above, below = lax.rem(s + 1, spaces), lax.rem(s + spaces - 1, spaces)
    wide = spaces // group
    within, outer = lax.rem(s, group), s // group
    rows = ROWS // loads

    def local(src, dst, index):
        return pltpu.make_async_copy(src, dst, load_sem.at[index])

    zones = [local(base_hbm, base, 5)]
    zones += [local(fac_hbm.at[k], fac.at[k], k) for k in range(2)] + [local(ids_hbm.at[k], ids.at[k], 2 + k) for k in range(2)]
    loaded = [local(msk_hbm, msk, 6), local(rhs_hbm.at[0], rhs, 7), local(fwd_hbm.at[0], fw.at[:, pl.ds(0, 2)], 4)]
    for copy in zones + loaded:
        copy.start()

    core, y = lax.rem(s, 2), lax.rem(s // 2, LONG)
    at_y = lambda step, c: {"space": outer * group + lax.rem(y + LONG + step, LONG) * 2 + c}
    at_x = lambda step: {"space": lax.rem(outer + wide + step, wide) * group + within}
    at_z = lambda step: {"load": lax.rem(load + loads + step, loads)}

    near = [{"space": above}, {"space": below}, at_y(0, 1 - core)]
    near += [at_y(step, c) for step in (1, -1) for c in range(2)] + [at_x(1), at_x(-1), at_z(1), at_z(-1)]
    next1 = [at_y(1, core), at_y(-1, core), at_x(1), at_x(-1), at_z(1), at_z(-1)]
    next2 = [at_y(2, core), at_y(-2, core), at_z(2), at_z(-2)]
    next3 = [at_x(1), at_x(-1), at_x(2)]

    def tell(sem, peers):
        for peer in peers:
            pl.semaphore_signal(sem, inc=1, device_id=peer, device_id_type=MESH)

    barrier = pltpu.get_barrier_semaphore()
    tell(barrier, near)

    far = lambda step, size: min(step, size - step)
    order1 = sorted(range(1, group), key=lambda i: -far(i // 2 + i % 2, LONG))
    order2 = sorted(
        ((i, j) for i in range(wide) for j in range(1, loads)), key=lambda ij: -far(ij[0], wide) - far(ij[1], loads)
    )
    stage1 = [lax.rem(within + i, group) for i in order1]
    peers1 = [{"space": outer * group + i} for i in stage1]
    stage2 = [lax.rem(outer + i, wide) * group + within for i in range(wide)]
    peers_own = [{"space": stage2[i]} for i in sorted(range(1, wide), key=lambda i: -far(i, wide))]
    peers_other = [{"space": stage2[i], "load": lax.rem(load + j, loads)} for i, j in order2]
    stage3 = [lax.rem(load + i, loads) for i in sorted(range(1, loads), key=lambda i: -far(i, loads))]
    peers3 = [{"load": i} for i in stage3]

    def remote(src, dst, send, recv, device):
        return pltpu.make_async_remote_copy(
            src_ref=src, dst_ref=dst, send_sem=send, recv_sem=recv, device_id=device, device_id_type=MESH
        )

    zero = jnp.zeros((TILE, ROWS), F32)
    past = slice(ROWS, ROWS + TILE)
    for layer in range(4):
        m[layer, 0:TILE, :] = zero
    for c in range(3):
        for k in range(2):
            passed[2 * c + k, 0:TILE, :] = zero
            for plane in range(3):
                y1x[plane, c, k, past, :] = zero
                fwx[plane, c, k, past, :] = zero
            for plane in range(4):
                y0x[plane, c, k, past, :] = zero

    for copy in zones:
        copy.wait()
    bases = [base[i] for i in range(base.shape[0])]

    def moduli(row, n=16):
        at = pl.ds(row, n)
        for layer in range(2):
            zone = ids[layer, at, :]
            scale = jnp.full((n, ROWS), bases[0], F32)
            for i in range(1, len(bases)):
                scale = jnp.where(zone == i, bases[i], scale)
            scale = UNIT * scale
            sc[layer, at, :] = scale
            m[1 + layer, pl.ds(row + TILE, n), :] = fac[layer, at, :] * scale

    over_rows(moduli, 16)
    pl.semaphore_wait(barrier, len(near))
    body_rows = pl.ds(TILE, ROWS)
    has_above, has_below = s < spaces - 1, s > 0
    up, down = {"space": above}, {"space": below}

    def start_up(*copies):
        @pl.when(has_above)
        def _():
            for copy in copies:
                copy.start()

    def start_down(*copies):
        @pl.when(has_below)
        def _():
            for copy in copies:
                copy.start()

    m_up = remote(m.at[2, body_rows], m.at[0, body_rows], halo_send.at[0], halo_recv.at[0], up)
    m_down = remote(m.at[1, body_rows], m.at[3, body_rows], halo_send.at[1], halo_recv.at[1], down)
    start_up(m_up)
    start_down(m_down)
    tell(known1, next1)

    loaded[0].wait()
    loaded[1].wait()

    def inverse_diagonal(low, high, row, n):
        here = m[low, pl.ds(row + TILE, n), :] + m[high, pl.ds(row + TILE, n), :]
        before = m[low, pl.ds(row + TILE - 1, n), :] + m[high, pl.ds(row + TILE - 1, n), :]
        total = here + before
        return 1.0 / ((DIAG / UNIT) * (total + shifted_up(total)))

    def own_first(row, n=64):
        at = pl.ds(row, n)
        free_low = (1 - msk[0, at, :]).astype(F32)
        free_high = (1 - msk[1, at, :]).astype(F32)
        inverse = free_high * inverse_diagonal(1, 2, row, n)
        inv[1, at, :] = inverse
        for c in range(3):
            r0[c, 0, at, :] = free_low * rhs[c, 0, at, :]
            high = free_high * rhs[c, 1, at, :]
            r0[c, 1, at, :] = high
            y0[c, 1, at, :] = inverse * high

    over_rows(own_first, 64)

    r_down, y_up, y1_down = [], [], []
    for i in range(CHUNKS):
        part_rows = pl.ds(CUTS[i], CUTS[i + 1] - CUTS[i])
        r_down.append(
            remote(r0.at[:, 0, part_rows], r0h.at[:, part_rows], halo_send.at[1], halo_recv.at[3 + i], down)
        )
        y_up.append(
            remote(
                y0.at[:, 1, part_rows], y0h.at[:, part_rows],
                halo_send.at[0], halo_recv.at[3 + CHUNKS + i], up,
            )
        )
    for i in range(PIECES):
        done = pl.ds(DONE[i], DONE[i + 1] - DONE[i])
        y1_down.append(
            remote(
                y1.at[:, 0, done], y1h.at[:, done],
                halo_send.at[1], halo_recv.at[4 + 2 * CHUNKS + i], down,
            )
        )
    start_down(*r_down)
    start_up(*y_up)
    loaded[2].wait()
    f_down = [
        remote(fw.at[:, 0, part_rows], fw.at[:, 2, part_rows], halo_send.at[1], halo_recv.at[sem], down)
        for part_rows, sem in ((pl.ds(0, EARLY), 2), (pl.ds(EARLY, ROWS - EARLY), 3 + 2 * CHUNKS))
    ]
    start_down(f_down[0])

    def cleared(ref):
        def body(row):
            ref[pl.ds(row, 32), :] = jnp.zeros((32, ROWS), F32)

        over_rows(body, 32)

    @pl.when(s == 0)
    def _():
        cleared(m.at[0, body_rows])
        for c in range(3):
            cleared(y0h.at[c])

    @pl.when(s == spaces - 1)
    def _():
        cleared(m.at[3, body_rows])
        for c in range(3):
            cleared(r0h.at[c])
            cleared(fw.at[c, 2])
            cleared(y1h.at[c])

    def wait_from_below(*copies):
        @pl.when(has_below)
        def _():
            for copy in copies:
                copy.wait_recv()

    def wait_from_above(*copies):
        @pl.when(has_above)
        def _():
            for copy in copies:
                copy.wait_recv()

    def along_x(value, out, at):
        after = shifted_down(value)
        out[0, at, :] = value + after
        out[1, at, :] = after - value

    def plane_along_x(planes, n):
        def body(row):
            at = pl.ds(row, n)
            for source, out in planes:
                for c in range(3):
                    along_x(source(c, at), out.at[c], at)

        over_rows(body, n)

    pairs = lambda ref: [(ref.at[c, 0], ref.at[c, 1]) for c in range(3)]
    y0_planes = [pairs(y0x.at[plane]) for plane in range(4)]
    y1_planes = [pairs(y1x.at[plane]) for plane in range(3)]
    fw_planes = [pairs(fwx.at[plane]) for plane in range(3)]

    def forward_stress(layer, n, start=0, stop=ROWS):
        def body(row):
            low = plane_modes(fw_planes[layer], row, n)
            high = plane_modes(fw_planes[layer + 1], row, n)
            for i, value in enumerate(stresses(strains(low, high))):
                ff[layer, i, pl.ds(row, n), :] = value

        over_rows(body, n, None, start, stop)

    plane_along_x([(lambda c, at: y0[c, 1, at, :], y0x.at[2])], 32)
    plane_along_x([(lambda c, at, k=k: fw[c, k, at, :], fwx.at[k]) for k in range(2)], 32)
    forward_stress(0, 32)

    wait_from_below(m_up)
    wait_from_above(m_down)
    pl.semaphore_wait(known1, len(next1))
    tell(known2, next2)

    def own_second(row, n=ROWS):
        at = pl.ds(row, n)
        inverse = (1 - msk[0, at, :]).astype(F32) * inverse_diagonal(0, 1, row, n)
        inv[0, at, :] = inverse
        beyond[at, :] = inverse_diagonal(2, 3, row, n)
        for c in range(3):
            field = inverse * r0[c, 0, at, :]
            y0[c, 0, at, :] = field
            along_x(field, y0x.at[1, c], at)

    over_rows(own_second, ROWS)

    def halo(row, n):
        at = pl.ds(row, n)
        inverse = beyond[at, :]
        for c in range(3):
            along_x(y0h[c, at, :], y0x.at[0, c], at)
            along_x(inverse * r0h[c, at, :], y0x.at[3, c], at)

    def product(row, next_norm, n=STEP):
        at = pl.ds(row, n)
        planes = [plane_modes(plane, row, n) for plane in y0_planes]
        layers = []
        for layer in range(3):
            modulus = m[layer, pl.ds(row + TILE, n), :]
            layers.append(corner_modes(stresses(strains(planes[layer], planes[layer + 1]), modulus)))
        for plane in range(2):
            inverse = inv[plane, at, :]
            for c in range(3):
                g = onto_plane(layers[plane][c], layers[plane + 1][c])
                sums = (g[0] - g[1]) + shifted_up(g[0] + g[1])
                slopes = (g[2] - g[3]) + shifted_up(g[2] + g[3])
                passed[3 * plane + c, pl.ds(row + TILE, n), :] = sums + slopes
                force = (sums - slopes) + passed[3 * plane + c, pl.ds(row + TILE - 1, n), :]
                image = inverse * force
                y1[c, plane, at, :] = image
                next_norm = next_norm + folded(force * image)
        return next_norm

    next_norm = zero
    for i in range(CHUNKS):
        wait_from_above(r_down[i])
        wait_from_below(y_up[i])
        halo(CUTS[i], CUTS[i + 1] - CUTS[i])
        for piece in range(i, PIECES if i == CHUNKS - 1 else i + 1):
            next_norm = over_rows(product, STEP, next_norm, DONE[piece], DONE[piece + 1])
            start_down(y1_down[piece])
    start_down(f_down[1])
    pl.semaphore_wait(known2, len(next2))
    tell(known3, next3)

    def against_forward(planes, out, n, start=0, stop=ROWS):
        def body(row):
            all_modes = [plane_modes(plane, row, n) for plane in planes]
            at = pl.ds(row, n)
            for layer in range(2):
                e = strains(all_modes[layer], all_modes[layer + 1])
                out[layer, at, :] = dot(e, [ff[layer, j, at, :] for j in range(18)])

        over_rows(body, n, None, start, stop)

    def energy_of(layer, n):
        def body(row, held):
            e = strains(plane_modes(y1_planes[layer], row, n), plane_modes(y1_planes[layer + 1], row, n))
            return held + folded(m[1 + layer, pl.ds(row + TILE, n), :] * dot(e, stresses(e)))

        return body

    def against_rhs(row, held, n=32):
        norm, curve = held
        at = pl.ds(row, n)
        for c in range(3):
            for plane in range(2):
                residual = r0[c, plane, at, :]
                norm = norm + folded(residual * y0[c, plane, at, :])
                curve = curve + folded(residual * y1[c, plane, at, :])
        return norm, curve

    plane_along_x([(lambda c, at, k=k: y1[c, k, at, :], y1x.at[k]) for k in range(2)], 32)
    energy = over_rows(energy_of(0, 32), 32, zero)
    norm, curve = over_rows(against_rhs, 32, (zero, zero))
    def forward_halo(start, stop):
        at = pl.ds(start, stop - start)
        for c in range(3):
            along_x(fw[c, 2, at, :], fwx.at[2, c], at)

    half = ROWS // 2
    wait_from_above(f_down[0])
    forward_halo(0, EARLY)
    forward_stress(1, 32, 0, half)
    against_forward(y0_planes[1:4], g0, 16, 0, half)

    def taken(sem, ref):
        pltpu.make_async_copy(ref, ref, sem).wait()

    def exchange(src, slots, chosen=None):
        for slot, peer in zip(stage3, peers3):
            copy = remote(
                src.at[:, pl.ds(pl.multiple_of(slot * rows, rows), rows)], gr.at[slots + load],
                sum_send.at[0], sum_recv.at[0], peer,
            )
            if chosen is None:
                copy.start()
            else:
                pl.when(chosen(slot))(copy.start)

    exchange(g0, 0, lambda slot: slot < loads // 2)
    summed_up = lambda value: jnp.sum(jnp.sum(value, axis=0, keepdims=True), axis=1, keepdims=True)
    sums = [summed_up(value) for value in (norm, curve, next_norm)]
    for i in range(PIECES):
        wait_from_above(y1_down[i])
        part_rows = pl.ds(DONE[i], DONE[i + 1] - DONE[i])
        for c in range(3):
            along_x(y1h[c, part_rows, :], y1x.at[2, c], part_rows)
        first, last = DONE[i] - STEP, DONE[i + 1] - STEP
        energy = over_rows(energy_of(1, STEP), STEP, energy, max(first, 0), ROWS if i == PIECES - 1 else last)

    lane = lax.broadcasted_iota(jnp.int32, (1, ROWS), 1)
    quarter = ROWS // 4
    last = summed_up(energy)
    part[...] = jnp.where(
        lane < 2 * quarter,
        jnp.where(lane < quarter, sums[0], sums[1]),
        jnp.where(lane < 3 * quarter, sums[2], last),
    )
    for peer in peers1:
        remote(part, r1.at[within], sum_send.at[1], sum_recv.at[1], peer).start()
    r1[within] = part[...]
    wait_from_above(f_down[1])
    forward_halo(EARLY, ROWS)
    forward_stress(1, 32, half, ROWS)
    against_forward(y0_planes[1:4], g0, 16, half, ROWS)
    exchange(g0, 0, lambda slot: slot >= loads // 2)
    against_forward(y1_planes, g1, 16)
    exchange(g1, loads)

    taken(sum_recv.at[1], r1.at[pl.ds(0, group - 1)])
    total = r1[0]
    for i in range(1, group):
        total = total + r1[i]
    mid[...] = total
    pl.semaphore_wait(known3, len(next3))
    for peer in peers_own:
        remote(mid, r2.at[outer, load], sum_send.at[2], sum_recv.at[2], peer).start()
    for peer in peers_other:
        remote(mid, r2.at[outer, load], sum_send.at[3], sum_recv.at[3], peer).start()
    r2[outer, load] = total

    def coefficients(sums):
        rr, rq, qq, qd = [sums[:, i * quarter : i * quarter + 1] for i in range(4)]
        step = rr / rq
        norm_next = step * (step * qq) - rr
        ratio = norm_next / rr
        curve_next = rq - 2.0 * (step * qq) + step * (step * qd)
        step_next = norm_next / (curve_next - ratio * norm_next / step)
        return step + step_next * (1.0 + ratio), -(step_next * step)

    def summed(j):
        total = r2[0, j]
        for i in range(1, wide):
            total = total + r2[i, j]
        return total

    taken(sum_recv.at[2], r2.at[pl.ds(0, wide - 1), 0])
    first, second = coefficients(summed(load))

    def solve(row, n=ROWS):
        at = pl.ds(row, n)
        for c in range(3):
            for plane in range(2):
                x_out[c, plane, at, :] = first * y0[c, plane, at, :] + second * y1[c, plane, at, :]

    over_rows(solve, ROWS)
    x_copy = pltpu.make_async_copy(x_out, x_hbm, load_sem.at[0])
    x_copy.start()

    mine = pl.ds(pl.multiple_of(load * rows, rows), rows)
    gr[load] = g0[:, mine, :]
    gr[loads + load] = g1[:, mine, :]
    taken(sum_recv.at[0], gr.at[pl.ds(0, 2 * (loads - 1))])

    taken(sum_send.at[0], gr.at[pl.ds(0, 2 * (loads - 1))])
    taken(sum_send.at[1], r1.at[pl.ds(0, group - 1)])

    @pl.when(has_above)
    def _():
        taken(halo_send.at[0], ff.at[0, pl.ds(0, 4)])

    @pl.when(has_below)
    def _():
        taken(halo_send.at[1], ff.at[0, pl.ds(0, 10)])

    taken(sum_recv.at[3], r2.at[pl.ds(0, wide), pl.ds(0, loads - 1)])
    for j in range(loads):
        coefs[0, j : j + 1, :] = summed(j)
    first, second = coefficients(coefs[0])
    coefs[0] = jnp.broadcast_to(first, (loads, ROWS))
    coefs[1] = jnp.broadcast_to(second, (loads, ROWS))
    total = None
    for i in range(loads):
        term = coefs[0, i : i + 1, :][None] * gr[i] + coefs[1, i : i + 1, :][None] * gr[loads + i]
        total = term if total is None else total + term
    grad_out[...] = sc[:, mine, :] * total
    grad_copy = pltpu.make_async_copy(grad_out, grad_hbm, load_sem.at[1])
    grad_copy.start()

    taken(sum_send.at[3], r2.at[pl.ds(0, wide), pl.ds(0, loads - 1)])
    taken(sum_send.at[2], r2.at[pl.ds(0, wide - 1), 0])
    x_copy.wait()
    grad_copy.wait()


def finish(x, grad, x_out, grad_out, sem):
    copies = [pltpu.make_async_copy(x, x_out.at[0], sem.at[0]), pltpu.make_async_copy(grad, grad_out, sem.at[1])]
    for copy in copies:
        copy.start()
    for copy in copies:
        copy.wait()


def solution(mesh):
    spaces, loads = mesh.shape["space"], mesh.shape["load"]
    group = 2 * LONG
    rows = ROWS // loads

    def shards(forward_disp, adjoint_rhs, modulus_factor, zone_base, zone_ids, fixed_mask):
        plane = (ROWS, ROWS)
        padded = (ROWS + TILE, ROWS)
        vmem = lambda *shape: pltpu.VMEM(shape, F32)
        ints = lambda *shape: pltpu.VMEM(shape, jnp.int32)
        dma = pltpu.SemaphoreType.DMA
        hbm = pl.BlockSpec(memory_space=pltpu.HBM)
        anywhere = pl.BlockSpec(memory_space=pl.ANY)
        out = lambda *shape: jax.ShapeDtypeStruct(shape, F32)
        pinned = [
            pltpu.with_memory_space_constraint(a, pltpu.HBM)
            for a in (forward_disp, adjoint_rhs, modulus_factor, zone_base, zone_ids, fixed_mask)
        ]
        x, grad = pl.pallas_call(
            functools.partial(kernel, spaces=spaces, loads=loads, group=group),
            out_shape=(out(3, 2, *plane), out(2, rows, ROWS)),
            in_specs=[hbm] * 6,
            out_specs=(anywhere,) * 2,
            scratch_shapes=[
                vmem(3, 2, *plane), vmem(2, rows, ROWS), pltpu.SMEM(zone_base.shape, F32),
                vmem(2, *plane), ints(2, *plane), ints(2, *plane), vmem(3, 2, *plane), vmem(3, 3, *plane),
                vmem(2, *plane), vmem(4, *padded), vmem(3, 2, *plane), vmem(3, 2, *plane), vmem(3, *plane), vmem(3, *plane),
                vmem(4, 3, 2, *padded), vmem(3, 3, 2, *padded), vmem(3, 3, 2, *padded), vmem(6, *padded),
                vmem(2, *plane), vmem(*plane), vmem(3, 2, *plane), vmem(3, *plane), vmem(2, 18, *plane),
                vmem(2, *plane), vmem(2, *plane), vmem(2 * loads, 2, rows, ROWS),
                vmem(1, ROWS), vmem(group, 1, ROWS), vmem(1, ROWS), vmem(spaces // group, loads, 1, ROWS),
                vmem(2, loads, ROWS),
                dma((8,)), dma((2,)), dma((4 + 2 * CHUNKS + PIECES,)), dma((4,)), dma((4,)),
                *[pltpu.SemaphoreType.REGULAR] * 3,
            ],
            compiler_params=pltpu.CompilerParams(collective_id=0, has_side_effects=True, vmem_limit_bytes=LIMIT),
        )(*pinned)
        return pl.pallas_call(
            finish,
            out_shape=(out(1, 3, 2, *plane), out(2, rows, ROWS)),
            in_specs=[anywhere] * 2,
            out_specs=(hbm, hbm),
            scratch_shapes=[dma((2,))],
            compiler_params=pltpu.CompilerParams(vmem_limit_bytes=4 * 2**20),
        )(x, grad)

    placed = (
        P("load", None, "space", None, None),
        P("load", None, "space", None, None),
        P("space", None, None),
        P(),
        P("space", None, None),
        P("space", None, None),
    )
    return jax.shard_map(
        shards,
        mesh=mesh,
        in_specs=placed,
        out_specs=(P("load", None, "space", None, None), P("space", "load", None)),
        check_vma=False,
    )
```

```python
import functools

import jax
import jax.numpy as jnp
import numpy as np
from jax import lax
from jax.experimental import pallas as pl
from jax.experimental.pallas import tpu as pltpu
from jax.sharding import PartitionSpec as P

F32 = jnp.float32
MESH = pl.DeviceIdType.MESH
ROWS = 128
TILE = 8
LONG = 8
STEP = 16
CUTS = [0, 32, 64, 96, 112, ROWS]
CHUNKS = len(CUTS) - 1
EARLY = 72
DONE = [0] + [cut - STEP for cut in CUTS[1:]] + [ROWS]
PIECES = len(DONE) - 1
LIMIT = 40 * 2**20

POISSON = 0.3
SHEAR = 0.5 / (1.0 + POISSON)
KAPPA = 2.0 * POISSON / (1.0 - 2.0 * POISSON)
UNIT = SHEAR / 16.0
DIAG = SHEAR * (KAPPA + 4.0) / 9.0


def shifted_down(value):
    last = lax.broadcasted_iota(jnp.int32, value.shape, 1) == ROWS - 1
    return jnp.where(last, 0.0, pltpu.roll(value, ROWS - 1, 1))


def shifted_up(value):
    first = lax.broadcasted_iota(jnp.int32, value.shape, 1) == 0
    return jnp.where(first, 0.0, pltpu.roll(value, 1, 1))


def plane_modes(pairs, row, n):
    out = []
    for sums, slopes in pairs:
        here, after = sums[pl.ds(row, n), :], sums[pl.ds(row + 1, n), :]
        slope, slope_after = slopes[pl.ds(row, n), :], slopes[pl.ds(row + 1, n), :]
        out.append((here + after, slope + slope_after, after - here, slope_after - slope))
    return out


def strains(low, high):
    (u, v, w) = [
        (
            l[1] + h[1],
            l[2] + h[2],
            h[0] - l[0],
            l[3] + h[3],
            h[1] - l[1],
            h[2] - l[2],
            h[3] - l[3],
        )
        for l, h in zip(low, high)
    ]
    return (
        u[0], v[1], w[2],
        u[1] + v[0], u[2] + w[0], v[2] + w[1],
        u[3], w[5], u[4], v[5], v[3], w[4],
        u[5], v[4], w[3],
        u[6], v[6], w[6],
    )


def stresses(e, modulus=None):
    third, last = 1.0 / 3.0, (KAPPA + 4.0) / 9.0
    if modulus is None:
        two = 2.0
        times = lambda value: value
    else:
        two, third, last = 2.0 * modulus, third * modulus, last * modulus
        times = lambda value: modulus * value
    half = (0.5 * KAPPA) * (e[0] + e[1] + e[2])
    out = [two * (e[0] + half), two * (e[1] + half), two * (e[2] + half), times(e[3]), times(e[4]), times(e[5])]
    for a, b in ((6, 7), (8, 9), (10, 11)):
        both = (KAPPA / 3.0) * (e[a] + e[b])
        out += [times(e[a] + both), times(e[b] + both)]
    shear = e[12] + e[13] + e[14]
    out += [third * (e[12] + shear), third * (e[13] + shear), third * (e[14] + shear)]
    out += [last * e[15], last * e[16], last * e[17]]
    return out


def corner_modes(f):
    return (
        (f[0], f[3], f[4], f[6], f[8], f[12], f[15]),
        (f[3], f[1], f[5], f[10], f[13], f[9], f[16]),
        (f[4], f[5], f[2], f[14], f[11], f[7], f[17]),
    )


def onto_plane(under, over):
    return (
        under[2] - over[2],
        (under[0] + under[4]) + (over[0] - over[4]),
        (under[1] + under[5]) + (over[1] - over[5]),
        (under[3] + under[6]) + (over[3] - over[6]),
    )


def dot(a, b):
    total = None
    for left, right in zip(a, b):
        term = left * right
        total = term if total is None else total + term
    return total


def folded(value):
    total = value[0:TILE]
    for i in range(1, value.shape[0] // TILE):
        total = total + value[i * TILE : (i + 1) * TILE]
    return total


def over_rows(body, size, carry=None, start=0, stop=ROWS):
    at = lambda b: pl.multiple_of(b * size, size)
    first, last = start // size, stop // size
    if carry is None:
        lax.fori_loop(first, last, lambda b, _: (body(at(b)), 0)[1], 0)
        return None
    return lax.fori_loop(first, last, lambda b, held: body(at(b), held), carry)


def kernel(
    fwd_hbm, rhs_hbm, fac_hbm, base_hbm, ids_hbm, msk_hbm,
    x_out, grad_out,
    base, fac, ids, msk, rhs, fw, sc, m, y0, y1, y0h, y1h, y0x, y1x, fwx, passed, inv, beyond, r0, r0h, ff, g0, g1, gr,
    part, r1, mid, r2, coefs,
    load_sem, halo_send, halo_recv, sum_send, sum_recv, known1, known2, known3,
    *, spaces, loads, group,
):
    s = lax.axis_index("space")
    load = lax.axis_index("load")
    above, below = lax.rem(s + 1, spaces), lax.rem(s + spaces - 1, spaces)
    wide = spaces // group
    within, outer = lax.rem(s, group), s // group
    rows = ROWS // loads

    def local(src, dst, index):
        return pltpu.make_async_copy(src, dst, load_sem.at[index])

    zones = [local(base_hbm, base, 5)]
    zones += [local(fac_hbm.at[k], fac.at[k], k) for k in range(2)] + [local(ids_hbm.at[k], ids.at[k], 2 + k) for k in range(2)]
    loaded = [local(msk_hbm, msk, 6), local(rhs_hbm.at[0], rhs, 7), local(fwd_hbm.at[0], fw.at[:, pl.ds(0, 2)], 4)]
    for copy in zones + loaded:
        copy.start()

    core, y = lax.rem(s, 2), lax.rem(s // 2, LONG)
    at_y = lambda step, c: {"space": outer * group + lax.rem(y + LONG + step, LONG) * 2 + c}
    at_x = lambda step: {"space": lax.rem(outer + wide + step, wide) * group + within}
    at_z = lambda step: {"load": lax.rem(load + loads + step, loads)}

    near = [{"space": above}, {"space": below}, at_y(0, 1 - core)]
    near += [at_y(step, c) for step in (1, -1) for c in range(2)] + [at_x(1), at_x(-1), at_z(1), at_z(-1)]
    next1 = [at_y(1, core), at_y(-1, core), at_x(1), at_x(-1), at_z(1), at_z(-1)]
    next2 = [at_y(2, core), at_y(-2, core), at_z(2), at_z(-2)]
    next3 = [at_x(1), at_x(-1), at_x(2)]

    def tell(sem, peers):
        for peer in peers:
            pl.semaphore_signal(sem, inc=1, device_id=peer, device_id_type=MESH)

    barrier = pltpu.get_barrier_semaphore()
    tell(barrier, near)

    far = lambda step, size: min(step, size - step)
    order1 = sorted(range(1, group), key=lambda i: -far(i // 2 + i % 2, LONG))
    order2 = sorted(
        ((i, j) for i in range(wide) for j in range(1, loads)), key=lambda ij: -far(ij[0], wide) - far(ij[1], loads)
    )
    stage1 = [lax.rem(within + i, group) for i in order1]
    peers1 = [{"space": outer * group + i} for i in stage1]
    stage2 = [lax.rem(outer + i, wide) * group + within for i in range(wide)]
    peers_own = [{"space": stage2[i]} for i in sorted(range(1, wide), key=lambda i: -far(i, wide))]
    peers_other = [{"space": stage2[i], "load": lax.rem(load + j, loads)} for i, j in order2]
    stage3 = [lax.rem(load + i, loads) for i in sorted(range(1, loads), key=lambda i: -far(i, loads))]
    peers3 = [{"load": i} for i in stage3]

    def remote(src, dst, send, recv, device):
        return pltpu.make_async_remote_copy(
            src_ref=src, dst_ref=dst, send_sem=send, recv_sem=recv, device_id=device, device_id_type=MESH
        )

    zero = jnp.zeros((TILE, ROWS), F32)
    past = slice(ROWS, ROWS + TILE)
    for layer in range(4):
        m[layer, 0:TILE, :] = zero
    for c in range(3):
        for k in range(2):
            passed[2 * c + k, 0:TILE, :] = zero
            for plane in range(3):
                y1x[plane, c, k, past, :] = zero
                fwx[plane, c, k, past, :] = zero
            for plane in range(4):
                y0x[plane, c, k, past, :] = zero

    for copy in zones:
        copy.wait()
    bases = [base[i] for i in range(base.shape[0])]

    def moduli(row, n=16):
        at = pl.ds(row, n)
        for layer in range(2):
            zone = ids[layer, at, :]
            scale = jnp.full((n, ROWS), bases[0], F32)
            for i in range(1, len(bases)):
                scale = jnp.where(zone == i, bases[i], scale)
            scale = UNIT * scale
            sc[layer, at, :] = scale
            m[1 + layer, pl.ds(row + TILE, n), :] = fac[layer, at, :] * scale

    over_rows(moduli, 16)
    pl.semaphore_wait(barrier, len(near))
    body_rows = pl.ds(TILE, ROWS)
    has_above, has_below = s < spaces - 1, s > 0
    up, down = {"space": above}, {"space": below}

    def start_up(*copies):
        @pl.when(has_above)
        def _():
            for copy in copies:
                copy.start()

    def start_down(*copies):
        @pl.when(has_below)
        def _():
            for copy in copies:
                copy.start()

    m_up = remote(m.at[2, body_rows], m.at[0, body_rows], halo_send.at[0], halo_recv.at[0], up)
    m_down = remote(m.at[1, body_rows], m.at[3, body_rows], halo_send.at[1], halo_recv.at[1], down)
    start_up(m_up)
    start_down(m_down)
    tell(known1, next1)

    loaded[0].wait()
    loaded[1].wait()

    def inverse_diagonal(low, high, row, n):
        here = m[low, pl.ds(row + TILE, n), :] + m[high, pl.ds(row + TILE, n), :]
        before = m[low, pl.ds(row + TILE - 1, n), :] + m[high, pl.ds(row + TILE - 1, n), :]
        total = here + before
        return 1.0 / ((DIAG / UNIT) * (total + shifted_up(total)))

    def own_first(row, n=64):
        at = pl.ds(row, n)
        free_low = (1 - msk[0, at, :]).astype(F32)
        free_high = (1 - msk[1, at, :]).astype(F32)
        inverse = free_high * inverse_diagonal(1, 2, row, n)
        inv[1, at, :] = inverse
        for c in range(3):
            r0[c, 0, at, :] = free_low * rhs[c, 0, at, :]
            high = free_high * rhs[c, 1, at, :]
            r0[c, 1, at, :] = high
            y0[c, 1, at, :] = inverse * high

    over_rows(own_first, 64)

    r_down, y_up, y1_down = [], [], []
    for i in range(CHUNKS):
        part_rows = pl.ds(CUTS[i], CUTS[i + 1] - CUTS[i])
        r_down.append(
            remote(r0.at[:, 0, part_rows], r0h.at[:, part_rows], halo_send.at[1], halo_recv.at[3 + i], down)
        )
        y_up.append(
            remote(
                y0.at[:, 1, part_rows], y0h.at[:, part_rows],
                halo_send.at[0], halo_recv.at[3 + CHUNKS + i], up,
            )
        )
    for i in range(PIECES):
        done = pl.ds(DONE[i], DONE[i + 1] - DONE[i])
        y1_down.append(
            remote(
                y1.at[:, 0, done], y1h.at[:, done],
                halo_send.at[1], halo_recv.at[4 + 2 * CHUNKS + i], down,
            )
        )
    start_down(*r_down)
    start_up(*y_up)
    loaded[2].wait()
    f_down = [
        remote(fw.at[:, 0, part_rows], fw.at[:, 2, part_rows], halo_send.at[1], halo_recv.at[sem], down)
        for part_rows, sem in ((pl.ds(0, EARLY), 2), (pl.ds(EARLY, ROWS - EARLY), 3 + 2 * CHUNKS))
    ]
    start_down(f_down[0])

    def cleared(ref):
        def body(row):
            ref[pl.ds(row, 32), :] = jnp.zeros((32, ROWS), F32)

        over_rows(body, 32)

    @pl.when(s == 0)
    def _():
        cleared(m.at[0, body_rows])
        for c in range(3):
            cleared(y0h.at[c])

    @pl.when(s == spaces - 1)
    def _():
        cleared(m.at[3, body_rows])
        for c in range(3):
            cleared(r0h.at[c])
            cleared(fw.at[c, 2])
            cleared(y1h.at[c])

    def wait_from_below(*copies):
        @pl.when(has_below)
        def _():
            for copy in copies:
                copy.wait_recv()

    def wait_from_above(*copies):
        @pl.when(has_above)
        def _():
            for copy in copies:
                copy.wait_recv()

    def along_x(value, out, at):
        after = shifted_down(value)
        out[0, at, :] = value + after
        out[1, at, :] = after - value

    def plane_along_x(planes, n):
        def body(row):
            at = pl.ds(row, n)
            for source, out in planes:
                for c in range(3):
                    along_x(source(c, at), out.at[c], at)

        over_rows(body, n)

    pairs = lambda ref: [(ref.at[c, 0], ref.at[c, 1]) for c in range(3)]
    y0_planes = [pairs(y0x.at[plane]) for plane in range(4)]
    y1_planes = [pairs(y1x.at[plane]) for plane in range(3)]
    fw_planes = [pairs(fwx.at[plane]) for plane in range(3)]

    def forward_stress(layer, n, start=0, stop=ROWS):
        def body(row):
            low = plane_modes(fw_planes[layer], row, n)
            high = plane_modes(fw_planes[layer + 1], row, n)
            for i, value in enumerate(stresses(strains(low, high))):
                ff[layer, i, pl.ds(row, n), :] = value

        over_rows(body, n, None, start, stop)

    plane_along_x([(lambda c, at: y0[c, 1, at, :], y0x.at[2])], 32)
    plane_along_x([(lambda c, at, k=k: fw[c, k, at, :], fwx.at[k]) for k in range(2)], 32)
    forward_stress(0, 32)

    wait_from_below(m_up)
    wait_from_above(m_down)
    pl.semaphore_wait(known1, len(next1))
    tell(known2, next2)

    def own_second(row, n=ROWS):
        at = pl.ds(row, n)
        inverse = (1 - msk[0, at, :]).astype(F32) * inverse_diagonal(0, 1, row, n)
        inv[0, at, :] = inverse
        beyond[at, :] = inverse_diagonal(2, 3, row, n)
        for c in range(3):
            field = inverse * r0[c, 0, at, :]
            y0[c, 0, at, :] = field
            along_x(field, y0x.at[1, c], at)

    over_rows(own_second, ROWS)

    def halo(row, n):
        at = pl.ds(row, n)
        inverse = beyond[at, :]
        for c in range(3):
            along_x(y0h[c, at, :], y0x.at[0, c], at)
            along_x(inverse * r0h[c, at, :], y0x.at[3, c], at)

    def product(row, next_norm, n=STEP):
        at = pl.ds(row, n)
        planes = [plane_modes(plane, row, n) for plane in y0_planes]
        layers = []
        for layer in range(3):
            modulus = m[layer, pl.ds(row + TILE, n), :]
            layers.append(corner_modes(stresses(strains(planes[layer], planes[layer + 1]), modulus)))
        for plane in range(2):
            inverse = inv[plane, at, :]
            for c in range(3):
                g = onto_plane(layers[plane][c], layers[plane + 1][c])
                sums = (g[0] - g[1]) + shifted_up(g[0] + g[1])
                slopes = (g[2] - g[3]) + shifted_up(g[2] + g[3])
                passed[3 * plane + c, pl.ds(row + TILE, n), :] = sums + slopes
                force = (sums - slopes) + passed[3 * plane + c, pl.ds(row + TILE - 1, n), :]
                image = inverse * force
                y1[c, plane, at, :] = image
                next_norm = next_norm + folded(force * image)
        return next_norm

    next_norm = zero
    for i in range(CHUNKS):
        wait_from_above(r_down[i])
        wait_from_below(y_up[i])
        halo(CUTS[i], CUTS[i + 1] - CUTS[i])
        for piece in range(i, PIECES if i == CHUNKS - 1 else i + 1):
            next_norm = over_rows(product, STEP, next_norm, DONE[piece], DONE[piece + 1])
            start_down(y1_down[piece])
    start_down(f_down[1])
    pl.semaphore_wait(known2, len(next2))
    tell(known3, next3)

    def against_forward(planes, out, n, start=0, stop=ROWS):
        def body(row):
            all_modes = [plane_modes(plane, row, n) for plane in planes]
            at = pl.ds(row, n)
            for layer in range(2):
                e = strains(all_modes[layer], all_modes[layer + 1])
                out[layer, at, :] = dot(e, [ff[layer, j, at, :] for j in range(18)])

        over_rows(body, n, None, start, stop)

    def energy_of(layer, n):
        def body(row, held):
            e = strains(plane_modes(y1_planes[layer], row, n), plane_modes(y1_planes[layer + 1], row, n))
            return held + folded(m[1 + layer, pl.ds(row + TILE, n), :] * dot(e, stresses(e)))

        return body

    def against_rhs(row, held, n=32):
        norm, curve = held
        at = pl.ds(row, n)
        for c in range(3):
            for plane in range(2):
                residual = r0[c, plane, at, :]
                norm = norm + folded(residual * y0[c, plane, at, :])
                curve = curve + folded(residual * y1[c, plane, at, :])
        return norm, curve

    plane_along_x([(lambda c, at, k=k: y1[c, k, at, :], y1x.at[k]) for k in range(2)], 32)
    energy = over_rows(energy_of(0, 32), 32, zero)
    norm, curve = over_rows(against_rhs, 32, (zero, zero))
    def forward_halo(start, stop):
        at = pl.ds(start, stop - start)
        for c in range(3):
            along_x(fw[c, 2, at, :], fwx.at[2, c], at)

    half = ROWS // 2
    wait_from_above(f_down[0])
    forward_halo(0, EARLY)
    forward_stress(1, 32, 0, half)
    against_forward(y0_planes[1:4], g0, 16, 0, half)

    def taken(sem, ref):
        pltpu.make_async_copy(ref, ref, sem).wait()

    def exchange(src, slots, chosen=None):
        for slot, peer in zip(stage3, peers3):
            copy = remote(
                src.at[:, pl.ds(pl.multiple_of(slot * rows, rows), rows)], gr.at[slots + load],
                sum_send.at[0], sum_recv.at[0], peer,
            )
            if chosen is None:
                copy.start()
            else:
                pl.when(chosen(slot))(copy.start)

    exchange(g0, 0, lambda slot: slot < loads // 2)
    summed_up = lambda value: jnp.sum(jnp.sum(value, axis=0, keepdims=True), axis=1, keepdims=True)
    sums = [summed_up(value) for value in (norm, curve, next_norm)]
    for i in range(PIECES):
        wait_from_above(y1_down[i])
        part_rows = pl.ds(DONE[i], DONE[i + 1] - DONE[i])
        for c in range(3):
            along_x(y1h[c, part_rows, :], y1x.at[2, c], part_rows)
        first, last = DONE[i] - STEP, DONE[i + 1] - STEP
        energy = over_rows(energy_of(1, STEP), STEP, energy, max(first, 0), ROWS if i == PIECES - 1 else last)

    lane = lax.broadcasted_iota(jnp.int32, (1, ROWS), 1)
    quarter = ROWS // 4
    last = summed_up(energy)
    part[...] = jnp.where(
        lane < 2 * quarter,
        jnp.where(lane < quarter, sums[0], sums[1]),
        jnp.where(lane < 3 * quarter, sums[2], last),
    )
    for peer in peers1:
        remote(part, r1.at[within], sum_send.at[1], sum_recv.at[1], peer).start()
    r1[within] = part[...]
    wait_from_above(f_down[1])
    forward_halo(EARLY, ROWS)
    forward_stress(1, 32, half, ROWS)
    against_forward(y0_planes[1:4], g0, 16, half, ROWS)
    exchange(g0, 0, lambda slot: slot >= loads // 2)
    against_forward(y1_planes, g1, 16)
    exchange(g1, loads)

    taken(sum_recv.at[1], r1.at[pl.ds(0, group - 1)])
    total = r1[0]
    for i in range(1, group):
        total = total + r1[i]
    mid[...] = total
    pl.semaphore_wait(known3, len(next3))
    for peer in peers_own:
        remote(mid, r2.at[outer, load], sum_send.at[2], sum_recv.at[2], peer).start()
    for peer in peers_other:
        remote(mid, r2.at[outer, load], sum_send.at[3], sum_recv.at[3], peer).start()
    r2[outer, load] = total

    def coefficients(sums):
        rr, rq, qq, qd = [sums[:, i * quarter : i * quarter + 1] for i in range(4)]
        step = rr / rq
        norm_next = step * (step * qq) - rr
        ratio = norm_next / rr
        curve_next = rq - 2.0 * (step * qq) + step * (step * qd)
        step_next = norm_next / (curve_next - ratio * norm_next / step)
        return step + step_next * (1.0 + ratio), -(step_next * step)

    def summed(j):
        total = r2[0, j]
        for i in range(1, wide):
            total = total + r2[i, j]
        return total

    taken(sum_recv.at[2], r2.at[pl.ds(0, wide - 1), 0])
    first, second = coefficients(summed(load))

    def solve(row, n=ROWS):
        at = pl.ds(row, n)
        for c in range(3):
            for plane in range(2):
                x_out[c, plane, at, :] = first * y0[c, plane, at, :] + second * y1[c, plane, at, :]

    over_rows(solve, ROWS)

    mine = pl.ds(pl.multiple_of(load * rows, rows), rows)
    gr[load] = g0[:, mine, :]
    gr[loads + load] = g1[:, mine, :]
    taken(sum_recv.at[0], gr.at[pl.ds(0, 2 * (loads - 1))])

    taken(sum_send.at[0], gr.at[pl.ds(0, 2 * (loads - 1))])
    taken(sum_send.at[1], r1.at[pl.ds(0, group - 1)])

    @pl.when(has_above)
    def _():
        taken(halo_send.at[0], ff.at[0, pl.ds(0, 4)])

    @pl.when(has_below)
    def _():
        taken(halo_send.at[1], ff.at[0, pl.ds(0, 10)])

    taken(sum_recv.at[3], r2.at[pl.ds(0, wide), pl.ds(0, loads - 1)])
    for j in range(loads):
        coefs[0, j : j + 1, :] = summed(j)
    first, second = coefficients(coefs[0])
    coefs[0] = jnp.broadcast_to(first, (loads, ROWS))
    coefs[1] = jnp.broadcast_to(second, (loads, ROWS))
    total = None
    for i in range(loads):
        term = coefs[0, i : i + 1, :][None] * gr[i] + coefs[1, i : i + 1, :][None] * gr[loads + i]
        total = term if total is None else total + term
    grad_out[...] = sc[:, mine, :] * total

    taken(sum_send.at[3], r2.at[pl.ds(0, wide), pl.ds(0, loads - 1)])
    taken(sum_send.at[2], r2.at[pl.ds(0, wide - 1), 0])


def finish(x, grad, x_out, grad_out, sem):
    copies = [pltpu.make_async_copy(x, x_out.at[0], sem.at[0]), pltpu.make_async_copy(grad, grad_out, sem.at[1])]
    for copy in copies:
        copy.start()
    for copy in copies:
        copy.wait()


def solution(mesh):
    spaces, loads = mesh.shape["space"], mesh.shape["load"]
    group = 2 * LONG
    rows = ROWS // loads

    def shards(forward_disp, adjoint_rhs, modulus_factor, zone_base, zone_ids, fixed_mask):
        plane = (ROWS, ROWS)
        padded = (ROWS + TILE, ROWS)
        vmem = lambda *shape: pltpu.VMEM(shape, F32)
        ints = lambda *shape: pltpu.VMEM(shape, jnp.int32)
        dma = pltpu.SemaphoreType.DMA
        hbm = pl.BlockSpec(memory_space=pltpu.HBM)
        anywhere = pl.BlockSpec(memory_space=pl.ANY)
        out = lambda *shape: jax.ShapeDtypeStruct(shape, F32)
        pinned = [
            pltpu.with_memory_space_constraint(a, pltpu.HBM)
            for a in (forward_disp, adjoint_rhs, modulus_factor, zone_base, zone_ids, fixed_mask)
        ]
        x, grad = pl.pallas_call(
            functools.partial(kernel, spaces=spaces, loads=loads, group=group),
            out_shape=(out(3, 2, *plane), out(2, rows, ROWS)),
            in_specs=[hbm] * 6,
            out_specs=(pl.BlockSpec(memory_space=pltpu.VMEM),) * 2,
            scratch_shapes=[
                pltpu.SMEM(zone_base.shape, F32),
                vmem(2, *plane), ints(2, *plane), ints(2, *plane), vmem(3, 2, *plane), vmem(3, 3, *plane),
                vmem(2, *plane), vmem(4, *padded), vmem(3, 2, *plane), vmem(3, 2, *plane), vmem(3, *plane), vmem(3, *plane),
                vmem(4, 3, 2, *padded), vmem(3, 3, 2, *padded), vmem(3, 3, 2, *padded), vmem(6, *padded),
                vmem(2, *plane), vmem(*plane), vmem(3, 2, *plane), vmem(3, *plane), vmem(2, 18, *plane),
                vmem(2, *plane), vmem(2, *plane), vmem(2 * loads, 2, rows, ROWS),
                vmem(1, ROWS), vmem(group, 1, ROWS), vmem(1, ROWS), vmem(spaces // group, loads, 1, ROWS),
                vmem(2, loads, ROWS),
                dma((8,)), dma((2,)), dma((4 + 2 * CHUNKS + PIECES,)), dma((4,)), dma((4,)),
                *[pltpu.SemaphoreType.REGULAR] * 3,
            ],
            compiler_params=pltpu.CompilerParams(collective_id=0, has_side_effects=True, vmem_limit_bytes=LIMIT),
        )(*pinned)
        return pl.pallas_call(
            finish,
            out_shape=(out(1, 3, 2, *plane), out(2, rows, ROWS)),
            in_specs=[anywhere] * 2,
            out_specs=(hbm, hbm),
            scratch_shapes=[dma((2,))],
            compiler_params=pltpu.CompilerParams(vmem_limit_bytes=4 * 2**20),
        )(x, grad)

    placed = (
        P("load", None, "space", None, None),
        P("load", None, "space", None, None),
        P("space", None, None),
        P(),
        P("space", None, None),
        P("space", None, None),
    )
    return jax.shard_map(
        shards,
        mesh=mesh,
        in_specs=placed,
        out_specs=(P("load", None, "space", None, None), P("space", "load", None)),
        check_vma=False,
    )
```
